32 devices in a mesh: dp: 8 (over z, x), tensor: 4 (over y, core).
Axes of the slice: x: 2, y: 2, z: 4, core: 2. Of those that a mesh axis runs over, the one named last changes fastest.
Arguments:
- tokens: bfloat16 [32768, 768], P(('dp', 'tensor')), may hold values from -6 to 6
- cotangent: bfloat16 [32768, 768], P(('dp', 'tensor')), may hold values from -6 to 6
- tie_index: int32 [1], replicated, may hold values from 0 to 11
- image_start: int32 [8], P('dp'), may hold values from 0 to 3840
- qkv_bank: bfloat16 [12, 768, 3, 768], P(None, 'dp', None, 'tensor'), may hold values from -0.21875 to 0.21875
- out_bank: bfloat16 [12, 768, 768], P(None, 'tensor', 'dp'), may hold values from -3.5 to 3.5
- up_bank: bfloat16 [12, 768, 3072], P(None, 'dp', 'tensor'), may hold values from -0.21875 to 0.21875
- down_bank: bfloat16 [12, 3072, 768], P(None, 'tensor', 'dp'), may hold values from -0.109375 to 0.109375
- gain_bank: bfloat16 [12, 2, 768], P(None, None, 'dp'), may hold values from 0.25 to 1.75
- shift_bank: bfloat16 [12, 4, 768], P(None, None, 'dp'), may hold values from -1.5 to 1.5
- head_bias_bank: bfloat16 [12, 2, 768], P(None, None, ('tensor', 'dp')), may hold values from -1.5 to 1.5
- hidden_bias_bank: bfloat16 [12, 3072], P(None, ('tensor', 'dp')), may hold values from -1.5 to 1.5
Outputs:
- layer_out: bfloat16 [32768, 768], P(('dp', 'tensor'))
- grad_tokens: bfloat16 [32768, 768], P(('dp', 'tensor'))
- grad_qkv: float32 [768, 3, 768], P('dp', None, 'tensor')
- grad_out: float32 [768, 768], P('tensor', 'dp')
- grad_up: float32 [768, 3072], P('dp', 'tensor')
- grad_down: float32 [3072, 768], P('tensor', 'dp')
- grad_gains: float32 [2, 768], P(None, 'dp')
- grad_shifts: float32 [4, 768], P(None, 'dp')
- grad_head_bias: float32 [2, 768], P(None, ('tensor', 'dp'))
- grad_hidden_bias: float32 [3072], P(('tensor', 'dp'))
The draws below stay inside these ranges and needn't reach their ends.
Inputs may be any that keep to these rules, and one draw needn't show every extreme that they name: `tie_index`: which of the 12 weight sets the block uses. Each sequence's image span is positions image_start to image_start + 255.
All inputs are finite; a program needn't handle non-finite values.
Results may differ from the reference program's by a relative error of at most 0.017.
Values may be sent and summed in bfloat16 or wider, within the bound.
No kernel may reach another device: no remote copies, remote signals or barrier semaphores. Data moves between devices by JAX's collectives and lax.ppermute only.
A program may use at most 256 MiB of HBM per device.

```python
import math
import jax
import jax.numpy as jnp
from jax import lax

D = 768
HEADS = 12
HEAD_DIM = 64
FF = 3072
BANK = 12
SEQ_LEN = 4096
IMG = 256
SEQS = 1
SEQUENCES = 8
TOKENS = 32768
N_DP = 8


def plant(drawn, key, least, top_value):
    longest = drawn.shape.index(max(drawn.shape))
    spots = []
    for shift in (0, 1):
        where = [jax.random.randint(jax.random.fold_in(key, axis), (), 0, length) for axis, length in enumerate(drawn.shape)]
        where[longest] = (where[longest] + shift) % drawn.shape[longest]
        spots.append(tuple(where))
    return drawn.at[spots[0]].set(least).at[spots[1]].set(top_value)


def raised(array, rng, source, target, shards_of, factor):
    owner, partner = [(jnp.arange(array.shape[dim]) // (array.shape[dim] // shards_of)).reshape([-1 if axis == dim else 1 for axis in range(array.ndim)]) for dim in (source, target)]
    chosen = jax.random.permutation(rng, shards_of)[partner]
    strong = (owner == chosen) | (owner == (partner + shards_of // 2) % shards_of)
    return jnp.where(strong, factor * array, array)


def block_levels(own_key, extent, cuts, least, high):
    level, own = 1.0, jax.random.fold_in(own_key, 6)
    for dim, parts in cuts:
        steps = jnp.exp(jax.random.uniform(jax.random.fold_in(own, dim), (parts,), jnp.float32, least / len(cuts), high / len(cuts)))
        level = level * jnp.repeat(steps, extent[dim] // parts).reshape([-1 if axis == dim else 1 for axis in range(len(extent))])
    return level


def noise(stream_key, shape, scale, reach, shards=(), kind=jnp.bfloat16):
    factor_of = block_levels(stream_key, shape, shards, -0.22, 0.18) if shards else 1.0
    drawn = jax.random.normal(stream_key, shape, jnp.float32) * scale * factor_of
    return jnp.minimum(jnp.maximum(drawn, -reach), reach).astype(kind)


def heavy_noise(stream_key, extent, deviation, limit, split, heavy, kind=jnp.bfloat16):
    array = deviation * jax.random.normal(stream_key, extent, jnp.float32)
    if split:
        array = array * block_levels(stream_key, extent, split, -0.22, 0.18)
    return jnp.clip(raised(array, jax.random.fold_in(stream_key, 3), *heavy), -limit, limit).astype(kind)


def setup_inputs(seed: int = 0) -> dict:
    keys = jax.random.split(jax.random.key(seed), 13)
    return {
        "tokens": heavy_noise(keys[0], (TOKENS, D), 1.0, 6.0, ((0, 32),), (0, 1, 32, 2.75)),
        "cotangent": heavy_noise(keys[1], (TOKENS, D), 1.0, 6.0, ((0, 32),), (0, 1, 32, 2.75)),
        "tie_index": jax.random.randint(keys[2], (1,), 0, BANK).astype(jnp.int32),
        "image_start": plant(jax.random.randint(keys[3], (SEQUENCES,), 0, SEQ_LEN - IMG + 1), jax.random.fold_in(keys[3], 1), 0, SEQ_LEN - IMG).astype(jnp.int32),
        "qkv_bank": noise(keys[4], (BANK, D, 3, D), D ** -0.5, 0.21875, ((1, 8), (3, 4))),
        "out_bank": noise(keys[5], (BANK, D, D), (max(D * 16 // SEQ_LEN, 1)) ** -0.5, 3.5, ((1, 4), (2, 8))),
        "up_bank": noise(keys[6], (BANK, D, FF), D ** -0.5, 0.21875, ((1, 8), (2, 4))),
        "down_bank": noise(keys[7], (BANK, FF, D), FF ** -0.5, 0.109375, ((1, 4), (2, 8))),
        "gain_bank": jnp.clip(1.0 + 0.15 * jax.random.normal(keys[8], (BANK, 2, D), jnp.float32), 0.25, 1.75).astype(jnp.bfloat16),
        "shift_bank": noise(keys[9], (BANK, 4, D), 0.3, 1.5, ((2, 8),)),
        "head_bias_bank": noise(keys[10], (BANK, 2, D), 0.3, 1.5, ((2, 32),)),
        "hidden_bias_bank": noise(keys[11], (BANK, FF), 0.3, 1.5, ((1, 32),)),
    }


HIGHEST_MODE = lax.Precision.HIGHEST
EPSILON = 1e-05

@jax.custom_vjp
def low(v):
    return lax.optimization_barrier(v.astype(jnp.bfloat16)).astype(jnp.float32)

@jax.custom_vjp
def low_back(v):
    return v

def low_keep(v):
    return (low(v), None)

def low_pass(kept, grad):
    return (grad,)

def back_keep(v):
    return (v, None)

def back_low(kept, grad):
    return (low(grad),)
low.defvjp(low_keep, low_pass)
low_back.defvjp(back_keep, back_low)

def norm_rows(values, gain, shift):
    average = lax.optimization_barrier(jnp.mean(values, axis=-1, keepdims=True))
    centred = values - average
    spread = lax.optimization_barrier(jnp.mean(centred * centred, axis=-1, keepdims=True))
    return centred * lax.rsqrt(spread + EPSILON) * gain + shift

def gelu_tanh(values):
    inner_arg = 0.7978845608028654 * (values + 0.044715 * values * values * values)
    return 0.5 * values * (1.0 + jnp.tanh(inner_arg))

def visible_mask(query_pos, key_pos, span_first):
    causal = key_pos[None, :] <= query_pos[:, None]
    query_in = (query_pos >= span_first) & (query_pos < span_first + IMG)
    key_in = (key_pos >= span_first) & (key_pos < span_first + IMG)
    return causal | query_in[:, None] & key_in[None, :]

def attend_sequence(element):
    queries, keys_low, values, span_first = element
    block_rows = min(512, SEQ_LEN)
    block_count = SEQ_LEN // block_rows
    factor = 1.0 / math.sqrt(HEAD_DIM)
    query_blocks = queries.reshape(block_count, block_rows, HEADS, HEAD_DIM)
    key_heads = keys_low.reshape(SEQ_LEN, HEADS, HEAD_DIM)
    value_heads = values.reshape(SEQ_LEN, HEADS, HEAD_DIM)
    key_pos = jnp.arange(SEQ_LEN, dtype=jnp.int32)

    def one_block(argument):
        query_block, position = argument
        query_pos = position * block_rows + jnp.arange(block_rows, dtype=jnp.int32)
        scores = low_back(jnp.einsum('qhe,khe->hqk', query_block, key_heads, precision=HIGHEST_MODE) * factor)
        visible = visible_mask(query_pos, key_pos, span_first)
        scores = jnp.where(visible[None], scores, -1e+30)
        weights = jax.nn.softmax(scores, axis=-1)
        return jnp.einsum('hqk,khe->qhe', low(weights), value_heads, precision=HIGHEST_MODE)
    mixed_out = lax.map(jax.checkpoint(one_block), (query_blocks, jnp.arange(block_count, dtype=jnp.int32)))
    return mixed_out.reshape(SEQ_LEN, D)

def layer(params, inputs, starts):
    w_qkv, w_out, w_up, w_down, gains, shifts, head_bias, hidden_bias = params
    normed_one = low(norm_rows(inputs, gains[0], shifts[0]))
    projected = jnp.einsum('td,dce->tce', normed_one, w_qkv, precision=HIGHEST_MODE)
    queries = low(low_back(projected[:, 0] + head_bias[0]))
    keys_low = low(low_back(projected[:, 1]))
    values = low(low_back(projected[:, 2] + head_bias[1]))
    shaped = (SEQS, SEQ_LEN, D)
    mixed_out = lax.map(attend_sequence, (queries.reshape(shaped), keys_low.reshape(shaped), values.reshape(shaped), starts))
    mixed_out = low(low_back(mixed_out.reshape(SEQS * SEQ_LEN, D)))
    attended = low_back(jnp.dot(mixed_out, w_out, precision=HIGHEST_MODE) + shifts[2])
    middle = inputs + attended
    normed_two = low(norm_rows(middle, gains[1], shifts[1]))
    pre_act = low_back(jnp.dot(normed_two, w_up, precision=HIGHEST_MODE) + hidden_bias)
    activ = low(gelu_tanh(pre_act))
    branch = low_back(jnp.dot(activ, w_down, precision=HIGHEST_MODE) + shifts[3])
    return middle + branch

def reference(tokens, cotangent, tie_index, image_start, qkv_bank, out_bank, up_bank, down_bank, gain_bank, shift_bank, head_bias_bank, hidden_bias_bank):
    chosen = tie_index[0]
    banks = (qkv_bank, out_bank, up_bank, down_bank, gain_bank, shift_bank, head_bias_bank, hidden_bias_bank)
    params = tuple((lax.dynamic_index_in_dim(stored, chosen, 0, keepdims=False).astype(jnp.float32) for stored in banks))
    group_rows = SEQS * SEQ_LEN
    inputs = tokens.astype(jnp.float32).reshape(N_DP, group_rows, D)
    grads_in = cotangent.astype(jnp.float32).reshape(N_DP, group_rows, D)
    starts = image_start.reshape(N_DP, SEQS)

    def one_group(totals, element):
        group_in, group_cot, group_starts = element

        def forward(weights_now, values_now):
            return layer(weights_now, values_now, group_starts)
        result, pull_back = jax.vjp(forward, params, group_in)
        grad_params, grad_input = pull_back(group_cot)
        totals = tuple((running + fresh for running, fresh in zip(totals, grad_params)))
        return (totals, (result.astype(jnp.bfloat16), grad_input.astype(jnp.bfloat16)))
    initial = tuple((jnp.zeros_like(weight_now) for weight_now in params))
    totals, (results, grad_inputs) = lax.scan(one_group, initial, (inputs, grads_in, starts))
    return (results.reshape(TOKENS, D), grad_inputs.reshape(TOKENS, D), totals[0], totals[1], totals[2], totals[3], totals[4], totals[5], totals[6], totals[7])
```

```python
import functools
import math

import jax
import jax.numpy as jnp
from jax import lax
from jax.experimental import pallas as pl
from jax.experimental.pallas import tpu as pltpu
from jax.sharding import PartitionSpec as P

HEAD_DIM = 64
SEQ_LEN = 4096
IMG = 256
EPSILON = 1e-05
LOG2E = 1.4426950408889634
BLOCK = 512
BLOCKS = SEQ_LEN // BLOCK
QUARTERS = 4
QUARTER = SEQ_LEN // QUARTERS
PER_QUARTER = QUARTER // BLOCK
PAIRS = BLOCKS * (BLOCKS + 1) // 2
F32 = jnp.float32
BF16 = jnp.bfloat16

NT = (((1,), (1,)), ((), ()))
NN = (((1,), (0,)), ((), ()))
TN = (((0,), (0,)), ((), ()))
CT = (((0,), (1,)), ((), ()))


def product(left, right, dims):
    return lax.dot_general(left, right, dims, preferred_element_type=F32)


def place(block, own):
    quarter = jnp.bitwise_xor(block // PER_QUARTER, own)
    return pl.multiple_of((quarter * PER_QUARTER + block % PER_QUARTER) * BLOCK, BLOCK)


def following(row, col, cross):
    wrap = col + 1 >= row + 1 + jnp.where(cross == row, 1, 0)
    return jnp.where(wrap, row + 1, row), jnp.where(wrap, 0, col + 1)


def crossing(start):
    low, high = start // BLOCK, (start + IMG - 1) // BLOCK
    cross = jnp.where(high > low, low, -1)
    return cross, PAIRS + jnp.where(cross >= 0, 1, 0)


def last_key(pos, start):
    return jnp.where((pos >= start) & (pos < start + IMG), start + (IMG - 1), pos)


def forward_kernel(
    info, q_ref, k_ref, v_ref, o_ref, lse_ref, k_rows, v_ones, s_a, s_b, top_a, top_b, top, total
):
    start, own = info[0], info[1]
    cross, pairs = crossing(start)

    def prepare(block, carry):
        at = pl.ds(pl.multiple_of(block * BLOCK, BLOCK), BLOCK)
        k_rows[at, :] = k_ref[0, 0, :, at].astype(F32).T.astype(BF16)
        return carry

    lax.fori_loop(0, BLOCKS, prepare, 0)
    v_ones[0:64, :] = v_ref[0, 0]
    v_ones[64:80, :] = jnp.ones((16, SEQ_LEN), BF16)
    total[...] = jnp.zeros_like(total)

    def score(row, col, dst, dst_top, masked):
        rows = pl.ds(place(jnp.minimum(row, BLOCKS - 1), own), BLOCK)
        s = product(k_rows[pl.ds(place(col, own), BLOCK), :], q_ref[0, 0, :, rows], NN)
        if masked:
            pos = row * BLOCK + lax.broadcasted_iota(jnp.int32, (1, BLOCK), 1)
            limit = last_key(pos, start) - col * BLOCK
            s = jnp.where(lax.broadcasted_iota(jnp.int32, (BLOCK, BLOCK), 0) <= limit, s, -1e30)
        dst[...] = s
        dst_top[...] = jnp.max(s, axis=0, keepdims=True)

    def step(src, src_top, dst, dst_top, col, next_row, next_col, masked):
        score(next_row, next_col, dst, dst_top, masked)
        old = jnp.where(col == 0, -1e30, top[...])
        new = jnp.maximum(old, src_top[...])
        p = jnp.exp2(src[...] - new).astype(BF16)
        mixed = product(v_ones[:, pl.ds(place(col, own), BLOCK)], p, NN)
        total[...] = total[...] * jnp.exp2(old - new) + mixed
        top[...] = new

    def half(src, src_top, dst, dst_top, row, col):
        next_row, next_col = following(row, col, cross)
        masked = next_col >= next_row

        @pl.when(masked)
        def _():
            step(src, src_top, dst, dst_top, col, next_row, next_col, True)

        @pl.when(jnp.logical_not(masked))
        def _():
            step(src, src_top, dst, dst_top, col, next_row, next_col, False)

        @pl.when(next_col == 0)
        def _():
            at = pl.ds(place(row, own), BLOCK)
            summed = total[64:65]
            o_ref[:, at] = (total[0:64] / summed).astype(BF16)
            lse_ref[:, at] = top[...] + jnp.log2(summed)

        return next_row, next_col

    score(0, 0, s_a, top_a, True)

    def both(turn, carry):
        row, col = half(s_a, top_a, s_b, top_b, *carry)
        return half(s_b, top_b, s_a, top_a, row, col)

    row, col = lax.fori_loop(0, pairs // 2, both, (jnp.int32(0), jnp.int32(0)))

    @pl.when(pairs % 2 == 1)
    def _():
        half(s_a, top_a, s_b, top_b, row, col)


def head_spec(head, part):
    return pl.BlockSpec((1, 1, HEAD_DIM, SEQ_LEN), lambda i, info: (head, part, 0, 0))


def attend_forward(info, qkv, head):
    whole = lambda rows: pl.BlockSpec((rows, SEQ_LEN), lambda i, info: (0, 0))
    return pl.pallas_call(
        forward_kernel,
        grid_spec=pltpu.PrefetchScalarGridSpec(
            num_scalar_prefetch=1,
            grid=(1,),
            in_specs=[head_spec(head, part) for part in range(3)],
            out_specs=[whole(HEAD_DIM), whole(1)],
            scratch_shapes=[
                pltpu.VMEM((SEQ_LEN, HEAD_DIM), BF16),
                pltpu.VMEM((80, SEQ_LEN), BF16),
                pltpu.VMEM((BLOCK, BLOCK), F32),
                pltpu.VMEM((BLOCK, BLOCK), F32),
                pltpu.VMEM((1, BLOCK), F32),
                pltpu.VMEM((1, BLOCK), F32),
                pltpu.VMEM((1, BLOCK), F32),
                pltpu.VMEM((80, BLOCK), F32),
            ],
        ),
        out_shape=[
            jax.ShapeDtypeStruct((HEAD_DIM, SEQ_LEN), BF16),
            jax.ShapeDtypeStruct((1, SEQ_LEN), F32),
        ],
        cost_estimate=pl.CostEstimate(
            flops=18_000_000_000, bytes_accessed=2_200_000, transcendentals=9_000_000
        ),
        name="attend_forward",
    )(info, qkv, qkv, qkv)


def pieces(values):
    high = values.astype(BF16).astype(F32)
    rest = values - high
    middle = rest.astype(BF16).astype(F32)
    return [high, middle, (rest - middle).astype(BF16).astype(F32)]


def backward_kernel(
    info, q_ref, k_ref, v_ref, g_ref, o_ref, lse_ref, d_ref,
    q_wide, k_wide, v_wide, g_wide, p_a, ds_a, p_b, ds_b, dq, dk, dv,
):
    start, own = info[0], info[1]
    cross, pairs = crossing(start)

    def prepare(block, carry):
        at = pl.ds(pl.multiple_of(block * BLOCK, BLOCK), BLOCK)
        ones = [jnp.ones((1, BLOCK), F32)] * 3

        def widen(columns, rows):
            rest = jnp.zeros((HEAD_DIM - 3, BLOCK), F32)
            return jnp.concatenate([columns.astype(F32)] + rows + [rest], axis=0).T.astype(BF16)

        grad = g_ref[:, at]
        centre = jnp.sum(grad.astype(F32) * o_ref[:, at].astype(F32), axis=0, keepdims=True)
        q_wide[at, :] = widen(q_ref[0, 0, :, at], pieces(-lse_ref[:, at]))
        k_wide[at, :] = widen(k_ref[0, 0, :, at], ones)
        v_wide[at, :] = widen(v_ref[0, 0, :, at], ones)
        g_wide[at, :] = widen(grad, pieces(-centre))
        return carry

    lax.fori_loop(0, BLOCKS, prepare, 0)
    dq[...] = jnp.zeros_like(dq)
    dk[...] = jnp.zeros_like(dk)
    dv[...] = jnp.zeros_like(dv)

    def score(row, col, p_dst, ds_dst, masked):
        rows = pl.ds(place(jnp.minimum(row, BLOCKS - 1), own), BLOCK)
        cols = pl.ds(place(col, own), BLOCK)
        s = product(q_wide[rows, :], k_wide[cols, :], NT)
        grad_p = product(g_wide[rows, :], v_wide[cols, :], NT)
        if masked:
            pos = row * BLOCK + lax.broadcasted_iota(jnp.int32, (BLOCK, 1), 0)
            limit = last_key(pos, start) - col * BLOCK
            s = jnp.where(lax.broadcasted_iota(jnp.int32, (BLOCK, BLOCK), 1) <= limit, s, -1e30)
        p = jnp.exp2(s)
        p_dst[...] = p.astype(BF16)
        ds_dst[...] = (p * grad_p).astype(BF16)

    def step(p, ds, p_dst, ds_dst, row, col, next_row, next_col, masked):
        score(next_row, next_col, p_dst, ds_dst, masked)
        rows = pl.ds(place(row, own), BLOCK)
        cols = pl.ds(place(col, own), BLOCK)
        dv[:, cols] += product(g_ref[:, rows], p[...], NN)
        dk[:, cols] += product(q_ref[0, 0, :, rows], ds[...], NN)
        dq[:, rows] += product(k_ref[0, 0, :, cols], ds[...], NT)

    def half(p, ds, p_dst, ds_dst, row, col):
        next_row, next_col = following(row, col, cross)
        masked = next_col >= next_row

        @pl.when(masked)
        def _():
            step(p, ds, p_dst, ds_dst, row, col, next_row, next_col, True)

        @pl.when(jnp.logical_not(masked))
        def _():
            step(p, ds, p_dst, ds_dst, row, col, next_row, next_col, False)

        return next_row, next_col

    score(0, 0, p_a, ds_a, True)

    def both(turn, carry):
        row, col = half(p_a, ds_a, p_b, ds_b, *carry)
        return half(p_b, ds_b, p_a, ds_a, row, col)

    row, col = lax.fori_loop(0, pairs // 2, both, (jnp.int32(0), jnp.int32(0)))

    @pl.when(pairs % 2 == 1)
    def _():
        half(p_a, ds_a, p_b, ds_b, row, col)

    d_ref[0:64, :] = (dq[...] * 0.125).astype(BF16)
    d_ref[64:128, :] = (dk[...] * (1.0 / LOG2E)).astype(BF16)
    d_ref[128:192, :] = dv[...].astype(BF16)


def attend_backward(info, qkv, grad, out, lse, head):
    whole = lambda rows: pl.BlockSpec((rows, SEQ_LEN), lambda i, info: (0, 0))
    return pl.pallas_call(
        backward_kernel,
        grid_spec=pltpu.PrefetchScalarGridSpec(
            num_scalar_prefetch=1,
            grid=(1,),
            in_specs=[head_spec(head, part) for part in range(3)]
            + [whole(HEAD_DIM), whole(HEAD_DIM), whole(1)],
            out_specs=whole(3 * HEAD_DIM),
            scratch_shapes=[pltpu.VMEM((SEQ_LEN, 128), BF16)] * 4
            + [pltpu.VMEM((BLOCK, BLOCK), BF16)] * 4
            + [pltpu.VMEM((HEAD_DIM, SEQ_LEN), F32)] * 3,
        ),
        out_shape=jax.ShapeDtypeStruct((3 * HEAD_DIM, SEQ_LEN), BF16),
        cost_estimate=pl.CostEstimate(
            flops=32_000_000_000, bytes_accessed=4_500_000, transcendentals=9_000_000
        ),
        name="attend_backward",
    )(info, qkv, qkv, qkv, grad, out, lse)


def normalise(values):
    centred = values - jnp.mean(values, axis=-1, keepdims=True)
    scale = lax.rsqrt(jnp.mean(centred * centred, axis=-1, keepdims=True) + EPSILON)
    return centred * scale, scale


def normalise_back(grad, unit, scale):
    return scale * (
        grad
        - jnp.mean(grad, axis=-1, keepdims=True)
        - unit * jnp.mean(grad * unit, axis=-1, keepdims=True)
    )


def gelu_both(u):
    inner = 0.7978845608028654 * (u + 0.044715 * u * u * u)
    bent = jnp.tanh(inner)
    slope = 0.7978845608028654 * (1.0 + 3 * 0.044715 * u * u)
    return 0.5 * u * (1.0 + bent), 0.5 * (1.0 + bent) + 0.5 * u * (1.0 - bent * bent) * slope


def swap(values, mask):
    return lax.ppermute(values, "tensor", [(i, i ^ mask) for i in range(QUARTERS)])


def gather_dp(part, count):
    if count > 8:
        return lax.all_gather(part, "dp", axis=0, tiled=False)
    ring = [part] + [
        lax.ppermute(part, "dp", [((i + k) % count, i) for i in range(count)])
        for k in range(1, count)
    ]
    twice = jnp.stack(ring + ring)
    first = lax.rem(count - lax.axis_index("dp"), count)
    return lax.dynamic_slice_in_dim(twice, first, count, 0)


def local(
    n_dp,
    tokens,
    cotangent,
    tie_index,
    image_start,
    qkv_bank,
    out_bank,
    up_bank,
    down_bank,
    gain_bank,
    shift_bank,
    head_bias_bank,
    hidden_bias_bank,
):
    own = lax.axis_index("tensor")
    chosen = tie_index[0]
    pick = lambda bank: lax.dynamic_index_in_dim(bank, chosen, 0, keepdims=False)
    width = tokens.shape[1]
    rows = qkv_bank.shape[1]
    local_width = qkv_bank.shape[3]
    heads = local_width // HEAD_DIM
    qkv_cols = 3 * local_width
    info = jnp.stack([image_start[0], own]).astype(jnp.int32)

    qkv_part = (
        pick(qkv_bank).reshape(rows, 3, heads, HEAD_DIM).transpose(0, 2, 1, 3).reshape(rows, qkv_cols)
    )
    out_part = pick(out_bank).T
    up_part = pick(up_bank)
    down_part = pick(down_bank).T
    gain_part = pick(gain_bank)
    shift_part = pick(shift_bank)
    head_part = pick(head_bias_bank)
    hidden_part = pick(hidden_bias_bank)
    few = head_part.shape[1]
    hidden_cols = up_part.shape[1]

    near = swap(tokens, 1)
    far = swap(tokens, 2)
    far_near = swap(far, 1)

    small = jnp.concatenate([gain_part.reshape(-1), shift_part.reshape(-1), head_part.reshape(-1)])
    small_rows = -(-small.shape[0] // qkv_cols)
    pad_rows = -(-small_rows // 16) * 16
    small = jnp.pad(small, (0, pad_rows * qkv_cols - small.shape[0])).reshape(pad_rows, qkv_cols)
    gathered = gather_dp(jnp.concatenate([qkv_part, small]), n_dp)
    w_qkv = gathered[:, :rows].reshape(width, qkv_cols)
    small = gathered[:, rows:].reshape(n_dp, -1).astype(F32)
    gains = small[:, : 2 * rows].reshape(n_dp, 2, rows).transpose(1, 0, 2).reshape(2, width)
    shifts = (
        small[:, 2 * rows : 6 * rows].reshape(n_dp, 4, rows).transpose(1, 0, 2).reshape(4, width)
    )
    head_bias = (
        small[:, 6 * rows : 6 * rows + 2 * few]
        .reshape(n_dp, 2, few)
        .transpose(1, 0, 2)
        .reshape(2, heads, 1, HEAD_DIM)
    )

    bank_part = jnp.concatenate(
        [
            up_part,
            down_part,
            out_part,
            qkv_part,
            jnp.pad(hidden_part.reshape(rows, -1), ((0, 0), (0, 127)))
            if hidden_part.shape[0] == rows
            else jnp.zeros((rows, 128), BF16),
        ],
        axis=1,
    )
    bank = lax.all_gather(bank_part, ("tensor", "dp"), axis=0, tiled=True)
    c_down, c_out, c_qkv, c_bias = (
        hidden_cols,
        2 * hidden_cols,
        2 * hidden_cols + local_width,
        2 * hidden_cols + local_width + qkv_cols,
    )
    block_of = lambda x: jnp.bitwise_xor(own, x) * width
    out_t = jnp.concatenate(
        [
            lax.dynamic_slice(bank, (block_of(x), c_out), (width, local_width))
            for x in range(QUARTERS)
        ],
        axis=1,
    )
    qkv_t = [
        lax.dynamic_slice(bank, (block_of(x), c_qkv), (width, qkv_cols)) for x in range(QUARTERS)
    ]

    zero_bias = jnp.zeros((heads, 1, HEAD_DIM), F32)
    bias = jnp.concatenate([head_bias[0], zero_bias, head_bias[1]], axis=1)[..., None]
    scale = jnp.array([LOG2E / 8.0, 1.0, 1.0], F32).reshape(1, 3, 1, 1)
    normed, projected = [], []
    for part in (tokens, near, far, far_near):
        unit, _ = normalise(part.astype(F32))
        rounded = (unit * gains[0] + shifts[0]).astype(BF16)
        flat = product(w_qkv, rounded, CT).reshape(heads, 3, HEAD_DIM, QUARTER)
        normed.append(rounded)
        projected.append(((flat + bias) * scale).astype(BF16))
    qkv = jnp.concatenate(projected, axis=3)
    normed = jnp.concatenate(normed, axis=0)

    outs, lses, mixed = [], [], [[None] * heads for _ in range(QUARTERS)]
    for head in range(heads):
        out, lse = attend_forward(info, qkv, head)
        outs.append(out)
        lses.append(lse)
        for x in range(QUARTERS):
            part = out[:, x * QUARTER : (x + 1) * QUARTER]
            mixed[x][head] = swap(part, x) if x else part
    mixed = jnp.concatenate([part for quarter in mixed for part in quarter], axis=0)

    inputs = tokens.astype(F32)
    middle = inputs + product(mixed, out_t, CT) + shifts[2]
    unit_two, scale_two = normalise(middle)
    normed_two = (unit_two * gains[1] + shifts[1]).astype(BF16)

    branch, grad_two = 0.0, 0.0
    grad_up, grad_down, grad_hidden = [], [], []
    for k in range(QUARTERS):
        w_up = bank[k * width : (k + 1) * width, :c_down]
        w_down = bank[k * width : (k + 1) * width, c_down:c_out]
        hidden_bias = bank[k * width : (k + 1) * width, c_bias].astype(F32)
        u = product(normed_two, w_up, NN) + hidden_bias
        value, slope = gelu_both(u)
        activ = value.astype(BF16)
        branch = branch + product(activ, w_down, NT)
        grad_u = (product(cotangent, w_down, NN) * slope).astype(BF16)
        grad_two = grad_two + product(grad_u, w_up, NT)
        grad_up.append(product(normed_two, grad_u, TN).astype(BF16))
        grad_down.append(product(cotangent, activ, TN).astype(BF16))
        grad_hidden.append(jnp.sum(grad_u, axis=0, dtype=F32))
    result = (middle + branch + shifts[3]).astype(BF16)

    grad_result = cotangent.astype(F32)
    grad_middle = grad_result + normalise_back(grad_two * gains[1], unit_two, scale_two)
    grad_low = grad_middle.astype(BF16)

    grad_out = product(grad_low, mixed, CT).astype(BF16)
    grads = jnp.concatenate(
        [
            jnp.concatenate(grad_up, axis=0),
            jnp.concatenate(grad_down, axis=0),
            jnp.zeros((QUARTERS * width, local_width), BF16),
        ],
        axis=1,
    )
    for x in range(QUARTERS):
        grads = lax.dynamic_update_slice(
            grads, grad_out[:, x * local_width : (x + 1) * local_width], (block_of(x), c_out)
        )
    shard = lax.psum_scatter(grads, ("tensor", "dp"), scatter_dimension=0, tiled=True).astype(F32)

    grad_mixed = product(out_t, grad_low, CT).astype(BF16)
    grad_one = 0.0
    grad_qkv, sums = [], []
    for head in range(heads):
        parts = []
        for x in range(QUARTERS):
            first = x * local_width + head * HEAD_DIM
            part = grad_mixed[first : first + HEAD_DIM]
            parts.append(swap(part, x) if x else part)
        deltas = attend_backward(
            info, qkv, jnp.concatenate(parts, axis=1), outs[head], lses[head], head
        )
        span = 3 * HEAD_DIM
        parts = []
        for x in range(QUARTERS):
            part = deltas[:, x * QUARTER : (x + 1) * QUARTER]
            parts.append(swap(part, x) if x else part)
        weights = jnp.concatenate([w[:, head * span : (head + 1) * span] for w in qkv_t], axis=1)
        grad_one = grad_one + product(jnp.concatenate(parts, axis=0), weights, CT)
        grad_qkv.append(product(normed, deltas, CT))
        sums.append(jnp.sum(deltas, axis=1, dtype=F32))
    grad_qkv = jnp.concatenate(grad_qkv, axis=1)
    sums = jnp.concatenate(sums)

    unit_one, scale_one = normalise(inputs)
    grad_tokens = (grad_middle + normalise_back(grad_one * gains[0], unit_one, scale_one)).astype(
        BF16
    )

    stats = jnp.stack(
        [
            jnp.sum(grad_two * unit_two, axis=0),
            jnp.sum(grad_two, axis=0),
            jnp.sum(grad_low, axis=0, dtype=F32),
            jnp.sum(grad_result, axis=0),
        ]
        + grad_hidden
    )
    kinds = stats.shape[0]
    stats = stats.reshape(kinds, n_dp, rows).transpose(1, 0, 2).reshape(n_dp, kinds * rows)
    stats = jnp.concatenate([stats, jnp.broadcast_to(sums, (n_dp, qkv_cols))], axis=1)
    length = stats.shape[1]
    stats = jnp.concatenate(pieces(stats), axis=1).astype(BF16)
    stat_rows = -(-3 * length // (16 * qkv_cols)) * 16
    stats = jnp.pad(stats, ((0, 0), (0, stat_rows * qkv_cols - 3 * length)))
    send = jnp.concatenate(
        [
            grad_qkv.astype(BF16).reshape(n_dp, rows, qkv_cols),
            stats.reshape(n_dp, stat_rows, qkv_cols),
        ],
        axis=1,
    )
    received = lax.all_to_all(send, "dp", 0, 0)
    qkv_total = jnp.sum(received[:, :rows], axis=0, dtype=F32)
    stats = jnp.sum(received[:, rows:], axis=0, dtype=F32).reshape(-1)[: 3 * length]
    stats = jnp.sum(stats.reshape(3, length), axis=0)
    sums = stats[kinds * rows :]

    shard_weights = qkv_part.astype(F32)
    shift_one = jnp.sum(shard_weights * sums, axis=1)
    gain_one = (
        jnp.sum(shard_weights * qkv_total, axis=1) - shift_part[0].astype(F32) * shift_one
    ) / gain_part[0].astype(F32)
    stats = jnp.concatenate([stats[: kinds * rows].reshape(kinds, rows), shift_one[None], gain_one[None]])
    stats = stats + swap(stats, 2)
    stats = stats + swap(stats, 1)

    qkv_shard = (
        qkv_total.reshape(rows, heads, 3, HEAD_DIM).transpose(0, 2, 1, 3).reshape(rows, 3, local_width)
    )
    by_part = sums.reshape(heads, 3, HEAD_DIM)
    head_sums = jnp.stack([by_part[:, 0].reshape(-1), by_part[:, 2].reshape(-1)])
    head_shard = lax.dynamic_slice_in_dim(head_sums, lax.axis_index("dp") * few, few, 1)
    hidden_shard = lax.dynamic_index_in_dim(stats[4:8], own, 0, keepdims=False)
    return (
        result,
        grad_tokens,
        qkv_shard,
        shard[:, c_out:].T,
        shard[:, :c_down],
        shard[:, c_down:c_out].T,
        jnp.stack([stats[9], stats[0]]),
        jnp.stack([stats[8], stats[1], stats[2], stats[3]]),
        head_shard,
        hidden_shard,
    )


def solution(mesh):
    placed = (
        P(("dp", "tensor"), None),
        P(("dp", "tensor"), None),
        P(),
        P("dp"),
        P(None, "dp", None, "tensor"),
        P(None, "tensor", "dp"),
        P(None, "dp", "tensor"),
        P(None, "tensor", "dp"),
        P(None, None, "dp"),
        P(None, None, "dp"),
        P(None, None, ("tensor", "dp")),
        P(None, ("tensor", "dp")),
    )
    return jax.shard_map(
        functools.partial(local, mesh.shape["dp"]),
        mesh=mesh,
        in_specs=placed,
        out_specs=(
            P(("dp", "tensor"), None),
            P(("dp", "tensor"), None),
            P("dp", None, "tensor"),
            P("tensor", "dp"),
            P("dp", "tensor"),
            P("tensor", "dp"),
            P(None, "dp"),
            P(None, "dp"),
            P(None, ("tensor", "dp")),
            P(("tensor", "dp")),
        ),
        check_vma=False,
    )
```

```python
import functools
import math

import jax
import jax.numpy as jnp
from jax import lax
from jax.experimental import pallas as pl
from jax.experimental.pallas import tpu as pltpu
from jax.sharding import PartitionSpec as P

HEAD_DIM = 64
SEQ_LEN = 4096
IMG = 256
EPSILON = 1e-05
LOG2E = 1.4426950408889634
BLOCK = 512
BLOCKS = SEQ_LEN // BLOCK
QUARTERS = 4
QUARTER = SEQ_LEN // QUARTERS
PER_QUARTER = QUARTER // BLOCK
PAIRS = BLOCKS * (BLOCKS + 1) // 2
F32 = jnp.float32
BF16 = jnp.bfloat16

NT = (((1,), (1,)), ((), ()))
NN = (((1,), (0,)), ((), ()))
TN = (((0,), (0,)), ((), ()))
CT = (((0,), (1,)), ((), ()))


def product(left, right, dims):
    return lax.dot_general(left, right, dims, preferred_element_type=F32)


def place(block, own):
    quarter = jnp.bitwise_xor(block // PER_QUARTER, own)
    return pl.multiple_of((quarter * PER_QUARTER + block % PER_QUARTER) * BLOCK, BLOCK)


def following(row, col, cross):
    wrap = col + 1 >= row + 1 + jnp.where(cross == row, 1, 0)
    return jnp.where(wrap, row + 1, row), jnp.where(wrap, 0, col + 1)


def crossing(start):
    low, high = start // BLOCK, (start + IMG - 1) // BLOCK
    cross = jnp.where(high > low, low, -1)
    return cross, PAIRS + jnp.where(cross >= 0, 1, 0)


def last_key(pos, start):
    return jnp.where((pos >= start) & (pos < start + IMG), start + (IMG - 1), pos)


def forward_kernel(
    skip, info, q_ref, k_ref, v_ref, *refs
):
    o_0, o_1, o_2, o_3, lse_ref, k_rows, v_ones, s_a, s_b, top_a, top_b, top, total, o_all = refs[skip:]
    start, own = info[0], info[1]
    cross, pairs = crossing(start)

    def prepare(block, carry):
        at = pl.ds(pl.multiple_of(block * BLOCK, BLOCK), BLOCK)
        k_rows[at, :] = k_ref[:, at].astype(F32).T.astype(BF16)
        return carry

    lax.fori_loop(0, BLOCKS, prepare, 0)
    v_ones[0:64, :] = v_ref[...]
    v_ones[64:80, :] = jnp.ones((16, SEQ_LEN), BF16)
    total[...] = jnp.zeros_like(total)

    def score(row, col, dst, dst_top, masked):
        rows = pl.ds(place(jnp.minimum(row, BLOCKS - 1), own), BLOCK)
        s = product(k_rows[pl.ds(place(col, own), BLOCK), :], q_ref[:, rows], NN)
        if masked:
            pos = row * BLOCK + lax.broadcasted_iota(jnp.int32, (1, BLOCK), 1)
            limit = last_key(pos, start) - col * BLOCK
            s = jnp.where(lax.broadcasted_iota(jnp.int32, (BLOCK, BLOCK), 0) <= limit, s, -1e30)
        dst[...] = s
        dst_top[...] = jnp.max(s, axis=0, keepdims=True)

    def step(src, src_top, dst, dst_top, col, next_row, next_col, masked):
        score(next_row, next_col, dst, dst_top, masked)
        old = jnp.where(col == 0, -1e30, top[...])
        new = jnp.maximum(old, src_top[...])
        p = jnp.exp2(src[...] - new).astype(BF16)
        mixed = product(v_ones[:, pl.ds(place(col, own), BLOCK)], p, NN)
        total[...] = total[...] * jnp.exp2(old - new) + mixed
        top[...] = new

    def half(src, src_top, dst, dst_top, row, col):
        next_row, next_col = following(row, col, cross)
        masked = next_col >= next_row

        @pl.when(masked)
        def _():
            step(src, src_top, dst, dst_top, col, next_row, next_col, True)

        @pl.when(jnp.logical_not(masked))
        def _():
            step(src, src_top, dst, dst_top, col, next_row, next_col, False)

        @pl.when(next_col == 0)
        def _():
            at = pl.ds(place(row, own), BLOCK)
            summed = total[64:65]
            o_all[:, at] = (total[0:64] / summed).astype(BF16)
            lse_ref[:, at] = top[...] + jnp.log2(summed)

        return next_row, next_col

    score(0, 0, s_a, top_a, True)

    def both(turn, carry):
        row, col = half(s_a, top_a, s_b, top_b, *carry)
        return half(s_b, top_b, s_a, top_a, row, col)

    row, col = lax.fori_loop(0, pairs // 2, both, (jnp.int32(0), jnp.int32(0)))

    @pl.when(pairs % 2 == 1)
    def _():
        half(s_a, top_a, s_b, top_b, row, col)

    for x, o_ref in enumerate((o_0, o_1, o_2, o_3)):
        o_ref[...] = o_all[:, x * QUARTER : (x + 1) * QUARTER]


def head_spec(head, part):
    return pl.BlockSpec((HEAD_DIM, SEQ_LEN), lambda i, info: (head * 3 + part, 0))


def whole(*shape):
    return pl.BlockSpec(shape, lambda i, info: (0, 0), pipeline_mode=pl.Buffered(1))


ANYWHERE = pl.BlockSpec(memory_space=pl.ANY)
SHORT = pl.CostEstimate(flops=1, bytes_accessed=1, transcendentals=0)


def attend_forward(info, qkv, head, after):
    return pl.pallas_call(
        functools.partial(forward_kernel, len(after)),
        grid_spec=pltpu.PrefetchScalarGridSpec(
            num_scalar_prefetch=1,
            grid=(1,),
            in_specs=[head_spec(head, part) for part in range(3)] + [ANYWHERE] * len(after),
            out_specs=[whole(HEAD_DIM, QUARTER)] * QUARTERS + [whole(1, SEQ_LEN)],
            scratch_shapes=[
                pltpu.VMEM((SEQ_LEN, HEAD_DIM), BF16),
                pltpu.VMEM((80, SEQ_LEN), BF16),
                pltpu.VMEM((BLOCK, BLOCK), F32),
                pltpu.VMEM((BLOCK, BLOCK), F32),
                pltpu.VMEM((1, BLOCK), F32),
                pltpu.VMEM((1, BLOCK), F32),
                pltpu.VMEM((1, BLOCK), F32),
                pltpu.VMEM((80, BLOCK), F32),
                pltpu.VMEM((HEAD_DIM, SEQ_LEN), BF16),
            ],
        ),
        out_shape=[jax.ShapeDtypeStruct((HEAD_DIM, QUARTER), BF16)] * QUARTERS
        + [jax.ShapeDtypeStruct((1, SEQ_LEN), F32)],
        cost_estimate=pl.CostEstimate(
            flops=18_000_000_000, bytes_accessed=2_200_000, transcendentals=9_000_000
        ),
        name="attend_forward",
    )(info, qkv, qkv, qkv, *after)


def pieces(values):
    high = values.astype(BF16).astype(F32)
    rest = values - high
    middle = rest.astype(BF16).astype(F32)
    return [high, middle, (rest - middle).astype(BF16).astype(F32)]


def backward_kernel(
    skip, info, q_ref, k_ref, v_ref, g_0, g_1, g_2, g_3, o_0, o_1, o_2, o_3, lse_ref, normed_ref, *refs
):
    d_0, d_1, d_2, d_3, weight_ref, sums_ref, *refs = refs[skip:]
    g_ref, q_wide, k_wide, v_wide, g_wide, p_a, ds_a, p_b, ds_b, *refs = refs
    dq, dk, dv, d_ref, normed, arrived = refs
    start, own = info[0], info[1]
    cross, pairs = crossing(start)
    fetch = pltpu.make_async_copy(normed_ref, normed, arrived)
    fetch.start()
    ones = [jnp.ones((1, BLOCK), F32)] * 3

    def widen(columns, rows):
        rest = jnp.zeros((HEAD_DIM - 3, BLOCK), F32)
        return jnp.concatenate([columns.astype(F32)] + rows + [rest], axis=0).T.astype(BF16)

    for x, (g_part, o_part) in enumerate(zip((g_0, g_1, g_2, g_3), (o_0, o_1, o_2, o_3))):

        def prepare(block, carry):
            here = pl.ds(pl.multiple_of(block * BLOCK, BLOCK), BLOCK)
            at = pl.ds(pl.multiple_of(x * QUARTER + block * BLOCK, BLOCK), BLOCK)
            grad = g_part[:, here]
            g_ref[:, at] = grad
            centre = jnp.sum(
                grad.astype(F32) * o_part[:, here].astype(F32), axis=0, keepdims=True
            )
            q_wide[at, :] = widen(q_ref[:, at], pieces(-lse_ref[:, at]))
            k_wide[at, :] = widen(k_ref[:, at], ones)
            v_wide[at, :] = widen(v_ref[:, at], ones)
            g_wide[at, :] = widen(grad, pieces(-centre))
            return carry

        lax.fori_loop(0, PER_QUARTER, prepare, 0)
    dq[...] = jnp.zeros_like(dq)
    dk[...] = jnp.zeros_like(dk)
    dv[...] = jnp.zeros_like(dv)

    def score(row, col, p_dst, ds_dst, masked):
        rows = pl.ds(place(jnp.minimum(row, BLOCKS - 1), own), BLOCK)
        cols = pl.ds(place(col, own), BLOCK)
        s = product(q_wide[rows, :], k_wide[cols, :], NT)
        grad_p = product(g_wide[rows, :], v_wide[cols, :], NT)
        if masked:
            pos = row * BLOCK + lax.broadcasted_iota(jnp.int32, (BLOCK, 1), 0)
            limit = last_key(pos, start) - col * BLOCK
            s = jnp.where(lax.broadcasted_iota(jnp.int32, (BLOCK, BLOCK), 1) <= limit, s, -1e30)
        p = jnp.exp2(s)
        p_dst[...] = p.astype(BF16)
        ds_dst[...] = (p * grad_p).astype(BF16)

    def step(p, ds, p_dst, ds_dst, row, col, next_row, next_col, masked):
        score(next_row, next_col, p_dst, ds_dst, masked)
        rows = pl.ds(place(row, own), BLOCK)
        cols = pl.ds(place(col, own), BLOCK)
        dv[:, cols] += product(g_ref[:, rows], p[...], NN)
        dk[:, cols] += product(q_ref[:, rows], ds[...], NN)
        dq[:, rows] += product(k_ref[:, cols], ds[...], NT)

    def half(p, ds, p_dst, ds_dst, row, col):
        next_row, next_col = following(row, col, cross)
        masked = next_col >= next_row

        @pl.when(masked)
        def _():
            step(p, ds, p_dst, ds_dst, row, col, next_row, next_col, True)

        @pl.when(jnp.logical_not(masked))
        def _():
            step(p, ds, p_dst, ds_dst, row, col, next_row, next_col, False)

        return next_row, next_col

    score(0, 0, p_a, ds_a, True)

    def both(turn, carry):
        row, col = half(p_a, ds_a, p_b, ds_b, *carry)
        return half(p_b, ds_b, p_a, ds_a, row, col)

    row, col = lax.fori_loop(0, pairs // 2, both, (jnp.int32(0), jnp.int32(0)))

    @pl.when(pairs % 2 == 1)
    def _():
        half(p_a, ds_a, p_b, ds_b, row, col)

    d_ref[0:64, :] = (dq[...] * 0.125).astype(BF16)
    d_ref[64:128, :] = (dk[...] * (1.0 / LOG2E)).astype(BF16)
    d_ref[128:192, :] = dv[...].astype(BF16)
    for x, part in enumerate((d_0, d_1, d_2, d_3)):
        part[...] = d_ref[:, x * QUARTER : (x + 1) * QUARTER]
    sums_ref[...] = jnp.sum(d_ref[...].astype(F32), axis=1, keepdims=True)
    fetch.wait()
    weight_ref[...] = product(d_ref[...], normed[...], NN).T.astype(BF16)


def attend_backward(info, qkv, grads, grad_row, outs, lse, normed, head, after):
    quarter = [whole(HEAD_DIM, QUARTER)] * QUARTERS
    grad_quarter = [
        pl.BlockSpec(
            (HEAD_DIM, QUARTER), lambda i, info: (grad_row, 0), pipeline_mode=pl.Buffered(1)
        )
    ] * QUARTERS
    rows = 3 * HEAD_DIM
    width = normed.shape[1]
    return pl.pallas_call(
        functools.partial(backward_kernel, len(after)),
        grid_spec=pltpu.PrefetchScalarGridSpec(
            num_scalar_prefetch=1,
            grid=(1,),
            in_specs=[head_spec(head, part) for part in range(3)]
            + grad_quarter
            + quarter
            + [whole(1, SEQ_LEN), ANYWHERE]
            + [ANYWHERE] * len(after),
            out_specs=[whole(rows, QUARTER)] * QUARTERS + [whole(width, rows), whole(rows, 1)],
            scratch_shapes=[pltpu.VMEM((HEAD_DIM, SEQ_LEN), BF16)]
            + [pltpu.VMEM((SEQ_LEN, 128), BF16)] * 4
            + [pltpu.VMEM((BLOCK, BLOCK), BF16)] * 4
            + [pltpu.VMEM((HEAD_DIM, SEQ_LEN), F32)] * 3
            + [
                pltpu.VMEM((rows, SEQ_LEN), BF16),
                pltpu.VMEM(normed.shape, BF16),
                pltpu.SemaphoreType.DMA,
            ],
        ),
        out_shape=[jax.ShapeDtypeStruct((rows, QUARTER), BF16)] * QUARTERS
        + [jax.ShapeDtypeStruct((width, rows), BF16), jax.ShapeDtypeStruct((rows, 1), F32)],
        cost_estimate=pl.CostEstimate(
            flops=32_000_000_000, bytes_accessed=12_000_000, transcendentals=9_000_000
        ),
        name="attend_backward",
    )(info, qkv, qkv, qkv, *grads, *outs, lse, normed, *after)


def normalise(values):
    centred = values - jnp.mean(values, axis=-1, keepdims=True)
    scale = lax.rsqrt(jnp.mean(centred * centred, axis=-1, keepdims=True) + EPSILON)
    return centred * scale, scale


def normalise_back(grad, unit, scale):
    return scale * (
        grad
        - jnp.mean(grad, axis=-1, keepdims=True)
        - unit * jnp.mean(grad * unit, axis=-1, keepdims=True)
    )


def gelu_both(u):
    inner = 0.7978845608028654 * (u + 0.044715 * u * u * u)
    bent = jnp.tanh(inner)
    slope = 0.7978845608028654 * (1.0 + 3 * 0.044715 * u * u)
    return 0.5 * u * (1.0 + bent), 0.5 * (1.0 + bent) + 0.5 * u * (1.0 - bent * bent) * slope


def swap(values, mask):
    return lax.ppermute(values, "tensor", [(i, i ^ mask) for i in range(QUARTERS)])


def pick_first_kernel(info, qkv_ref, gain_ref, shift_ref, head_ref, hidden_ref, out_ref):
    rows = qkv_ref.shape[2]
    heads = qkv_ref.shape[3] // HEAD_DIM
    base = out_ref.shape[1] - 16
    out_ref[...] = jnp.zeros_like(out_ref)
    for h in range(heads):
        for part in range(3):
            at = (h * 3 + part) * HEAD_DIM
            out_ref[0, 0:rows, at : at + HEAD_DIM] = qkv_ref[
                0, part, :, h * HEAD_DIM : (h + 1) * HEAD_DIM
            ]
    few = head_ref.shape[2]
    hidden = hidden_ref[...].astype(F32)
    mine = lax.broadcasted_iota(jnp.int32, hidden.shape, 0) == info[3]
    hidden = jnp.sum(jnp.where(mine, hidden, 0.0), axis=0, keepdims=True)
    wide = lambda item: jnp.pad(
        item.astype(F32), ((0, 0), (0, out_ref.shape[2] - item.shape[1]))
    )
    out_ref[0, base:, :] = jnp.concatenate(
        [
            wide(gain_ref[0]),
            wide(shift_ref[0]),
            wide(head_ref[0]),
            wide(hidden),
            jnp.zeros((7, out_ref.shape[2]), F32),
        ],
        axis=0,
    ).astype(BF16)


def chosen_block(bank):
    rest = bank.shape[1:]
    return pl.BlockSpec((1, *rest), lambda i, info: (info[3],) + (0,) * len(rest))


def pick_first(info, qkv_bank, gain_bank, shift_bank, head_bank, hidden_bank):
    qkv_bank = qkv_bank.transpose(0, 2, 1, 3)
    rows, columns = qkv_bank.shape[2], 3 * qkv_bank.shape[3]
    shape = (1, -(-rows // 16) * 16 + 16, columns)
    return pl.pallas_call(
        pick_first_kernel,
        grid_spec=pltpu.PrefetchScalarGridSpec(
            num_scalar_prefetch=1,
            grid=(1,),
            in_specs=[
                chosen_block(bank) for bank in (qkv_bank, gain_bank, shift_bank, head_bank)
            ]
            + [whole(*hidden_bank.shape)],
            out_specs=pl.BlockSpec(shape, lambda i, info: (0, 0, 0)),
        ),
        out_shape=jax.ShapeDtypeStruct(shape, BF16),
        cost_estimate=SHORT,
        name="pick_first",
    )(info, qkv_bank, gain_bank, shift_bank, head_bank, hidden_bank)


def pick_rest_kernel(info, up_ref, down_ref, out_ref, after_ref, packed_ref):
    first, second = up_ref.shape[2], up_ref.shape[2] + down_ref.shape[2]
    packed_ref[:, :first] = up_ref[0]
    packed_ref[:, first:second] = down_ref[0]
    packed_ref[:, second:] = out_ref[0].astype(F32).T.astype(BF16)


def pick_rest(info, up_bank, down_bank, out_bank, after):
    down_bank = down_bank.transpose(0, 2, 1)
    shape = (up_bank.shape[1], up_bank.shape[2] + down_bank.shape[2] + out_bank.shape[1])
    return pl.pallas_call(
        pick_rest_kernel,
        grid_spec=pltpu.PrefetchScalarGridSpec(
            num_scalar_prefetch=1,
            grid=(1,),
            in_specs=[chosen_block(bank) for bank in (up_bank, down_bank, out_bank)] + [ANYWHERE],
            out_specs=whole(*shape),
        ),
        out_shape=jax.ShapeDtypeStruct(shape, BF16),
        cost_estimate=SHORT,
        name="pick_rest",
    )(info, up_bank, down_bank, out_bank, after)


def assemble_kernel(order, info, far_ref, turned_ref, vec_ref, bias_ref, own_ref, rows_ref, small_ref):
    count = len(order)
    rows = turned_ref.shape[1] // count
    for n, k in enumerate(order):
        owner = jnp.bitwise_xor(info[2], k)
        at = pl.ds(pl.multiple_of(owner * rows, rows), rows)
        rows_ref[at, :] = far_ref[n, :rows]
        small_ref[at, :] = far_ref[n, rows:, 0:128].astype(F32).T[:rows]
    own_ref[...] = far_ref[0, :rows]
    turned_ref[...] = rows_ref[...].astype(F32).T.astype(BF16)
    small = small_ref[...]
    wide = jnp.concatenate([small, jnp.zeros((small.shape[0], 112), F32)], axis=1)
    vec_ref[...] = wide.T[0:16]
    heads = turned_ref.shape[0] // (3 * HEAD_DIM)
    few = heads * HEAD_DIM // count
    column = lambda n: jnp.concatenate(
        [small[p * rows : p * rows + few, n : n + 1] for p in range(count)], axis=0
    )
    q_bias, v_bias = column(6), column(7)
    for h in range(heads):
        at = h * 3 * HEAD_DIM
        bias_ref[at : at + HEAD_DIM, :] = q_bias[h * HEAD_DIM : (h + 1) * HEAD_DIM]
        bias_ref[at + HEAD_DIM : at + 2 * HEAD_DIM, :] = jnp.zeros((HEAD_DIM, 1), F32)
        bias_ref[at + 2 * HEAD_DIM : at + 3 * HEAD_DIM, :] = v_bias[h * HEAD_DIM : (h + 1) * HEAD_DIM]


def gather_qkv(info, part, count, rows, far):
    _, depth, columns = part.shape
    heads = columns // (3 * HEAD_DIM)
    few = heads * HEAD_DIM // count
    if count != 8 or rows % 16 or few % 8:
        parts = lax.all_gather(part[0], "dp", axis=0, tiled=False)
        turned = parts[:, :rows].reshape(count * rows, columns).T
        small = parts[:, depth - 16 :].astype(F32).transpose(1, 0, 2)
        vectors = small[:, :, :rows].reshape(16, count * rows)
        bias = small[6:8, :, :few].reshape(2, heads, HEAD_DIM)
        bias = jnp.stack([bias[0], jnp.zeros_like(bias[0]), bias[1]], axis=1)
        return turned, vectors, bias.reshape(columns, 1), part[0, :rows], part
    joined, order, others = part, [0], []
    for n, mask in enumerate((4, 2, 1)):
        if n:
            joined = jnp.where(far[n - 1][0, 0] > 1e30, jnp.zeros_like(joined), joined)
        other = lax.ppermute(joined, "dp", [(i, i ^ mask) for i in range(count)])
        others.append(other)
        joined = jnp.concatenate([joined, other])
        order = order + [k ^ mask for k in order]
    fixed = lambda *shape: pl.BlockSpec(shape, lambda i, info: (0,) * len(shape))
    outs = [
        ((columns, count * rows), BF16),
        ((16, count * rows), F32),
        ((columns, 1), F32),
        ((rows, columns), BF16),
    ]
    found = pl.pallas_call(
        functools.partial(assemble_kernel, order),
        grid_spec=pltpu.PrefetchScalarGridSpec(
            num_scalar_prefetch=1,
            grid=(1,),
            in_specs=[fixed(*joined.shape)],
            out_specs=[fixed(*shape) for shape, _ in outs],
            scratch_shapes=[
                pltpu.VMEM((count * rows, columns), BF16),
                pltpu.VMEM((count * rows, 16), F32),
            ],
        ),
        out_shape=[jax.ShapeDtypeStruct(shape, kind) for shape, kind in outs],
        cost_estimate=SHORT,
        name="assemble",
    )(info, joined)
    return *found, others[1]


def enter_kernel(spans, w_ref, vec_ref, bias_ref, *refs):
    parts, (qkv_ref, normed_ref) = refs[:-2], refs[-2:]
    row = lax.broadcasted_iota(jnp.int32, (w_ref.shape[0], 1), 0)
    scale = jnp.where(lax.rem(row, 3 * HEAD_DIM) < HEAD_DIM, LOG2E / 8.0, 1.0)
    for part, (first, last) in zip(parts, spans):

        @pl.when((pl.program_id(0) >= first) & (pl.program_id(0) < last))
        def _():
            unit, _ = normalise(part[...].astype(F32))
            rounded = (unit * vec_ref[0:1] + vec_ref[2:3]).astype(BF16)
            normed_ref[...] = rounded
            flat = product(w_ref[...], rounded, NT)
            qkv_ref[...] = ((flat + bias_ref[...]) * scale).astype(BF16)


def enter(parts, turned, vectors, bias):
    block = min(part.shape[0] for part in parts)
    width = parts[0].shape[1]
    columns = turned.shape[0]
    fixed = lambda shape: pl.BlockSpec(shape, lambda i: (0, 0), pipeline_mode=pl.Buffered(1))
    spans, specs, first = [], [], 0
    for part in parts:
        blocks = part.shape[0] // block
        spans.append((first, first + blocks))
        specs.append(
            pl.BlockSpec(
                (block, width), lambda i, first=first, n=blocks: (jnp.clip(i - first, 0, n - 1), 0)
            )
        )
        first += blocks
    return pl.pallas_call(
        functools.partial(enter_kernel, spans),
        grid=(first,),
        in_specs=[fixed(turned.shape), fixed(vectors.shape), fixed(bias.shape)] + specs,
        out_specs=[
            pl.BlockSpec((columns, block), lambda i: (0, i)),
            pl.BlockSpec((block, width), lambda i: (i, 0)),
        ],
        out_shape=[
            jax.ShapeDtypeStruct((columns, first * block), BF16),
            jax.ShapeDtypeStruct((first * block, width), BF16),
        ],
        cost_estimate=SHORT,
        name="enter",
    )(turned, vectors, bias, *parts)


TILE = 256


def middle_kernel(parts, info, tokens_ref, cot_ref, out_ref, vec_ref, up_ref, down_ref, *refs):
    given, refs = refs[:parts], refs[parts:]
    (result_ref, grads_ref, grad_ref, stats_ref), refs = refs[:4], refs[4:]
    back, refs = refs[: 2 * QUARTERS], refs[2 * QUARTERS :]
    mixed, middle, low, low_t, cot_t, activ, grad_u, branch, grad_two, *bufs = refs
    k = pl.program_id(0)
    count, width = tokens_ref.shape
    tiles = count // TILE
    local_width = width // QUARTERS
    spans = [slice(m * TILE, (m + 1) * TILE) for m in range(tiles)]

    @pl.when(k == 0)
    def _():
        for n, part in enumerate(given):
            mixed[n * HEAD_DIM : (n + 1) * HEAD_DIM, :] = part[...]
        for at in spans:
            attended = product(mixed[:, at], out_ref[...], CT)
            value = tokens_ref[at, :].astype(F32) + attended + vec_ref[4:5]
            middle[at, :] = value
            unit, _ = normalise(value)
            rounded = (unit * vec_ref[1:2] + vec_ref[3:4]).astype(BF16)
            low[at, :] = rounded
            low_t[:, at] = rounded.astype(F32).T.astype(BF16)
            cot_t[:, at] = cot_ref[at, :].astype(F32).T.astype(BF16)
            branch[at, :] = jnp.zeros((TILE, width), F32)
            grad_two[at, :] = jnp.zeros((TILE, width), F32)

    bias = vec_ref[pl.ds(8 + jnp.bitwise_xor(k, info[1]), 1), :]

    def first(m, u, g):
        u[...] = product(low[spans[m], :], up_ref[...], NN) + bias
        g[...] = product(cot_ref[spans[m], :], down_ref[...], NN)

    def second(m, u, g):
        value, slope = gelu_both(u[...])
        a = value.astype(BF16)
        gu = (g[...] * slope).astype(BF16)
        activ[spans[m], :] = a
        grad_u[spans[m], :] = gu
        branch[spans[m], :] += product(a, down_ref[...], NT)
        grad_two[spans[m], :] += product(gu, up_ref[...], NT)
        return jnp.sum(gu.astype(F32), axis=0, keepdims=True)

    turns = (bufs[:2], bufs[2:])
    first(0, *turns[0])
    hidden = 0.0
    for m in range(tiles):
        if m + 1 < tiles:
            first(m + 1, *turns[(m + 1) % 2])
        hidden = hidden + second(m, *turns[m % 2])
    stats_ref[pl.ds(4 + k, 1), :] = hidden
    rows = pl.ds(pl.multiple_of(k * width, width), width)
    grads_ref[rows, 0:width] = product(low_t[...], grad_u[...], NN).astype(BF16)
    grads_ref[rows, width : 2 * width] = product(cot_t[...], activ[...], NN).astype(BF16)

    @pl.when(k == pl.num_programs(0) - 1)
    def _():
        sums = [0.0] * 4
        for at in spans:
            value = middle[at, :]
            result_ref[at, :] = (value + branch[at, :] + vec_ref[5:6]).astype(BF16)
            unit, scale = normalise(value)
            grad = grad_two[at, :]
            cot = cot_ref[at, :].astype(F32)
            total = cot + normalise_back(grad * vec_ref[1:2], unit, scale)
            grad_ref[at, :] = total
            e = total.astype(BF16)
            low[at, :] = e
            mixed_grad = product(out_ref[...], e, CT).astype(BF16)
            for n, part in enumerate(back):
                row = n // 2 * local_width + n % 2 * HEAD_DIM
                part[:, at] = mixed_grad[row : row + part.shape[0]]
            for n, item in enumerate((grad * unit, grad, e.astype(F32), cot)):
                sums[n] = sums[n] + jnp.sum(item, axis=0, keepdims=True)
        for n in range(4):
            stats_ref[n : n + 1, :] = sums[n]
        grad_out = product(low[...], mixed[...], CT).astype(BF16)
        for x in range(QUARTERS):
            owner = jnp.bitwise_xor(info[1], x)
            grads_ref[pl.ds(pl.multiple_of(owner * width, width), width), 2 * width :] = grad_out[
                :, x * local_width : (x + 1) * local_width
            ]


def middle_part(info, tokens, cotangent, out_t, vectors, bank, mixed):
    count, width = tokens.shape
    local_width = width // QUARTERS
    outs = [
        ((count, width), BF16),
        ((QUARTERS * width, 2 * width + local_width), BF16),
        ((count, width), F32),
        ((8, width), F32),
    ] + [((HEAD_DIM, count), BF16), ((local_width - HEAD_DIM, count), BF16)] * QUARTERS
    return pl.pallas_call(
        functools.partial(middle_kernel, len(mixed)),
        grid_spec=pltpu.PrefetchScalarGridSpec(
            num_scalar_prefetch=1,
            grid=(QUARTERS,),
            in_specs=[
                whole(count, width),
                whole(count, width),
                whole(width, width),
                whole(16, width),
                pl.BlockSpec((width, width), lambda k, info: (k, 0)),
                pl.BlockSpec((width, width), lambda k, info: (k, 1)),
            ]
            + [whole(HEAD_DIM, count)] * len(mixed),
            out_specs=[whole(*shape) for shape, _ in outs],
            scratch_shapes=[
                pltpu.VMEM((width, count), BF16),
                pltpu.VMEM((count, width), F32),
                pltpu.VMEM((count, width), BF16),
                pltpu.VMEM((width, count), BF16),
                pltpu.VMEM((width, count), BF16),
                pltpu.VMEM((count, width), BF16),
                pltpu.VMEM((count, width), BF16),
                pltpu.VMEM((count, width), F32),
                pltpu.VMEM((count, width), F32),
            ]
            + [pltpu.VMEM((TILE, width), F32)] * 4,
        ),
        out_shape=[jax.ShapeDtypeStruct(shape, kind) for shape, kind in outs],
        compiler_params=pltpu.CompilerParams(vmem_limit_bytes=66_000_000),
        cost_estimate=pl.CostEstimate(
            flops=40_000_000_000, bytes_accessed=40_000_000, transcendentals=3_200_000
        ),
        name="middle",
    )(info, tokens, cotangent, out_t, vectors, bank, bank, *mixed)


def exit_first_kernel(info, *refs):
    deltas, weights, (partial_ref, d_all, w_all) = refs[:-7], refs[-7:-3], refs[-3:]
    heads = len(deltas) // QUARTERS
    span = deltas[0].shape[0]
    for x in range(QUARTERS):
        for h in range(heads):
            at = (x * heads + h) * span
            d_all[at : at + span, :] = deltas[h * QUARTERS + x][...]
        at = x * heads * span
        w_all[:, at : at + heads * span] = weights[x][:, : heads * span]
    partial_ref[...] = product(w_all[...], d_all[...], NN)


def exit_last_kernel(info, *refs):
    deltas, weights, refs = refs[:4], refs[4:8], refs[8:]
    partial_ref, tokens_ref, grad_ref, vec_ref, out_ref, d_all, w_all = refs
    span = deltas[0].shape[0]
    first = weights[0].shape[1] - span
    for x in range(QUARTERS):
        d_all[x * span : (x + 1) * span, :] = deltas[x][...]
        w_all[:, x * span : (x + 1) * span] = weights[x][:, first:]
    for m in range(tokens_ref.shape[0] // TILE):
        at = slice(m * TILE, (m + 1) * TILE)
        grad = (partial_ref[:, at] + product(w_all[...], d_all[:, at], NN)).T
        unit, scale = normalise(tokens_ref[at, :].astype(F32))
        back = normalise_back(grad * vec_ref[0:1], unit, scale)
        out_ref[at, :] = (grad_ref[at, :] + back).astype(BF16)


def stored_blocks(rows, columns):
    return [
        pl.BlockSpec(
            (rows, columns),
            lambda i, info, x=x: (jnp.bitwise_xor(info[1], x), 0),
            pipeline_mode=pl.Buffered(1),
        )
        for x in range(QUARTERS)
    ]


def exit_first(info, deltas, weights):
    columns = weights.shape[1]
    width = weights.shape[0] // QUARTERS
    span, count = deltas[0].shape
    depth = len(deltas) * span
    return pl.pallas_call(
        exit_first_kernel,
        grid_spec=pltpu.PrefetchScalarGridSpec(
            num_scalar_prefetch=1,
            grid=(1,),
            in_specs=[whole(span, count)] * len(deltas) + stored_blocks(width, columns),
            out_specs=whole(width, count),
            scratch_shapes=[pltpu.VMEM((depth, count), BF16), pltpu.VMEM((width, depth), BF16)],
        ),
        out_shape=jax.ShapeDtypeStruct((width, count), F32),
        cost_estimate=SHORT,
        name="exit_first",
    )(info, *deltas, *[weights] * QUARTERS)


def exit_last(info, deltas, weights, partial, tokens, grad, vectors):
    columns = weights.shape[1]
    count, width = tokens.shape
    span = deltas[0].shape[0]
    depth = len(deltas) * span
    return pl.pallas_call(
        exit_last_kernel,
        grid_spec=pltpu.PrefetchScalarGridSpec(
            num_scalar_prefetch=1,
            grid=(1,),
            in_specs=[whole(span, count)] * len(deltas)
            + stored_blocks(width, columns)
            + [whole(width, count), whole(count, width), whole(count, width), whole(8, width)],
            out_specs=whole(count, width),
            scratch_shapes=[pltpu.VMEM((depth, count), BF16), pltpu.VMEM((width, depth), BF16)],
        ),
        out_shape=jax.ShapeDtypeStruct((count, width), BF16),
        cost_estimate=SHORT,
        name="exit_last",
    )(info, *deltas, *[weights] * QUARTERS, partial, tokens, grad, vectors)


def pack_kernel(rows, heads, *refs):
    stats_ref, out_ref = refs[2 * heads], refs[-1]
    weights, sums = refs[:heads], refs[heads : 2 * heads]
    span = weights[0].shape[1]
    count, depth, columns = out_ref.shape
    base = depth - 32
    lined = [jnp.broadcast_to(item[...], (span, 128)).T[0:1] for item in sums]
    lined = jnp.concatenate(pieces(jnp.concatenate(lined, axis=1)), axis=0)
    lined = jnp.concatenate([lined, jnp.zeros((5, columns), F32)], axis=0)
    stats = jnp.concatenate(pieces(stats_ref[...]), axis=0)
    for p in range(count):
        for h in range(heads):
            out_ref[p, 0:rows, h * span : (h + 1) * span] = weights[h][p * rows : (p + 1) * rows]
        part = jnp.concatenate(
            [stats[:, p * rows : (p + 1) * rows], jnp.zeros((24, columns - rows), F32)], axis=1
        )
        out_ref[p, base:, :] = jnp.concatenate([part, lined], axis=0).astype(BF16)


def pack(weights, sums, stats, count, after):
    width, span = weights[0].shape
    rows = width // count
    depth = -(-rows // 16) * 16 + 32
    fixed = lambda shape: pl.BlockSpec(shape, lambda i: (0,) * len(shape))
    shape = (count, depth, len(weights) * span)
    return pl.pallas_call(
        functools.partial(pack_kernel, rows, len(weights)),
        grid=(1,),
        in_specs=[fixed(item.shape) for item in (*weights, *sums, stats)] + [ANYWHERE] * len(after),
        out_specs=fixed(shape),
        out_shape=jax.ShapeDtypeStruct(shape, BF16),
        cost_estimate=SHORT,
        name="pack",
    )(*weights, *sums, stats, *after)


def finish_kernel(rows, received_ref, weight_ref, small_ref, total_ref, stats_ref, sums_ref):
    count, depth, columns = received_ref.shape
    base = depth - 32
    total = received_ref[0].astype(F32)
    for p in range(1, count):
        total = total + received_ref[p].astype(F32)
    grads = total[:rows]
    sums = total[base + 24 : base + 25] + total[base + 25 : base + 26] + total[base + 26 : base + 27]
    stats = total[base : base + 8] + total[base + 8 : base + 16] + total[base + 16 : base + 24]
    weights = weight_ref[...].astype(F32)
    shift = jnp.sum(weights * sums, axis=1, keepdims=True)
    gain = jnp.sum(weights * grads, axis=1, keepdims=True)
    gain = (gain - small_ref[:, 1:2] * shift) / small_ref[:, 0:1]
    sums_ref[...] = sums
    for n in range(columns // HEAD_DIM):
        at = n // 3 * HEAD_DIM
        total_ref[n % 3, :, at : at + HEAD_DIM] = grads[:, n * HEAD_DIM : (n + 1) * HEAD_DIM]
    turned = jnp.concatenate([shift, gain, jnp.zeros((rows, 6), F32)], axis=1).T
    stats_ref[...] = jnp.concatenate([stats[:, :rows], turned], axis=0)


def finish(received, weights, small):
    rows, columns = weights.shape
    fixed = lambda shape: pl.BlockSpec(shape, lambda i: (0,) * len(shape))
    outs = [(3, rows, columns // 3), (16, rows), (1, columns)]
    return pl.pallas_call(
        functools.partial(finish_kernel, rows),
        grid=(1,),
        in_specs=[fixed(item.shape) for item in (received, weights, small)],
        out_specs=[fixed(shape) for shape in outs],
        out_shape=[jax.ShapeDtypeStruct(shape, F32) for shape in outs],
        cost_estimate=SHORT,
        name="finish",
    )(received, weights, small)


def local(
    n_dp,
    tokens,
    cotangent,
    tie_index,
    image_start,
    qkv_bank,
    out_bank,
    up_bank,
    down_bank,
    gain_bank,
    shift_bank,
    head_bias_bank,
    hidden_bias_bank,
):
    own = lax.axis_index("tensor")
    own_dp = lax.axis_index("dp")
    width = tokens.shape[1]
    rows = qkv_bank.shape[1]
    local_width = qkv_bank.shape[3]
    hidden_cols = up_bank.shape[2]
    heads = local_width // HEAD_DIM
    qkv_cols = 3 * local_width
    few = head_bias_bank.shape[2]
    info = jnp.stack([image_start[0], own, own_dp, tie_index[0]]).astype(jnp.int32)

    step = QUARTER // 4
    far = [swap(tokens[n * step : (n + 1) * step], 2) for n in range(4)]
    near = swap(tokens, 1)
    far_near = [swap(part, 1) for part in far]

    packed = pick_first(info, qkv_bank, gain_bank, shift_bank, head_bias_bank, hidden_bias_bank)
    turned, vectors, bias, qkv_part, started = gather_qkv(info, packed, n_dp, rows, far)
    own_small = packed[0, -16:].astype(F32)
    hidden_bias = vectors[8:9]
    hidden_bias = jnp.concatenate(
        [hidden_bias] + [swap(hidden_bias, x) for x in range(1, QUARTERS)]
    )

    bank_part = pick_rest(info, up_bank, down_bank, out_bank, started)
    bank = lax.all_gather(bank_part, ("tensor", "dp"), axis=0, tiled=True)
    qkv_all = lax.all_gather(qkv_part, ("tensor", "dp"), axis=0, tiled=True)
    c_out = 2 * hidden_cols
    out_t = jnp.concatenate(
        [
            lax.dynamic_slice(
                bank, (jnp.bitwise_xor(own, x) * width, c_out), (width, local_width)
            )
            for x in range(QUARTERS)
        ],
        axis=1,
    )

    qkv, normed = enter([tokens, near] + far + far_near, turned, vectors, bias)

    outs, lses, mixed = [], [], [[None] * heads for _ in range(QUARTERS)]
    for head in range(heads):
        after = [mixed[x][head - 2] for x in range(1, QUARTERS)] if head > 1 else []
        *out, lse = attend_forward(info, qkv, head, after)
        outs.append(out)
        lses.append(lse)
        for x in range(QUARTERS):
            mixed[x][head] = swap(out[x], x) if x else out[x]

    rows_two = jnp.concatenate([vectors[0:8], hidden_bias, vectors[8:12]])
    result, grads, grad_middle, stats, *mixed_grads = middle_part(
        info, tokens, cotangent, out_t, rows_two, bank, [part for quarter in mixed for part in quarter]
    )
    shard = lax.psum_scatter(grads, ("tensor", "dp"), scatter_dimension=0, tiled=True).astype(F32)

    deltas, weight_grads, sums = [], [], []
    grads_first = [swap(mixed_grads[2 * x], x) if x else mixed_grads[0] for x in range(QUARTERS)]
    grads_rest = [swap(mixed_grads[2 * x + 1], x) if x else mixed_grads[1] for x in range(QUARTERS)]
    for head in range(heads):
        *parts, weight_grad, summed = attend_backward(
            info,
            qkv,
            grads_rest if head else grads_first,
            max(head - 1, 0),
            outs[head],
            lses[head],
            normed,
            head,
            deltas[head - 2][1:] if head > 1 else [],
        )
        deltas.append([swap(parts[x], x) if x else parts[x] for x in range(QUARTERS)])
        weight_grads.append(weight_grad)
        sums.append(summed)
    early = [part for parts in deltas[:-1] for part in parts]
    partial = exit_first(info, early, qkv_all)

    packed = pack(weight_grads, sums, stats, n_dp, [partial])
    received = lax.all_to_all(
        packed.reshape(-1, qkv_cols), "dp", split_axis=0, concat_axis=0, tiled=True
    ).reshape(packed.shape)
    small = jnp.stack([own_small[0, :rows], own_small[2, :rows]], axis=1)
    qkv_total, stats, sums = finish(received, qkv_part, small)
    stats = stats + swap(stats, 2)
    stats = stats + swap(stats, 1)

    grad_tokens = exit_last(info, deltas[-1], qkv_all, partial, tokens, grad_middle, vectors[0:8])

    by_part = sums.reshape(heads, 3, HEAD_DIM)
    head_sums = jnp.stack([by_part[:, 0].reshape(-1), by_part[:, 2].reshape(-1)])
    head_shard = lax.dynamic_slice_in_dim(head_sums, own_dp * few, few, 1)
    hidden_shard = lax.dynamic_index_in_dim(stats[4:8], own, 0, keepdims=False)
    return (
        result,
        grad_tokens,
        qkv_total.transpose(1, 0, 2),
        shard[:, c_out:].T,
        shard[:, :hidden_cols],
        shard[:, hidden_cols:c_out].T,
        jnp.stack([stats[9], stats[0]]),
        jnp.stack([stats[8], stats[1], stats[2], stats[3]]),
        head_shard,
        hidden_shard,
    )


def solution(mesh):
    placed = (
        P(("dp", "tensor"), None),
        P(("dp", "tensor"), None),
        P(),
        P("dp"),
        P(None, "dp", None, "tensor"),
        P(None, "tensor", "dp"),
        P(None, "dp", "tensor"),
        P(None, "tensor", "dp"),
        P(None, None, "dp"),
        P(None, None, "dp"),
        P(None, None, ("tensor", "dp")),
        P(None, ("tensor", "dp")),
    )
    return jax.shard_map(
        functools.partial(local, mesh.shape["dp"]),
        mesh=mesh,
        in_specs=placed,
        out_specs=(
            P(("dp", "tensor"), None),
            P(("dp", "tensor"), None),
            P("dp", None, "tensor"),
            P("tensor", "dp"),
            P("dp", "tensor"),
            P("tensor", "dp"),
            P(None, "dp"),
            P(None, "dp"),
            P(None, ("tensor", "dp")),
            P(("tensor", "dp")),
        ),
        check_vma=False,
    )
```

```python
import functools
import math

import jax
import jax.numpy as jnp
from jax import lax
from jax.experimental import pallas as pl
from jax.experimental.pallas import tpu as pltpu
from jax.sharding import PartitionSpec as P

HEAD_DIM = 64
SEQ_LEN = 4096
IMG = 256
EPSILON = 1e-05
LOG2E = 1.4426950408889634
BLOCK = 512
BLOCKS = SEQ_LEN // BLOCK
QUARTERS = 4
QUARTER = SEQ_LEN // QUARTERS
PER_QUARTER = QUARTER // BLOCK
PAIRS = BLOCKS * (BLOCKS + 1) // 2
F32 = jnp.float32
BF16 = jnp.bfloat16

NT = (((1,), (1,)), ((), ()))
NN = (((1,), (0,)), ((), ()))
TN = (((0,), (0,)), ((), ()))
CT = (((0,), (1,)), ((), ()))


def product(left, right, dims):
    return lax.dot_general(left, right, dims, preferred_element_type=F32)


def place(block, own):
    quarter = jnp.bitwise_xor(block // PER_QUARTER, own)
    return pl.multiple_of((quarter * PER_QUARTER + block % PER_QUARTER) * BLOCK, BLOCK)


def following(row, col, cross):
    wrap = col + 1 >= row + 1 + jnp.where(cross == row, 1, 0)
    return jnp.where(wrap, row + 1, row), jnp.where(wrap, 0, col + 1)


def crossing(start):
    low, high = start // BLOCK, (start + IMG - 1) // BLOCK
    cross = jnp.where(high > low, low, -1)
    return cross, PAIRS + jnp.where(cross >= 0, 1, 0)


def last_key(pos, start):
    return jnp.where((pos >= start) & (pos < start + IMG), start + (IMG - 1), pos)


def forward_kernel(
    skip, info, q_ref, k_ref, v_ref, *refs
):
    o_0, o_1, o_2, o_3, lse_ref, k_rows, v_ones, s_a, s_b, top_a, top_b, top, total, o_all = refs[skip:]
    start, own = info[0], info[1]
    cross, pairs = crossing(start)

    def prepare(block, carry):
        at = pl.ds(pl.multiple_of(block * BLOCK, BLOCK), BLOCK)
        k_rows[at, :] = k_ref[:, at].astype(F32).T.astype(BF16)
        return carry

    lax.fori_loop(0, BLOCKS, prepare, 0)
    v_ones[0:64, :] = v_ref[...]
    v_ones[64:80, :] = jnp.ones((16, SEQ_LEN), BF16)
    total[...] = jnp.zeros_like(total)

    def score(row, col, dst, dst_top, masked):
        rows = pl.ds(place(jnp.minimum(row, BLOCKS - 1), own), BLOCK)
        s = product(k_rows[pl.ds(place(col, own), BLOCK), :], q_ref[:, rows], NN)
        if masked:
            pos = row * BLOCK + lax.broadcasted_iota(jnp.int32, (1, BLOCK), 1)
            limit = last_key(pos, start) - col * BLOCK
            s = jnp.where(lax.broadcasted_iota(jnp.int32, (BLOCK, BLOCK), 0) <= limit, s, -1e30)
        dst[...] = s
        dst_top[...] = jnp.max(s, axis=0, keepdims=True)

    def step(src, src_top, dst, dst_top, col, next_row, next_col, masked):
        score(next_row, next_col, dst, dst_top, masked)
        old = jnp.where(col == 0, -1e30, top[...])
        new = jnp.maximum(old, src_top[...])
        p = jnp.exp2(src[...] - new).astype(BF16)
        mixed = product(v_ones[:, pl.ds(place(col, own), BLOCK)], p, NN)
        total[...] = total[...] * jnp.exp2(old - new) + mixed
        top[...] = new

    def half(src, src_top, dst, dst_top, row, col):
        next_row, next_col = following(row, col, cross)
        masked = next_col >= next_row

        @pl.when(masked)
        def _():
            step(src, src_top, dst, dst_top, col, next_row, next_col, True)

        @pl.when(jnp.logical_not(masked))
        def _():
            step(src, src_top, dst, dst_top, col, next_row, next_col, False)

        @pl.when(next_col == 0)
        def _():
            at = pl.ds(place(row, own), BLOCK)
            summed = total[64:65]
            o_all[:, at] = (total[0:64] / summed).astype(BF16)
            lse_ref[:, at] = top[...] + jnp.log2(summed)

        return next_row, next_col

    score(0, 0, s_a, top_a, True)

    def both(turn, carry):
        row, col = half(s_a, top_a, s_b, top_b, *carry)
        return half(s_b, top_b, s_a, top_a, row, col)

    row, col = lax.fori_loop(0, pairs // 2, both, (jnp.int32(0), jnp.int32(0)))

    @pl.when(pairs % 2 == 1)
    def _():
        half(s_a, top_a, s_b, top_b, row, col)

    for x, o_ref in enumerate((o_0, o_1, o_2, o_3)):
        o_ref[...] = o_all[:, x * QUARTER : (x + 1) * QUARTER]


def head_spec(head, part):
    return pl.BlockSpec((HEAD_DIM, SEQ_LEN), lambda i, info: (head * 3 + part, 0))


def whole(*shape):
    return pl.BlockSpec(shape, lambda i, info: (0, 0), pipeline_mode=pl.Buffered(1))


ANYWHERE = pl.BlockSpec(memory_space=pl.ANY)
SHORT = pl.CostEstimate(flops=1, bytes_accessed=1, transcendentals=0)


def attend_forward(info, qkv, head, after):
    return pl.pallas_call(
        functools.partial(forward_kernel, len(after)),
        grid_spec=pltpu.PrefetchScalarGridSpec(
            num_scalar_prefetch=1,
            grid=(1,),
            in_specs=[head_spec(head, part) for part in range(3)] + [ANYWHERE] * len(after),
            out_specs=[whole(HEAD_DIM, QUARTER)] * QUARTERS + [whole(1, SEQ_LEN)],
            scratch_shapes=[
                pltpu.VMEM((SEQ_LEN, HEAD_DIM), BF16),
                pltpu.VMEM((80, SEQ_LEN), BF16),
                pltpu.VMEM((BLOCK, BLOCK), F32),
                pltpu.VMEM((BLOCK, BLOCK), F32),
                pltpu.VMEM((1, BLOCK), F32),
                pltpu.VMEM((1, BLOCK), F32),
                pltpu.VMEM((1, BLOCK), F32),
                pltpu.VMEM((80, BLOCK), F32),
                pltpu.VMEM((HEAD_DIM, SEQ_LEN), BF16),
            ],
        ),
        out_shape=[jax.ShapeDtypeStruct((HEAD_DIM, QUARTER), BF16)] * QUARTERS
        + [jax.ShapeDtypeStruct((1, SEQ_LEN), F32)],
        cost_estimate=pl.CostEstimate(
            flops=18_000_000_000, bytes_accessed=2_200_000, transcendentals=9_000_000
        ),
        name="attend_forward",
    )(info, qkv, qkv, qkv, *after)


def pieces(values):
    high = values.astype(BF16).astype(F32)
    rest = values - high
    middle = rest.astype(BF16).astype(F32)
    return [high, middle, (rest - middle).astype(BF16).astype(F32)]


def backward_kernel(
    skip, info, q_ref, k_ref, v_ref, g_0, g_1, g_2, g_3, o_0, o_1, o_2, o_3, lse_ref, normed_ref, *refs
):
    d_0, d_1, d_2, d_3, weight_ref, sums_ref, *refs = refs[skip:]
    g_ref, q_wide, k_wide, v_wide, g_wide, p_a, ds_a, p_b, ds_b, *refs = refs
    dq, dk, dv, d_ref, normed, arrived = refs
    start, own = info[0], info[1]
    cross, pairs = crossing(start)
    fetch = pltpu.make_async_copy(normed_ref, normed, arrived)
    fetch.start()
    ones = [jnp.ones((1, BLOCK), F32)] * 3

    def widen(columns, rows):
        rest = jnp.zeros((HEAD_DIM - 3, BLOCK), F32)
        return jnp.concatenate([columns.astype(F32)] + rows + [rest], axis=0).T.astype(BF16)

    for x, (g_part, o_part) in enumerate(zip((g_0, g_1, g_2, g_3), (o_0, o_1, o_2, o_3))):
        g_ref[:, x * QUARTER : (x + 1) * QUARTER] = g_part[...]
        d_ref[0:HEAD_DIM, x * QUARTER : (x + 1) * QUARTER] = o_part[...]

    def prepare(block, carry):
        at = pl.ds(pl.multiple_of(block * BLOCK, BLOCK), BLOCK)
        grad = g_ref[:, at]
        centre = jnp.sum(
            grad.astype(F32) * d_ref[0:HEAD_DIM, at].astype(F32), axis=0, keepdims=True
        )
        q_wide[at, :] = widen(q_ref[:, at], pieces(-lse_ref[:, at]))
        k_wide[at, :] = widen(k_ref[:, at], ones)
        v_wide[at, :] = widen(v_ref[:, at], ones)
        g_wide[at, :] = widen(grad, pieces(-centre))
        return carry

    lax.fori_loop(0, BLOCKS, prepare, 0)
    dq[...] = jnp.zeros_like(dq)
    dk[...] = jnp.zeros_like(dk)
    dv[...] = jnp.zeros_like(dv)

    def score(row, col, p_dst, ds_dst, masked):
        rows = pl.ds(place(jnp.minimum(row, BLOCKS - 1), own), BLOCK)
        cols = pl.ds(place(col, own), BLOCK)
        s = product(q_wide[rows, :], k_wide[cols, :], NT)
        grad_p = product(g_wide[rows, :], v_wide[cols, :], NT)
        if masked:
            pos = row * BLOCK + lax.broadcasted_iota(jnp.int32, (BLOCK, 1), 0)
            limit = last_key(pos, start) - col * BLOCK
            s = jnp.where(lax.broadcasted_iota(jnp.int32, (BLOCK, BLOCK), 1) <= limit, s, -1e30)
        p = jnp.exp2(s)
        p_dst[...] = p.astype(BF16)
        ds_dst[...] = (p * grad_p).astype(BF16)

    def step(p, ds, p_dst, ds_dst, row, col, next_row, next_col, masked):
        score(next_row, next_col, p_dst, ds_dst, masked)
        rows = pl.ds(place(row, own), BLOCK)
        cols = pl.ds(place(col, own), BLOCK)
        dv[:, cols] += product(g_ref[:, rows], p[...], NN)
        dk[:, cols] += product(q_ref[:, rows], ds[...], NN)
        dq[:, rows] += product(k_ref[:, cols], ds[...], NT)

    def half(p, ds, p_dst, ds_dst, row, col):
        next_row, next_col = following(row, col, cross)
        masked = next_col >= next_row

        @pl.when(masked)
        def _():
            step(p, ds, p_dst, ds_dst, row, col, next_row, next_col, True)

        @pl.when(jnp.logical_not(masked))
        def _():
            step(p, ds, p_dst, ds_dst, row, col, next_row, next_col, False)

        return next_row, next_col

    score(0, 0, p_a, ds_a, True)

    def both(turn, carry):
        row, col = half(p_a, ds_a, p_b, ds_b, *carry)
        return half(p_b, ds_b, p_a, ds_a, row, col)

    row, col = lax.fori_loop(0, pairs // 2, both, (jnp.int32(0), jnp.int32(0)))

    @pl.when(pairs % 2 == 1)
    def _():
        half(p_a, ds_a, p_b, ds_b, row, col)

    d_ref[0:64, :] = (dq[...] * 0.125).astype(BF16)
    d_ref[64:128, :] = (dk[...] * (1.0 / LOG2E)).astype(BF16)
    d_ref[128:192, :] = dv[...].astype(BF16)
    for x, part in enumerate((d_0, d_1, d_2, d_3)):
        part[...] = d_ref[:, x * QUARTER : (x + 1) * QUARTER]
    sums_ref[...] = jnp.sum(d_ref[...].astype(F32), axis=1, keepdims=True)
    fetch.wait()
    weight_ref[...] = product(d_ref[...], normed[...], NN).T.astype(BF16)


def attend_backward(info, qkv, grads, grad_row, outs, lse, normed, head, after):
    quarter = [whole(HEAD_DIM, QUARTER)] * QUARTERS
    grad_quarter = [
        pl.BlockSpec(
            (HEAD_DIM, QUARTER), lambda i, info: (grad_row, 0), pipeline_mode=pl.Buffered(1)
        )
    ] * QUARTERS
    rows = 3 * HEAD_DIM
    width = normed.shape[1]
    return pl.pallas_call(
        functools.partial(backward_kernel, len(after)),
        grid_spec=pltpu.PrefetchScalarGridSpec(
            num_scalar_prefetch=1,
            grid=(1,),
            in_specs=[head_spec(head, part) for part in range(3)]
            + grad_quarter
            + quarter
            + [whole(1, SEQ_LEN), ANYWHERE]
            + [ANYWHERE] * len(after),
            out_specs=[whole(rows, QUARTER)] * QUARTERS + [whole(width, rows), whole(rows, 1)],
            scratch_shapes=[pltpu.VMEM((HEAD_DIM, SEQ_LEN), BF16)]
            + [pltpu.VMEM((SEQ_LEN, 128), BF16)] * 4
            + [pltpu.VMEM((BLOCK, BLOCK), BF16)] * 4
            + [pltpu.VMEM((HEAD_DIM, SEQ_LEN), F32)] * 3
            + [
                pltpu.VMEM((rows, SEQ_LEN), BF16),
                pltpu.VMEM(normed.shape, BF16),
                pltpu.SemaphoreType.DMA,
            ],
        ),
        out_shape=[jax.ShapeDtypeStruct((rows, QUARTER), BF16)] * QUARTERS
        + [jax.ShapeDtypeStruct((width, rows), BF16), jax.ShapeDtypeStruct((rows, 1), F32)],
        cost_estimate=pl.CostEstimate(
            flops=32_000_000_000, bytes_accessed=12_000_000, transcendentals=9_000_000
        ),
        name="attend_backward",
    )(info, qkv, qkv, qkv, *grads, *outs, lse, normed, *after)


def normalise(values):
    centred = values - jnp.mean(values, axis=-1, keepdims=True)
    scale = lax.rsqrt(jnp.mean(centred * centred, axis=-1, keepdims=True) + EPSILON)
    return centred * scale, scale


def normalise_back(grad, unit, scale):
    return scale * (
        grad
        - jnp.mean(grad, axis=-1, keepdims=True)
        - unit * jnp.mean(grad * unit, axis=-1, keepdims=True)
    )


def gelu_both(u):
    square = u * u
    weight = 0.7978845608028654 + (0.7978845608028654 * 0.044715) * square
    share = 0.5 + 0.5 * jnp.tanh(u * weight)
    value = u * share
    rise = 6.0 * weight - 4.0 * 0.7978845608028654
    return value, share + value * (1.0 - share) * rise


def swap(values, mask):
    return lax.ppermute(values, "tensor", [(i, i ^ mask) for i in range(QUARTERS)])


def pick_first_kernel(info, qkv_ref, gain_ref, shift_ref, head_ref, hidden_ref, out_ref):
    rows = qkv_ref.shape[2]
    heads = qkv_ref.shape[3] // HEAD_DIM
    base = out_ref.shape[1] - 16
    out_ref[...] = jnp.zeros_like(out_ref)
    for h in range(heads):
        for part in range(3):
            at = (h * 3 + part) * HEAD_DIM
            out_ref[0, 0:rows, at : at + HEAD_DIM] = qkv_ref[
                0, part, :, h * HEAD_DIM : (h + 1) * HEAD_DIM
            ]
    few = head_ref.shape[2]
    hidden = hidden_ref[...].astype(F32)
    mine = lax.broadcasted_iota(jnp.int32, hidden.shape, 0) == info[3]
    hidden = jnp.sum(jnp.where(mine, hidden, 0.0), axis=0, keepdims=True)
    wide = lambda item: jnp.pad(
        item.astype(F32), ((0, 0), (0, out_ref.shape[2] - item.shape[1]))
    )
    out_ref[0, base:, :] = jnp.concatenate(
        [
            wide(gain_ref[0]),
            wide(shift_ref[0]),
            wide(head_ref[0]),
            wide(hidden),
            jnp.zeros((7, out_ref.shape[2]), F32),
        ],
        axis=0,
    ).astype(BF16)


def chosen_block(bank):
    rest = bank.shape[1:]
    return pl.BlockSpec((1, *rest), lambda i, info: (info[3],) + (0,) * len(rest))


def pick_first(info, qkv_bank, gain_bank, shift_bank, head_bank, hidden_bank):
    qkv_bank = qkv_bank.transpose(0, 2, 1, 3)
    rows, columns = qkv_bank.shape[2], 3 * qkv_bank.shape[3]
    shape = (1, -(-rows // 16) * 16 + 16, columns)
    return pl.pallas_call(
        pick_first_kernel,
        grid_spec=pltpu.PrefetchScalarGridSpec(
            num_scalar_prefetch=1,
            grid=(1,),
            in_specs=[
                chosen_block(bank) for bank in (qkv_bank, gain_bank, shift_bank, head_bank)
            ]
            + [whole(*hidden_bank.shape)],
            out_specs=pl.BlockSpec(shape, lambda i, info: (0, 0, 0)),
        ),
        out_shape=jax.ShapeDtypeStruct(shape, BF16),
        cost_estimate=SHORT,
        name="pick_first",
    )(info, qkv_bank, gain_bank, shift_bank, head_bank, hidden_bank)


def pick_rest_kernel(info, up_ref, down_ref, out_ref, after_ref, packed_ref):
    first, second = up_ref.shape[2], up_ref.shape[2] + down_ref.shape[2]
    packed_ref[:, :first] = up_ref[0]
    packed_ref[:, first:second] = down_ref[0]
    packed_ref[:, second:] = out_ref[0].astype(F32).T.astype(BF16)


def pick_rest(info, up_bank, down_bank, out_bank, after):
    down_bank = down_bank.transpose(0, 2, 1)
    shape = (up_bank.shape[1], up_bank.shape[2] + down_bank.shape[2] + out_bank.shape[1])
    return pl.pallas_call(
        pick_rest_kernel,
        grid_spec=pltpu.PrefetchScalarGridSpec(
            num_scalar_prefetch=1,
            grid=(1,),
            in_specs=[chosen_block(bank) for bank in (up_bank, down_bank, out_bank)] + [ANYWHERE],
            out_specs=whole(*shape),
        ),
        out_shape=jax.ShapeDtypeStruct(shape, BF16),
        cost_estimate=SHORT,
        name="pick_rest",
    )(info, up_bank, down_bank, out_bank, after)


def assemble_kernel(order, info, far_ref, turned_ref, vec_ref, bias_ref, own_ref, rows_ref, small_ref):
    count = len(order)
    rows = turned_ref.shape[1] // count
    for n, k in enumerate(order):
        owner = jnp.bitwise_xor(info[2], k)
        at = pl.ds(pl.multiple_of(owner * rows, rows), rows)
        rows_ref[at, :] = far_ref[n, :rows]
        small_ref[at, :] = far_ref[n, rows:, 0:128].astype(F32).T[:rows]
    own_ref[...] = far_ref[0, :rows]
    turned_ref[...] = rows_ref[...].astype(F32).T.astype(BF16)
    small = small_ref[...]
    wide = jnp.concatenate([small, jnp.zeros((small.shape[0], 112), F32)], axis=1)
    vec_ref[...] = wide.T[0:16]
    heads = turned_ref.shape[0] // (3 * HEAD_DIM)
    few = heads * HEAD_DIM // count
    column = lambda n: jnp.concatenate(
        [small[p * rows : p * rows + few, n : n + 1] for p in range(count)], axis=0
    )
    q_bias, v_bias = column(6), column(7)
    for h in range(heads):
        at = h * 3 * HEAD_DIM
        bias_ref[at : at + HEAD_DIM, :] = q_bias[h * HEAD_DIM : (h + 1) * HEAD_DIM]
        bias_ref[at + HEAD_DIM : at + 2 * HEAD_DIM, :] = jnp.zeros((HEAD_DIM, 1), F32)
        bias_ref[at + 2 * HEAD_DIM : at + 3 * HEAD_DIM, :] = v_bias[h * HEAD_DIM : (h + 1) * HEAD_DIM]


def gather_qkv(info, part, count, rows, far):
    _, depth, columns = part.shape
    heads = columns // (3 * HEAD_DIM)
    few = heads * HEAD_DIM // count
    if count != 8 or rows % 16 or few % 8:
        parts = lax.all_gather(part[0], "dp", axis=0, tiled=False)
        turned = parts[:, :rows].reshape(count * rows, columns).T
        small = parts[:, depth - 16 :].astype(F32).transpose(1, 0, 2)
        vectors = small[:, :, :rows].reshape(16, count * rows)
        bias = small[6:8, :, :few].reshape(2, heads, HEAD_DIM)
        bias = jnp.stack([bias[0], jnp.zeros_like(bias[0]), bias[1]], axis=1)
        return turned, vectors, bias.reshape(columns, 1), part[0, :rows], part, part
    joined, order, others = part, [0], []
    for n, mask in enumerate((4, 2, 1)):
        if n == 1:
            joined = jnp.where(far[0][0, 0] > 1e30, jnp.zeros_like(joined), joined)
        other = lax.ppermute(joined, "dp", [(i, i ^ mask) for i in range(count)])
        others.append(other)
        joined = jnp.concatenate([joined, other])
        order = order + [k ^ mask for k in order]
    fixed = lambda *shape: pl.BlockSpec(shape, lambda i, info: (0,) * len(shape))
    outs = [
        ((columns, count * rows), BF16),
        ((16, count * rows), F32),
        ((columns, 1), F32),
        ((rows, columns), BF16),
    ]
    found = pl.pallas_call(
        functools.partial(assemble_kernel, order),
        grid_spec=pltpu.PrefetchScalarGridSpec(
            num_scalar_prefetch=1,
            grid=(1,),
            in_specs=[fixed(*joined.shape)],
            out_specs=[fixed(*shape) for shape, _ in outs],
            scratch_shapes=[
                pltpu.VMEM((count * rows, columns), BF16),
                pltpu.VMEM((count * rows, 16), F32),
            ],
        ),
        out_shape=[jax.ShapeDtypeStruct(shape, kind) for shape, kind in outs],
        cost_estimate=SHORT,
        name="assemble",
    )(info, joined)
    return *found, others[1], others[2]


def enter_kernel(spans, w_ref, vec_ref, bias_ref, *refs):
    parts, (qkv_ref, normed_ref, hidden_ref, held) = refs[:-4], refs[-4:]
    for part, (first, last) in zip(parts, spans):

        @pl.when((pl.program_id(0) >= first) & (pl.program_id(0) < last))
        def _():
            held[...] = part[...]

    row = lax.broadcasted_iota(jnp.int32, (w_ref.shape[0], 1), 0)
    scale = jnp.where(lax.rem(row, 3 * HEAD_DIM) < HEAD_DIM, LOG2E / 8.0, 1.0)
    unit, _ = normalise(held[...].astype(F32))
    rounded = (unit * vec_ref[0:1] + vec_ref[2:3]).astype(BF16)
    normed_ref[...] = rounded
    flat = product(w_ref[...], rounded, NT)
    qkv_ref[...] = ((flat + bias_ref[...]) * scale).astype(BF16)
    hidden_ref[...] = vec_ref[8:9]


def enter(parts, turned, vectors, bias):
    block = min(part.shape[0] for part in parts)
    width = parts[0].shape[1]
    columns = turned.shape[0]
    fixed = lambda shape: pl.BlockSpec(shape, lambda i: (0, 0), pipeline_mode=pl.Buffered(1))
    spans, specs, first = [], [], 0
    for part in parts:
        blocks = part.shape[0] // block
        spans.append((first, first + blocks))
        specs.append(
            pl.BlockSpec(
                (block, width), lambda i, first=first, n=blocks: (jnp.clip(i - first, 0, n - 1), 0)
            )
        )
        first += blocks
    return pl.pallas_call(
        functools.partial(enter_kernel, spans),
        grid=(first,),
        in_specs=[fixed(turned.shape), fixed(vectors.shape), fixed(bias.shape)] + specs,
        out_specs=[
            pl.BlockSpec((columns, block), lambda i: (0, i)),
            pl.BlockSpec((block, width), lambda i: (i, 0)),
            fixed((1, width)),
        ],
        out_shape=[
            jax.ShapeDtypeStruct((columns, first * block), BF16),
            jax.ShapeDtypeStruct((first * block, width), BF16),
            jax.ShapeDtypeStruct((1, width), F32),
        ],
        scratch_shapes=[pltpu.VMEM((block, width), BF16)],
        cost_estimate=SHORT,
        name="enter",
    )(turned, vectors, bias, *parts)


TILE = 256
TALL = 512


def middle_kernel(parts, info, tokens_ref, cot_ref, out_ref, vec_ref, up_ref, down_ref, *refs):
    given, refs = refs[:parts], refs[parts:]
    (result_ref, grads_ref, grad_ref, stats_ref), refs = refs[:4], refs[4:]
    back, refs = refs[: 2 * QUARTERS], refs[2 * QUARTERS :]
    mixed, middle, low, low_t, cot_t, activ, grad_u, branch, grad_two, *bufs = refs
    k = pl.program_id(0)
    count, width = tokens_ref.shape
    tiles = count // TALL
    local_width = width // QUARTERS
    spans = [slice(m * TALL, (m + 1) * TALL) for m in range(tiles)]

    def tiled(body):
        def at_tile(m, carry):
            return body(pl.ds(pl.multiple_of(m * TALL, TALL), TALL), carry)

        return at_tile

    @pl.when(k == 0)
    def _():
        for n, part in enumerate(given):
            mixed[n * HEAD_DIM : (n + 1) * HEAD_DIM, :] = part[...]
        low_t[width:, :] = jnp.ones((16, count), BF16)

        @tiled
        def begin(at, carry):
            attended = product(mixed[:, at], out_ref[...], CT)
            value = tokens_ref[at, :].astype(F32) + attended + vec_ref[4:5]
            middle[at, :] = value
            unit, _ = normalise(value)
            rounded = (unit * vec_ref[1:2] + vec_ref[3:4]).astype(BF16)
            low[at, :] = rounded
            low_t[0:width, at] = rounded.astype(F32).T.astype(BF16)
            cot_t[:, at] = cot_ref[at, :].astype(F32).T.astype(BF16)
            branch[at, :] = jnp.zeros((TALL, width), F32)
            grad_two[at, :] = jnp.zeros((TALL, width), F32)
            return carry

        lax.fori_loop(0, tiles, begin, 0)

    bias = vec_ref[pl.ds(8 + jnp.bitwise_xor(k, info[1]), 1), :]

    def first(m, u, g):
        u[...] = product(low[spans[m], :], up_ref[...], NN) + bias
        g[...] = product(cot_ref[spans[m], :], down_ref[...], NN)

    def second(m, u, g):
        value, slope = gelu_both(u[...])
        a = value.astype(BF16)
        gu = (g[...] * slope).astype(BF16)
        activ[spans[m], :] = a
        grad_u[spans[m], :] = gu
        branch[spans[m], :] += product(a, down_ref[...], NT)
        grad_two[spans[m], :] += product(gu, up_ref[...], NT)

    turns = (bufs[:2], bufs[2:])
    first(0, *turns[0])
    for m in range(tiles):
        if m + 1 < tiles:
            first(m + 1, *turns[(m + 1) % 2])
        second(m, *turns[m % 2])
    rows = pl.ds(pl.multiple_of(k * width, width), width)
    grad_up = product(low_t[...], grad_u[...], NN)
    grads_ref[rows, 0:width] = grad_up[:width].astype(BF16)
    stats_ref[pl.ds(4 + k, 1), :] = grad_up[width : width + 1]
    grads_ref[rows, width : 2 * width] = product(cot_t[...], activ[...], NN).astype(BF16)

    @pl.when(k == pl.num_programs(0) - 1)
    def _():
        @tiled
        def end(at, sums):
            value = middle[at, :]
            result_ref[at, :] = (value + branch[at, :] + vec_ref[5:6]).astype(BF16)
            unit, scale = normalise(value)
            grad = grad_two[at, :]
            cot = cot_ref[at, :].astype(F32)
            total = cot + normalise_back(grad * vec_ref[1:2], unit, scale)
            grad_ref[at, :] = total
            e = total.astype(BF16)
            low[at, :] = e
            mixed_grad = product(out_ref[...], e, CT).astype(BF16)
            for n, part in enumerate(back):
                row = n // 2 * local_width + n % 2 * HEAD_DIM
                part[:, at] = mixed_grad[row : row + part.shape[0]]
            items = (grad * unit, grad, e.astype(F32), cot)
            return tuple(
                old + jnp.sum(item, axis=0, keepdims=True) for old, item in zip(sums, items)
            )

        sums = lax.fori_loop(0, tiles, end, (jnp.zeros((1, width), F32),) * 4)
        for n in range(4):
            stats_ref[n : n + 1, :] = sums[n]
        grad_out = product(low[...], mixed[...], CT).astype(BF16)
        for x in range(QUARTERS):
            owner = jnp.bitwise_xor(info[1], x)
            grads_ref[pl.ds(pl.multiple_of(owner * width, width), width), 2 * width :] = grad_out[
                :, x * local_width : (x + 1) * local_width
            ]


def middle_part(info, tokens, cotangent, out_t, vectors, bank, mixed):
    count, width = tokens.shape
    local_width = width // QUARTERS
    outs = [
        ((count, width), BF16),
        ((QUARTERS * width, 2 * width + local_width), BF16),
        ((count, width), F32),
        ((8, width), F32),
    ] + [((HEAD_DIM, count), BF16), ((local_width - HEAD_DIM, count), BF16)] * QUARTERS
    return pl.pallas_call(
        functools.partial(middle_kernel, len(mixed)),
        grid_spec=pltpu.PrefetchScalarGridSpec(
            num_scalar_prefetch=1,
            grid=(QUARTERS,),
            in_specs=[
                whole(count, width),
                whole(count, width),
                whole(width, width),
                whole(16, width),
                pl.BlockSpec((width, width), lambda k, info: (k, 0)),
                pl.BlockSpec((width, width), lambda k, info: (k, 1)),
            ]
            + [whole(HEAD_DIM, count)] * len(mixed),
            out_specs=[whole(*shape) for shape, _ in outs],
            scratch_shapes=[
                pltpu.VMEM((width, count), BF16),
                pltpu.VMEM((count, width), F32),
                pltpu.VMEM((count, width), BF16),
                pltpu.VMEM((width + 16, count), BF16),
                pltpu.VMEM((width, count), BF16),
                pltpu.VMEM((count, width), BF16),
                pltpu.VMEM((count, width), BF16),
                pltpu.VMEM((count, width), F32),
                pltpu.VMEM((count, width), F32),
            ]
            + [pltpu.VMEM((TALL, width), F32)] * 4,
        ),
        out_shape=[jax.ShapeDtypeStruct(shape, kind) for shape, kind in outs],
        compiler_params=pltpu.CompilerParams(vmem_limit_bytes=66_000_000),
        cost_estimate=pl.CostEstimate(
            flops=40_000_000_000, bytes_accessed=40_000_000, transcendentals=3_200_000
        ),
        name="middle",
    )(info, tokens, cotangent, out_t, vectors, bank, bank, *mixed)


def exit_first_kernel(info, *refs):
    deltas, weights, (partial_ref, d_all, w_all) = refs[:-7], refs[-7:-3], refs[-3:]
    heads = len(deltas) // QUARTERS
    span = deltas[0].shape[0]

    @pl.when(pl.program_id(0) == 0)
    def _():
        for x in range(QUARTERS):
            at = x * heads * span
            w_all[:, at : at + heads * span] = weights[x][:, : heads * span]

    for x in range(QUARTERS):
        for h in range(heads):
            at = (x * heads + h) * span
            d_all[at : at + span, :] = deltas[h * QUARTERS + x][...]
    partial_ref[...] = product(w_all[...], d_all[...], NN)


def exit_last_kernel(skip, info, *refs):
    deltas, weights, refs = refs[:4], refs[4:8], refs[8:]
    partial_ref, tokens_ref, grad_ref, vec_ref, *refs = refs
    out_ref, d_all, w_all = refs[skip:]
    span = deltas[0].shape[0]
    first = weights[0].shape[1] - span

    @pl.when(pl.program_id(0) == 0)
    def _():
        for x in range(QUARTERS):
            w_all[:, x * span : (x + 1) * span] = weights[x][:, first:]

    for x in range(QUARTERS):
        d_all[x * span : (x + 1) * span, :] = deltas[x][...]
    grad = (partial_ref[...] + product(w_all[...], d_all[...], NN)).T
    unit, scale = normalise(tokens_ref[...].astype(F32))
    back = normalise_back(grad * vec_ref[0:1], unit, scale)
    out_ref[...] = (grad_ref[...] + back).astype(BF16)


def stored_blocks(rows, columns):
    return [
        pl.BlockSpec(
            (rows, columns),
            lambda i, info, x=x: (jnp.bitwise_xor(info[1], x), 0),
            pipeline_mode=pl.Buffered(1),
        )
        for x in range(QUARTERS)
    ]


def lanes(rows):
    return pl.BlockSpec((rows, TILE), lambda i, info: (0, i))


def exit_first(info, deltas, weights):
    columns = weights.shape[1]
    width = weights.shape[0] // QUARTERS
    span, count = deltas[0].shape
    depth = len(deltas) * span
    return pl.pallas_call(
        exit_first_kernel,
        grid_spec=pltpu.PrefetchScalarGridSpec(
            num_scalar_prefetch=1,
            grid=(count // TILE,),
            in_specs=[lanes(span)] * len(deltas) + stored_blocks(width, columns),
            out_specs=lanes(width),
            scratch_shapes=[pltpu.VMEM((depth, TILE), BF16), pltpu.VMEM((width, depth), BF16)],
        ),
        out_shape=jax.ShapeDtypeStruct((width, count), F32),
        cost_estimate=SHORT,
        name="exit_first",
    )(info, *deltas, *[weights] * QUARTERS)


def exit_last(info, deltas, weights, partial, tokens, grad, vectors, after):
    columns = weights.shape[1]
    count, width = tokens.shape
    span = deltas[0].shape[0]
    depth = len(deltas) * span
    tile = pl.BlockSpec((TILE, width), lambda i, info: (i, 0))
    return pl.pallas_call(
        functools.partial(exit_last_kernel, len(after)),
        grid_spec=pltpu.PrefetchScalarGridSpec(
            num_scalar_prefetch=1,
            grid=(count // TILE,),
            in_specs=[lanes(span)] * len(deltas)
            + stored_blocks(width, columns)
            + [lanes(width), tile, tile, whole(*vectors.shape)]
            + [ANYWHERE] * len(after),
            out_specs=tile,
            scratch_shapes=[pltpu.VMEM((depth, TILE), BF16), pltpu.VMEM((width, depth), BF16)],
        ),
        out_shape=jax.ShapeDtypeStruct((count, width), BF16),
        cost_estimate=SHORT,
        name="exit_last",
    )(info, *deltas, *[weights] * QUARTERS, partial, tokens, grad, vectors, *after)


def pack_first_kernel(rows, weights, stats_ref, out_ref):
    span = weights[0].shape[1]
    count, depth, columns = out_ref.shape
    stats = jnp.concatenate(pieces(stats_ref[...]), axis=0)
    for p in range(count):
        for h, weight in enumerate(weights):
            out_ref[p, 0:rows, h * span : (h + 1) * span] = weight[p * rows : (p + 1) * rows]
        part = jnp.concatenate(
            [stats[:, p * rows : (p + 1) * rows], jnp.zeros((24, columns - rows), F32)], axis=1
        )
        part = jnp.concatenate([part, jnp.zeros((8, columns), F32)], axis=0)
        out_ref[p, depth - 32 :, :] = part.astype(BF16)


def pack_last_kernel(rows, weight, sums, out_ref):
    span = weight.shape[1]
    count, depth, columns = out_ref.shape
    lined = [jnp.broadcast_to(item[...], (span, 128)).T[0:1] for item in sums]
    lined = [piece for item in lined for piece in pieces(item)]
    lined = jnp.concatenate(lined + [jnp.zeros((16 - len(lined), span), F32)], axis=0)
    lined = jnp.concatenate([lined, jnp.zeros((16, columns - span), F32)], axis=1).astype(BF16)
    out_ref[...] = jnp.zeros_like(out_ref)
    for p in range(count):
        out_ref[p, 0:rows, 0:span] = weight[p * rows : (p + 1) * rows]
        out_ref[p, depth - 16 :, :] = lined


def exchange(kernel, count, items, below, columns, after, name):
    width = items[0].shape[0]
    rows = width // count
    fixed = lambda shape: pl.BlockSpec(shape, lambda i: (0,) * len(shape))
    shape = (count, -(-rows // 16) * 16 + below, columns)

    def body(*refs):
        kernel(rows, refs[: len(items)], refs[-1])

    packed = pl.pallas_call(
        body,
        grid=(1,),
        in_specs=[fixed(item.shape) for item in items] + [ANYWHERE] * len(after),
        out_specs=fixed(shape),
        out_shape=jax.ShapeDtypeStruct(shape, BF16),
        cost_estimate=SHORT,
        name=name,
    )(*items, *after)
    received = lax.all_to_all(
        packed.reshape(-1, columns), "dp", split_axis=0, concat_axis=0, tiled=True
    )
    return received.reshape(shape)


def exchange_first(weights, stats, count):
    kernel = lambda rows, refs, out: pack_first_kernel(rows, refs[:-1], refs[-1], out)
    columns = sum(weight.shape[1] for weight in weights)
    return exchange(kernel, count, [*weights, stats], 32, columns, [], "pack_first")


def exchange_last(weight, sums, count, after):
    kernel = lambda rows, refs, out: pack_last_kernel(rows, refs[0], refs[1:], out)
    return exchange(kernel, count, [weight, *sums], 16, 256, after, "pack_last")


def finish_kernel(heads, early_ref, late_ref, weight_ref, small_ref, total_ref, stats_ref, sums_ref):
    rows, columns = weight_ref.shape
    span = columns // heads
    early, late = early_ref[0].astype(F32), late_ref[0].astype(F32)
    for p in range(1, early_ref.shape[0]):
        early = early + early_ref[p].astype(F32)
        late = late + late_ref[p].astype(F32)
    grads = jnp.concatenate([early[:rows], late[:rows, :span]], axis=1)
    base = early.shape[0] - 32
    stats = early[base : base + 8] + early[base + 8 : base + 16] + early[base + 16 : base + 24]
    lined = late[late.shape[0] - 16 :, :span]
    sums = jnp.concatenate(
        [lined[3 * h : 3 * h + 1] + lined[3 * h + 1 : 3 * h + 2] + lined[3 * h + 2 : 3 * h + 3]
         for h in range(heads)],
        axis=1,
    )
    weights = weight_ref[...].astype(F32)
    shift = jnp.sum(weights * sums, axis=1, keepdims=True)
    gain = jnp.sum(weights * grads, axis=1, keepdims=True)
    gain = (gain - small_ref[:, 1:2] * shift) / small_ref[:, 0:1]
    sums_ref[...] = sums
    for n in range(columns // HEAD_DIM):
        at = n // 3 * HEAD_DIM
        total_ref[n % 3, :, at : at + HEAD_DIM] = grads[:, n * HEAD_DIM : (n + 1) * HEAD_DIM]
    turned = jnp.concatenate([shift, gain, jnp.zeros((rows, 6), F32)], axis=1).T
    stats_ref[...] = jnp.concatenate([stats[:, :rows], turned], axis=0)


def finish(early, late, weights, small):
    rows, columns = weights.shape
    heads = columns // (3 * HEAD_DIM)
    fixed = lambda shape: pl.BlockSpec(shape, lambda i: (0,) * len(shape))
    outs = [(3, rows, columns // 3), (16, rows), (1, columns)]
    return pl.pallas_call(
        functools.partial(finish_kernel, heads),
        grid=(1,),
        in_specs=[fixed(item.shape) for item in (early, late, weights, small)],
        out_specs=[fixed(shape) for shape in outs],
        out_shape=[jax.ShapeDtypeStruct(shape, F32) for shape in outs],
        cost_estimate=SHORT,
        name="finish",
    )(early, late, weights, small)


def unpack_kernel(shard_ref, up_ref, down_ref, out_ref):
    first, second = up_ref.shape[1], up_ref.shape[1] + down_ref.shape[1]
    up_ref[...] = shard_ref[:, :first].astype(F32)
    down_ref[...] = shard_ref[:, first:second].astype(F32)
    out_ref[...] = shard_ref[:, second:].astype(F32).T


def unpack(shard, first, second):
    rows, columns = shard.shape
    outs = [(rows, first), (rows, second - first), (columns - second, rows)]
    fixed = lambda shape: pl.BlockSpec(shape, lambda i: (0, 0))
    return pl.pallas_call(
        unpack_kernel,
        grid=(1,),
        in_specs=[fixed(shard.shape)],
        out_specs=[fixed(shape) for shape in outs],
        out_shape=[jax.ShapeDtypeStruct(shape, F32) for shape in outs],
        cost_estimate=SHORT,
        name="unpack",
    )(shard)


def local(
    n_dp,
    tokens,
    cotangent,
    tie_index,
    image_start,
    qkv_bank,
    out_bank,
    up_bank,
    down_bank,
    gain_bank,
    shift_bank,
    head_bias_bank,
    hidden_bias_bank,
):
    own = lax.axis_index("tensor")
    own_dp = lax.axis_index("dp")
    width = tokens.shape[1]
    rows = qkv_bank.shape[1]
    local_width = qkv_bank.shape[3]
    hidden_cols = up_bank.shape[2]
    heads = local_width // HEAD_DIM
    qkv_cols = 3 * local_width
    few = head_bias_bank.shape[2]
    info = jnp.stack([image_start[0], own, own_dp, tie_index[0]]).astype(jnp.int32)

    step = QUARTER // 2
    far = [swap(tokens[n * step : (n + 1) * step], 2) for n in range(2)]
    near = swap(tokens, 1)

    packed = pick_first(info, qkv_bank, gain_bank, shift_bank, head_bias_bank, hidden_bias_bank)
    turned, vectors, bias, qkv_part, started, ended = gather_qkv(info, packed, n_dp, rows, far)
    held = jnp.where(ended[0, 0, 0] > 1e30, jnp.zeros_like(far[1]), far[1])
    far_near = [swap(far[0], 1), swap(held, 1)]
    own_small = packed[0, -16:].astype(F32)
    bank_part = pick_rest(info, up_bank, down_bank, out_bank, started)
    bank = lax.all_gather(bank_part, ("tensor", "dp"), axis=0, tiled=True)
    qkv_all = lax.all_gather(qkv_part, ("tensor", "dp"), axis=0, tiled=True)
    c_out = 2 * hidden_cols
    out_t = jnp.concatenate(
        [
            lax.dynamic_slice(
                bank, (jnp.bitwise_xor(own, x) * width, c_out), (width, local_width)
            )
            for x in range(QUARTERS)
        ],
        axis=1,
    )

    qkv, normed, hidden_bias = enter([tokens, near] + far + far_near, turned, vectors, bias)
    hidden_bias = jnp.concatenate(
        [hidden_bias] + [swap(hidden_bias, x) for x in range(1, QUARTERS)]
    )

    outs, lses, mixed = [], [], [[None] * heads for _ in range(QUARTERS)]
    for head in range(heads):
        after = [mixed[x][head - 2] for x in range(1, QUARTERS)] if head > 1 else []
        *out, lse = attend_forward(info, qkv, head, after)
        outs.append(out)
        lses.append(lse)
        for x in range(QUARTERS):
            mixed[x][head] = swap(out[x], x) if x else out[x]

    rows_two = jnp.concatenate([vectors[0:8], hidden_bias, vectors[8:12]])
    result, grads, grad_middle, stats, *mixed_grads = middle_part(
        info, tokens, cotangent, out_t, rows_two, bank, [part for quarter in mixed for part in quarter]
    )
    shard = lax.psum_scatter(grads, ("tensor", "dp"), scatter_dimension=0, tiled=True)
    up_shard, down_shard, out_shard = unpack(shard, hidden_cols, c_out)

    deltas, weight_grads, sums = [], [], []
    grads_first = [swap(mixed_grads[2 * x], x) if x else mixed_grads[0] for x in range(QUARTERS)]
    grads_rest = [swap(mixed_grads[2 * x + 1], x) if x else mixed_grads[1] for x in range(QUARTERS)]
    for head in range(heads):
        *parts, weight_grad, summed = attend_backward(
            info,
            qkv,
            grads_rest if head else grads_first,
            max(head - 1, 0),
            outs[head],
            lses[head],
            normed,
            head,
            deltas[head - 2][1:] if head > 1 else [],
        )
        deltas.append([swap(parts[x], x) if x else parts[x] for x in range(QUARTERS)])
        weight_grads.append(weight_grad)
        sums.append(summed)
        if head == heads - 2:
            early_sums = exchange_first(weight_grads, stats, n_dp)
    early = [part for parts in deltas[:-1] for part in parts]

    late_sums = exchange_last(weight_grads[-1], sums, n_dp, [*deltas[-2][1:], early_sums])
    small = jnp.stack([own_small[0, :rows], own_small[2, :rows]], axis=1)
    qkv_total, stats, sums = finish(early_sums, late_sums, qkv_part, small)
    stats = stats + swap(stats, 2)
    stats = stats + swap(stats, 1)

    by_part = sums.reshape(heads, 3, HEAD_DIM)
    head_sums = jnp.stack([by_part[:, 0].reshape(-1), by_part[:, 2].reshape(-1)])
    head_shard = lax.dynamic_slice_in_dim(head_sums, own_dp * few, few, 1)
    hidden_shard = lax.dynamic_index_in_dim(stats[4:8], own, 0, keepdims=False)
    gain_grads = jnp.stack([stats[9], stats[0]])
    shift_grads = jnp.stack([stats[8], stats[1], stats[2], stats[3]])

    partial = exit_first(info, early, qkv_all)
    grad_tokens = exit_last(
        info, deltas[-1], qkv_all, partial, tokens, grad_middle, vectors,
        [gain_grads, shift_grads, head_shard, hidden_shard],
    )

    return (
        result,
        grad_tokens,
        qkv_total.transpose(1, 0, 2),
        out_shard,
        up_shard,
        down_shard.T,
        gain_grads,
        shift_grads,
        head_shard,
        hidden_shard,
    )


def solution(mesh):
    placed = (
        P(("dp", "tensor"), None),
        P(("dp", "tensor"), None),
        P(),
        P("dp"),
        P(None, "dp", None, "tensor"),
        P(None, "tensor", "dp"),
        P(None, "dp", "tensor"),
        P(None, "tensor", "dp"),
        P(None, None, "dp"),
        P(None, None, "dp"),
        P(None, None, ("tensor", "dp")),
        P(None, ("tensor", "dp")),
    )
    return jax.shard_map(
        functools.partial(local, mesh.shape["dp"]),
        mesh=mesh,
        in_specs=placed,
        out_specs=(
            P(("dp", "tensor"), None),
            P(("dp", "tensor"), None),
            P("dp", None, "tensor"),
            P("tensor", "dp"),
            P("dp", "tensor"),
            P("tensor", "dp"),
            P(None, "dp"),
            P(None, "dp"),
            P(None, ("tensor", "dp")),
            P(("tensor", "dp")),
        ),
        check_vma=False,
    )
```

```python
import functools
import math

import jax
import jax.numpy as jnp
from jax import lax
from jax.experimental import pallas as pl
from jax.experimental.pallas import tpu as pltpu
from jax.sharding import PartitionSpec as P

HEAD_DIM = 64
SEQ_LEN = 4096
IMG = 256
EPSILON = 1e-05
LOG2E = 1.4426950408889634
BLOCK = 512
BLOCKS = SEQ_LEN // BLOCK
QUARTERS = 4
QUARTER = SEQ_LEN // QUARTERS
PER_QUARTER = QUARTER // BLOCK
PAIRS = BLOCKS * (BLOCKS + 1) // 2
F32 = jnp.float32
BF16 = jnp.bfloat16

NT = (((1,), (1,)), ((), ()))
NN = (((1,), (0,)), ((), ()))
TN = (((0,), (0,)), ((), ()))
CT = (((0,), (1,)), ((), ()))


def product(left, right, dims):
    return lax.dot_general(left, right, dims, preferred_element_type=F32)


def place(block, own):
    quarter = jnp.bitwise_xor(block // PER_QUARTER, own)
    return pl.multiple_of((quarter * PER_QUARTER + block % PER_QUARTER) * BLOCK, BLOCK)


def following(row, col, cross):
    wrap = col + 1 >= row + 1 + jnp.where(cross == row, 1, 0)
    return jnp.where(wrap, row + 1, row), jnp.where(wrap, 0, col + 1)


def crossing(start):
    low, high = start // BLOCK, (start + IMG - 1) // BLOCK
    cross = jnp.where(high > low, low, -1)
    return cross, PAIRS + jnp.where(cross >= 0, 1, 0)


def last_key(pos, start):
    return jnp.where((pos >= start) & (pos < start + IMG), start + (IMG - 1), pos)


def forward_kernel(
    skip, info, q_ref, k_ref, v_ref, *refs
):
    o_0, o_1, o_2, o_3, lse_ref, k_rows, v_ones, s_a, s_b, top_a, top_b, top, total, o_all = refs[skip:]
    start, own = info[0], info[1]
    cross, pairs = crossing(start)

    def prepare(block, carry):
        at = pl.ds(pl.multiple_of(block * BLOCK, BLOCK), BLOCK)
        k_rows[at, :] = k_ref[:, at].T
        return carry

    lax.fori_loop(0, BLOCKS, prepare, 0)
    v_ones[0:64, :] = v_ref[...]
    v_ones[64:80, :] = jnp.ones((16, SEQ_LEN), BF16)
    total[...] = jnp.zeros_like(total)

    def score(row, col, dst, dst_top, masked):
        rows = pl.ds(place(jnp.minimum(row, BLOCKS - 1), own), BLOCK)
        s = product(k_rows[pl.ds(place(col, own), BLOCK), :], q_ref[:, rows], NN)
        if masked:
            pos = row * BLOCK + lax.broadcasted_iota(jnp.int32, (1, BLOCK), 1)
            limit = last_key(pos, start) - col * BLOCK
            s = jnp.where(lax.broadcasted_iota(jnp.int32, (BLOCK, BLOCK), 0) <= limit, s, -1e30)
        dst[...] = s
        dst_top[...] = jnp.max(s, axis=0, keepdims=True)

    def step(src, src_top, dst, dst_top, col, next_row, next_col, masked):
        score(next_row, next_col, dst, dst_top, masked)
        old = jnp.where(col == 0, -1e30, top[...])
        new = jnp.maximum(old, src_top[...])
        p = jnp.exp2(src[...] - new).astype(BF16)
        mixed = product(v_ones[:, pl.ds(place(col, own), BLOCK)], p, NN)
        total[...] = total[...] * jnp.exp2(old - new) + mixed
        top[...] = new

    def half(src, src_top, dst, dst_top, row, col, live):
        next_row, next_col = following(row, col, cross)
        masked = next_col >= next_row

        @pl.when(live & masked)
        def _():
            step(src, src_top, dst, dst_top, col, next_row, next_col, True)

        @pl.when(live & jnp.logical_not(masked))
        def _():
            step(src, src_top, dst, dst_top, col, next_row, next_col, False)

        @pl.when(live & (next_col == 0))
        def _():
            at = pl.ds(place(row, own), BLOCK)
            summed = total[64:65]
            o_all[:, at] = (total[0:64] / summed).astype(BF16)
            lse_ref[:, at] = top[...] + jnp.log2(summed)

        return next_row, next_col

    score(0, 0, s_a, top_a, True)

    def both(turn, carry):
        row, col = half(s_a, top_a, s_b, top_b, *carry, turn >= 0)
        return half(s_b, top_b, s_a, top_a, row, col, 2 * turn + 1 < pairs)

    lax.fori_loop(0, (pairs + 1) // 2, both, (jnp.int32(0), jnp.int32(0)))

    for x, o_ref in enumerate((o_0, o_1, o_2, o_3)):
        o_ref[...] = o_all[:, x * QUARTER : (x + 1) * QUARTER]


def gate(items, after):
    def kernel(*refs):
        pass

    return pl.pallas_call(
        kernel,
        in_specs=[ANYWHERE] * (len(items) + len(after)),
        out_specs=[ANYWHERE] * len(items),
        out_shape=[jax.ShapeDtypeStruct(item.shape, item.dtype) for item in items],
        input_output_aliases={n: n for n in range(len(items))},
        cost_estimate=SHORT,
        name="gate",
    )(*items, *after)


def head_spec(head, part):
    return pl.BlockSpec((HEAD_DIM, SEQ_LEN), lambda i, info: (head * 3 + part, 0))


def whole(*shape):
    return pl.BlockSpec(shape, lambda i, info: (0, 0), pipeline_mode=pl.Buffered(1))


ANYWHERE = pl.BlockSpec(memory_space=pl.ANY)
SHORT = pl.CostEstimate(flops=1, bytes_accessed=1, transcendentals=0)


def attend_forward(info, qkv, head, after):
    return pl.pallas_call(
        functools.partial(forward_kernel, len(after)),
        grid_spec=pltpu.PrefetchScalarGridSpec(
            num_scalar_prefetch=1,
            grid=(1,),
            in_specs=[head_spec(head, part) for part in range(3)] + [ANYWHERE] * len(after),
            out_specs=[whole(HEAD_DIM, QUARTER)] * QUARTERS + [whole(1, SEQ_LEN)],
            scratch_shapes=[
                pltpu.VMEM((SEQ_LEN, HEAD_DIM), BF16),
                pltpu.VMEM((80, SEQ_LEN), BF16),
                pltpu.VMEM((BLOCK, BLOCK), F32),
                pltpu.VMEM((BLOCK, BLOCK), F32),
                pltpu.VMEM((1, BLOCK), F32),
                pltpu.VMEM((1, BLOCK), F32),
                pltpu.VMEM((1, BLOCK), F32),
                pltpu.VMEM((80, BLOCK), F32),
                pltpu.VMEM((HEAD_DIM, SEQ_LEN), BF16),
            ],
        ),
        out_shape=[jax.ShapeDtypeStruct((HEAD_DIM, QUARTER), BF16)] * QUARTERS
        + [jax.ShapeDtypeStruct((1, SEQ_LEN), F32)],
        cost_estimate=pl.CostEstimate(
            flops=18_000_000_000, bytes_accessed=2_200_000, transcendentals=9_000_000
        ),
        name="attend_forward",
    )(info, qkv, qkv, qkv, *after)


def pieces(values):
    high = values.astype(BF16).astype(F32)
    rest = values - high
    middle = rest.astype(BF16).astype(F32)
    return [high, middle, (rest - middle).astype(BF16).astype(F32)]


def backward_kernel(
    skip, info, q_ref, k_ref, v_ref, g_0, g_1, g_2, g_3, o_0, o_1, o_2, o_3, lse_ref, normed_ref, *refs
):
    d_0, d_1, d_2, d_3, weight_ref, sums_ref, *refs = refs[skip:]
    g_ref, q_wide, k_wide, v_wide, g_wide, p_a, ds_a, p_b, ds_b, *refs = refs
    dq, dk, dv, d_ref, normed, arrived = refs
    start, own = info[0], info[1]
    cross, pairs = crossing(start)
    fetch = pltpu.make_async_copy(normed_ref, normed, arrived)
    fetch.start()
    ones = [jnp.ones((1, BLOCK), F32)] * 3

    def widen(columns, rows):
        rest = jnp.concatenate(rows + [jnp.zeros((HEAD_DIM - 3, BLOCK), F32)], axis=0)
        return jnp.concatenate([columns, rest.astype(BF16)], axis=0).T

    for x, (g_part, o_part) in enumerate(zip((g_0, g_1, g_2, g_3), (o_0, o_1, o_2, o_3))):
        g_ref[:, x * QUARTER : (x + 1) * QUARTER] = g_part[...]
        d_ref[0:HEAD_DIM, x * QUARTER : (x + 1) * QUARTER] = o_part[...]

    def prepare(block, carry):
        at = pl.ds(pl.multiple_of(block * BLOCK, BLOCK), BLOCK)
        grad = g_ref[:, at]
        centre = jnp.sum(
            grad.astype(F32) * d_ref[0:HEAD_DIM, at].astype(F32), axis=0, keepdims=True
        )
        q_wide[at, :] = widen(q_ref[:, at], pieces(-lse_ref[:, at]))
        k_wide[at, :] = widen(k_ref[:, at], ones)
        v_wide[at, :] = widen(v_ref[:, at], ones)
        g_wide[at, :] = widen(grad, pieces(-centre))
        return carry

    lax.fori_loop(0, BLOCKS, prepare, 0)
    dq[...] = jnp.zeros_like(dq)
    dk[...] = jnp.zeros_like(dk)
    dv[...] = jnp.zeros_like(dv)

    def score(row, col, p_dst, ds_dst, masked):
        rows = pl.ds(place(jnp.minimum(row, BLOCKS - 1), own), BLOCK)
        cols = pl.ds(place(col, own), BLOCK)
        s = product(q_wide[rows, :], k_wide[cols, :], NT)
        grad_p = product(g_wide[rows, :], v_wide[cols, :], NT)
        if masked:
            pos = row * BLOCK + lax.broadcasted_iota(jnp.int32, (BLOCK, 1), 0)
            limit = last_key(pos, start) - col * BLOCK
            s = jnp.where(lax.broadcasted_iota(jnp.int32, (BLOCK, BLOCK), 1) <= limit, s, -1e30)
        p = jnp.exp2(s)
        p_dst[...] = p.astype(BF16)
        ds_dst[...] = (p * grad_p).astype(BF16)

    def step(p, ds, p_dst, ds_dst, row, col, next_row, next_col, masked):
        score(next_row, next_col, p_dst, ds_dst, masked)
        rows = pl.ds(place(row, own), BLOCK)
        cols = pl.ds(place(col, own), BLOCK)
        dv[:, cols] += product(g_ref[:, rows], p[...], NN)
        dk[:, cols] += product(q_ref[:, rows], ds[...], NN)
        dq[:, rows] += product(k_ref[:, cols], ds[...], NT)

    def half(p, ds, p_dst, ds_dst, row, col, live):
        next_row, next_col = following(row, col, cross)
        masked = next_col >= next_row

        @pl.when(live & masked)
        def _():
            step(p, ds, p_dst, ds_dst, row, col, next_row, next_col, True)

        @pl.when(live & jnp.logical_not(masked))
        def _():
            step(p, ds, p_dst, ds_dst, row, col, next_row, next_col, False)

        return next_row, next_col

    score(0, 0, p_a, ds_a, True)

    def both(turn, carry):
        row, col = half(p_a, ds_a, p_b, ds_b, *carry, turn >= 0)
        return half(p_b, ds_b, p_a, ds_a, row, col, 2 * turn + 1 < pairs)

    lax.fori_loop(0, (pairs + 1) // 2, both, (jnp.int32(0), jnp.int32(0)))

    d_ref[0:64, :] = (dq[...] * 0.125).astype(BF16)
    d_ref[64:128, :] = (dk[...] * (1.0 / LOG2E)).astype(BF16)
    d_ref[128:192, :] = dv[...].astype(BF16)
    for x, part in enumerate((d_0, d_1, d_2, d_3)):
        part[...] = d_ref[:, x * QUARTER : (x + 1) * QUARTER]
    sums_ref[...] = jnp.sum(d_ref[...].astype(F32), axis=1, keepdims=True)
    fetch.wait()
    weight_ref[...] = product(d_ref[...], normed[...], NN).T.astype(BF16)


def attend_backward(info, qkv, grads, grad_row, outs, lse, normed, head, after):
    quarter = [whole(HEAD_DIM, QUARTER)] * QUARTERS
    grad_quarter = [
        pl.BlockSpec(
            (HEAD_DIM, QUARTER), lambda i, info: (grad_row, 0), pipeline_mode=pl.Buffered(1)
        )
    ] * QUARTERS
    rows = 3 * HEAD_DIM
    width = normed.shape[1]
    return pl.pallas_call(
        functools.partial(backward_kernel, len(after)),
        grid_spec=pltpu.PrefetchScalarGridSpec(
            num_scalar_prefetch=1,
            grid=(1,),
            in_specs=[head_spec(head, part) for part in range(3)]
            + grad_quarter
            + quarter
            + [whole(1, SEQ_LEN), ANYWHERE]
            + [ANYWHERE] * len(after),
            out_specs=[whole(rows, QUARTER)] * QUARTERS + [whole(width, rows), whole(rows, 1)],
            scratch_shapes=[pltpu.VMEM((HEAD_DIM, SEQ_LEN), BF16)]
            + [pltpu.VMEM((SEQ_LEN, 128), BF16)] * 4
            + [pltpu.VMEM((BLOCK, BLOCK), BF16)] * 4
            + [pltpu.VMEM((HEAD_DIM, SEQ_LEN), F32)] * 3
            + [
                pltpu.VMEM((rows, SEQ_LEN), BF16),
                pltpu.VMEM(normed.shape, BF16),
                pltpu.SemaphoreType.DMA,
            ],
        ),
        out_shape=[jax.ShapeDtypeStruct((rows, QUARTER), BF16)] * QUARTERS
        + [jax.ShapeDtypeStruct((width, rows), BF16), jax.ShapeDtypeStruct((rows, 1), F32)],
        cost_estimate=pl.CostEstimate(
            flops=32_000_000_000, bytes_accessed=12_000_000, transcendentals=9_000_000
        ),
        name="attend_backward",
    )(info, qkv, qkv, qkv, *grads, *outs, lse, normed, *after)


def normalise(values):
    centred = values - jnp.mean(values, axis=-1, keepdims=True)
    scale = lax.rsqrt(jnp.mean(centred * centred, axis=-1, keepdims=True) + EPSILON)
    return centred * scale, scale


def normalise_back(grad, unit, scale):
    return scale * (
        grad
        - jnp.mean(grad, axis=-1, keepdims=True)
        - unit * jnp.mean(grad * unit, axis=-1, keepdims=True)
    )


def gelu_both(u):
    square = u * u
    weight = 0.7978845608028654 + (0.7978845608028654 * 0.044715) * square
    share = 0.5 + 0.5 * jnp.tanh(u * weight)
    value = u * share
    rise = 6.0 * weight - 4.0 * 0.7978845608028654
    return value, share + value * (1.0 - share) * rise


def swap(values, mask):
    return lax.ppermute(values, "tensor", [(i, i ^ mask) for i in range(QUARTERS)])


def pick_first_kernel(info, qkv_ref, gain_ref, shift_ref, head_ref, hidden_ref, out_ref):
    rows = qkv_ref.shape[2]
    heads = qkv_ref.shape[3] // HEAD_DIM
    base = out_ref.shape[1] - 16
    out_ref[...] = jnp.zeros_like(out_ref)
    for h in range(heads):
        for part in range(3):
            at = (h * 3 + part) * HEAD_DIM
            out_ref[0, 0:rows, at : at + HEAD_DIM] = qkv_ref[
                0, part, :, h * HEAD_DIM : (h + 1) * HEAD_DIM
            ]
    few = head_ref.shape[2]
    hidden = hidden_ref[...].astype(F32)
    mine = lax.broadcasted_iota(jnp.int32, hidden.shape, 0) == info[3]
    hidden = jnp.sum(jnp.where(mine, hidden, 0.0), axis=0, keepdims=True)
    wide = lambda item: jnp.pad(
        item.astype(F32), ((0, 0), (0, out_ref.shape[2] - item.shape[1]))
    )
    out_ref[0, base:, :] = jnp.concatenate(
        [
            wide(gain_ref[0]),
            wide(shift_ref[0]),
            wide(head_ref[0]),
            wide(hidden),
            jnp.zeros((7, out_ref.shape[2]), F32),
        ],
        axis=0,
    ).astype(BF16)


def chosen_block(bank):
    rest = bank.shape[1:]
    return pl.BlockSpec((1, *rest), lambda i, info: (info[3],) + (0,) * len(rest))


def pick_first(info, qkv_bank, gain_bank, shift_bank, head_bank, hidden_bank):
    qkv_bank = qkv_bank.transpose(0, 2, 1, 3)
    rows, columns = qkv_bank.shape[2], 3 * qkv_bank.shape[3]
    shape = (1, -(-rows // 16) * 16 + 16, columns)
    return pl.pallas_call(
        pick_first_kernel,
        grid_spec=pltpu.PrefetchScalarGridSpec(
            num_scalar_prefetch=1,
            grid=(1,),
            in_specs=[
                chosen_block(bank) for bank in (qkv_bank, gain_bank, shift_bank, head_bank)
            ]
            + [whole(*hidden_bank.shape)],
            out_specs=pl.BlockSpec(shape, lambda i, info: (0, 0, 0)),
        ),
        out_shape=jax.ShapeDtypeStruct(shape, BF16),
        cost_estimate=SHORT,
        name="pick_first",
    )(info, qkv_bank, gain_bank, shift_bank, head_bank, hidden_bank)


def pick_rest_kernel(info, up_ref, down_ref, out_ref, qkv_ref, *refs):
    packed_ref = refs[-1]
    rows, first = up_ref.shape[1:]
    second = first + down_ref.shape[2]
    third = second + qkv_ref.shape[2]
    packed_ref[:, :first] = up_ref[0]
    packed_ref[:, first:second] = down_ref[0]
    packed_ref[:, second:third] = qkv_ref[0, :rows]
    packed_ref[:, third:] = out_ref[0].astype(F32).T.astype(BF16)


def pick_rest(info, up_bank, down_bank, out_bank, first, after):
    down_bank = down_bank.transpose(0, 2, 1)
    columns = up_bank.shape[2] + down_bank.shape[2] + out_bank.shape[1] + first.shape[2]
    shape = (up_bank.shape[1], columns)
    return pl.pallas_call(
        pick_rest_kernel,
        grid_spec=pltpu.PrefetchScalarGridSpec(
            num_scalar_prefetch=1,
            grid=(1,),
            in_specs=[chosen_block(bank) for bank in (up_bank, down_bank, out_bank)]
            + [pl.BlockSpec(first.shape, lambda i, info: (0, 0, 0))]
            + [ANYWHERE] * len(after),
            out_specs=whole(*shape),
        ),
        out_shape=jax.ShapeDtypeStruct(shape, BF16),
        cost_estimate=SHORT,
        name="pick_rest",
    )(info, up_bank, down_bank, out_bank, first, *after)


def assemble_kernel(order, info, *refs):
    parts, refs = refs[:-6], refs[-6:]
    turned_ref, vec_ref, bias_ref, own_ref, rows_ref, small_ref = refs
    count = len(order)
    held = [(part, n) for part in parts for n in range(part.shape[0])]
    rows = turned_ref.shape[1] // count
    for (part, n), k in zip(held, order):
        owner = jnp.bitwise_xor(info[2], k)
        at = pl.ds(pl.multiple_of(owner * rows, rows), rows)
        rows_ref[at, :] = part[n, :rows]
        small_ref[at, :] = part[n, rows:, 0:128].astype(F32).T[:rows]
    own_ref[...] = parts[0][0, :rows]
    turned_ref[...] = rows_ref[...].T
    small = small_ref[...]
    wide = jnp.concatenate([small, jnp.zeros((small.shape[0], 112), F32)], axis=1)
    vec_ref[...] = wide.T[0:16]
    heads = turned_ref.shape[0] // (3 * HEAD_DIM)
    few = heads * HEAD_DIM // count
    column = lambda n: jnp.concatenate(
        [small[p * rows : p * rows + few, n : n + 1] for p in range(count)], axis=0
    )
    q_bias, v_bias = column(6), column(7)
    for h in range(heads):
        at = h * 3 * HEAD_DIM
        bias_ref[at : at + HEAD_DIM, :] = q_bias[h * HEAD_DIM : (h + 1) * HEAD_DIM]
        bias_ref[at + HEAD_DIM : at + 2 * HEAD_DIM, :] = jnp.zeros((HEAD_DIM, 1), F32)
        bias_ref[at + 2 * HEAD_DIM : at + 3 * HEAD_DIM, :] = v_bias[h * HEAD_DIM : (h + 1) * HEAD_DIM]


def gather_qkv(info, part, count, rows):
    _, depth, columns = part.shape
    heads = columns // (3 * HEAD_DIM)
    few = heads * HEAD_DIM // count
    if count != 8 or rows % 16 or few % 8:
        parts = lax.all_gather(part[0], "dp", axis=0, tiled=False)
        turned = parts[:, :rows].reshape(count * rows, columns).T
        small = parts[:, depth - 16 :].astype(F32).transpose(1, 0, 2)
        vectors = small[:, :, :rows].reshape(16, count * rows)
        bias = small[6:8, :, :few].reshape(2, heads, HEAD_DIM)
        bias = jnp.stack([bias[0], jnp.zeros_like(bias[0]), bias[1]], axis=1)
        return turned, vectors, bias.reshape(columns, 1), part[0, :rows], part, part
    joined, order, others = part, [0], []
    for mask in (4, 2, 1):
        other = lax.ppermute(joined, "dp", [(i, i ^ mask) for i in range(count)])
        others.append(other)
        if mask > 1:
            joined = jnp.concatenate([joined, other])
        order = order + [k ^ mask for k in order]
    fixed = lambda *shape: pl.BlockSpec(shape, lambda i, info: (0,) * len(shape))
    outs = [
        ((columns, count * rows), BF16),
        ((16, count * rows), F32),
        ((columns, 1), F32),
        ((rows, columns), BF16),
    ]
    found = pl.pallas_call(
        functools.partial(assemble_kernel, order),
        grid_spec=pltpu.PrefetchScalarGridSpec(
            num_scalar_prefetch=1,
            grid=(1,),
            in_specs=[fixed(*item.shape) for item in (part, *others)],
            out_specs=[fixed(*shape) for shape, _ in outs],
            scratch_shapes=[
                pltpu.VMEM((count * rows, columns), BF16),
                pltpu.VMEM((count * rows, 16), F32),
            ],
        ),
        out_shape=[jax.ShapeDtypeStruct(shape, kind) for shape, kind in outs],
        cost_estimate=SHORT,
        name="assemble",
    )(info, part, *others)
    return *found, others[0], others[2]


def enter_kernel(spans, w_ref, vec_ref, bias_ref, *refs):
    parts, (qkv_ref, normed_ref, hidden_ref, held) = refs[:-4], refs[-4:]
    for part, (first, last) in zip(parts, spans):

        @pl.when((pl.program_id(0) >= first) & (pl.program_id(0) < last))
        def _():
            held[...] = part[...]

    row = lax.broadcasted_iota(jnp.int32, (w_ref.shape[0], 1), 0)
    scale = jnp.where(lax.rem(row, 3 * HEAD_DIM) < HEAD_DIM, LOG2E / 8.0, 1.0)
    unit, _ = normalise(held[...].astype(F32))
    rounded = (unit * vec_ref[0:1] + vec_ref[2:3]).astype(BF16)
    normed_ref[...] = rounded
    flat = product(w_ref[...], rounded, NT)
    qkv_ref[...] = ((flat + bias_ref[...]) * scale).astype(BF16)
    hidden_ref[...] = vec_ref[8:9]


def enter(parts, turned, vectors, bias):
    block = min(part.shape[0] for part in parts)
    width = parts[0].shape[1]
    columns = turned.shape[0]
    fixed = lambda shape: pl.BlockSpec(shape, lambda i: (0, 0), pipeline_mode=pl.Buffered(1))
    spans, specs, first = [], [], 0
    for part in parts:
        blocks = part.shape[0] // block
        spans.append((first, first + blocks))
        specs.append(
            pl.BlockSpec(
                (block, width), lambda i, first=first, n=blocks: (jnp.clip(i - first, 0, n - 1), 0)
            )
        )
        first += blocks
    return pl.pallas_call(
        functools.partial(enter_kernel, spans),
        grid=(first,),
        in_specs=[fixed(turned.shape), fixed(vectors.shape), fixed(bias.shape)] + specs,
        out_specs=[
            pl.BlockSpec((columns, block), lambda i: (0, i)),
            pl.BlockSpec((block, width), lambda i: (i, 0)),
            fixed((1, width)),
        ],
        out_shape=[
            jax.ShapeDtypeStruct((columns, first * block), BF16),
            jax.ShapeDtypeStruct((first * block, width), BF16),
            jax.ShapeDtypeStruct((1, width), F32),
        ],
        scratch_shapes=[pltpu.VMEM((block, width), BF16)],
        cost_estimate=SHORT,
        name="enter",
    )(turned, vectors, bias, *parts)


TILE = 256
TALL = 512


def middle_kernel(parts, info, tokens_ref, cot_ref, out_ref, vec_ref, up_ref, down_ref, *refs):
    given, refs = refs[:parts], refs[parts:]
    (result_ref, grads_out, grad_ref, stats_ref), refs = refs[:4], refs[4:]
    back, refs = refs[: 2 * QUARTERS], refs[2 * QUARTERS :]
    mixed, middle, low, low_t, cot_t, activ, grad_u, branch, grad_two, *bufs = refs
    *bufs, grads_ref, sent = bufs
    k = pl.program_id(0)
    count, width = tokens_ref.shape
    tiles = count // TALL
    local_width = width // QUARTERS
    spans = [slice(m * TALL, (m + 1) * TALL) for m in range(tiles)]

    def tiled(body):
        def at_tile(m, carry):
            return body(pl.ds(pl.multiple_of(m * TALL, TALL), TALL), carry)

        return at_tile

    @pl.when(k == 0)
    def _():
        for n, part in enumerate(given):
            mixed[n * HEAD_DIM : (n + 1) * HEAD_DIM, :] = part[...]
        low_t[width:, :] = jnp.ones((16, count), BF16)

        @tiled
        def begin(at, carry):
            attended = product(mixed[:, at], out_ref[...], CT)
            value = tokens_ref[at, :].astype(F32) + attended + vec_ref[4:5]
            middle[at, :] = value
            unit, _ = normalise(value)
            rounded = (unit * vec_ref[1:2] + vec_ref[3:4]).astype(BF16)
            low[at, :] = rounded
            low_t[0:width, at] = rounded.T
            cot_t[:, at] = cot_ref[at, :].T
            branch[at, :] = jnp.zeros((TALL, width), F32)
            grad_two[at, :] = jnp.zeros((TALL, width), F32)
            return carry

        lax.fori_loop(0, tiles, begin, 0)

    bias = vec_ref[pl.ds(8 + jnp.bitwise_xor(k, info[1]), 1), :]

    def first(m, u, g):
        u[...] = product(low[spans[m], :], up_ref[...], NN) + bias
        g[...] = product(cot_ref[spans[m], :], down_ref[...], NN)

    def second(m, u, g):
        value, slope = gelu_both(u[...])
        a = value.astype(BF16)
        gu = (g[...] * slope).astype(BF16)
        activ[spans[m], :] = a
        grad_u[spans[m], :] = gu
        branch[spans[m], :] += product(a, down_ref[...], NT)
        grad_two[spans[m], :] += product(gu, up_ref[...], NT)

    turns = (bufs[:2], bufs[2:])
    first(0, *turns[0])
    for m in range(tiles):
        if m + 1 < tiles:
            first(m + 1, *turns[(m + 1) % 2])
        second(m, *turns[m % 2])
    rows = pl.ds(pl.multiple_of(k * width, width), width)

    grad_up = product(low_t[...], grad_u[...], NN)
    grads_ref[rows, 0:width] = grad_up[:width].astype(BF16)
    stats_ref[pl.ds(4 + k, 1), :] = grad_up[width : width + 1]
    grads_ref[rows, width : 2 * width] = product(cot_t[...], activ[...], NN).astype(BF16)

    def leaving(n, columns):
        part = pl.ds(n * width, width)
        return pltpu.make_async_copy(
            grads_ref.at[part, columns], grads_out.at[part, columns], sent.at[n, columns.start // width // 2]
        )

    wide, narrow = slice(0, 2 * width), slice(2 * width, 2 * width + local_width)
    for n in range(QUARTERS):

        @pl.when(k == n)
        def _():
            leaving(n, wide).start()

    @pl.when(k == pl.num_programs(0) - 1)
    def _():
        @tiled
        def end(at, sums):
            value = middle[at, :]
            result_ref[at, :] = (value + branch[at, :] + vec_ref[5:6]).astype(BF16)
            unit, scale = normalise(value)
            grad = grad_two[at, :]
            cot = cot_ref[at, :].astype(F32)
            total = cot + normalise_back(grad * vec_ref[1:2], unit, scale)
            grad_ref[at, :] = total
            e = total.astype(BF16)
            low[at, :] = e
            mixed_grad = product(out_ref[...], e, CT).astype(BF16)
            for n, part in enumerate(back):
                row = n // 2 * local_width + n % 2 * HEAD_DIM
                part[:, at] = mixed_grad[row : row + part.shape[0]]
            items = (grad * unit, grad, e.astype(F32), cot)
            return tuple(
                old + jnp.sum(item, axis=0, keepdims=True) for old, item in zip(sums, items)
            )

        sums = lax.fori_loop(0, tiles, end, (jnp.zeros((1, width), F32),) * 4)
        for n in range(4):
            stats_ref[n : n + 1, :] = sums[n]
        grad_out = product(low[...], mixed[...], CT).astype(BF16)
        for x in range(QUARTERS):
            owner = jnp.bitwise_xor(info[1], x)
            grads_ref[pl.ds(pl.multiple_of(owner * width, width), width), 2 * width :] = grad_out[
                :, x * local_width : (x + 1) * local_width
            ]
        for n in range(QUARTERS):
            leaving(n, narrow).start()
        for n in range(QUARTERS):
            leaving(n, wide).wait()
            leaving(n, narrow).wait()


def middle_part(info, tokens, cotangent, out_t, vectors, bank, mixed):
    count, width = tokens.shape
    local_width = width // QUARTERS
    outs = [
        ((count, width), BF16),
        ((QUARTERS * width, 2 * width + local_width), BF16),
        ((count, width), F32),
        ((8, width), F32),
    ] + [((HEAD_DIM, count), BF16), ((local_width - HEAD_DIM, count), BF16)] * QUARTERS
    return pl.pallas_call(
        functools.partial(middle_kernel, len(mixed)),
        grid_spec=pltpu.PrefetchScalarGridSpec(
            num_scalar_prefetch=1,
            grid=(QUARTERS,),
            in_specs=[
                whole(count, width),
                whole(count, width),
                whole(width, width),
                whole(16, width),
                pl.BlockSpec((width, width), lambda k, info: (k, 0)),
                pl.BlockSpec((width, width), lambda k, info: (k, 1)),
            ]
            + [whole(HEAD_DIM, count)] * len(mixed),
            out_specs=[whole(*outs[0][0]), ANYWHERE] + [whole(*shape) for shape, _ in outs[2:]],
            scratch_shapes=[
                pltpu.VMEM((width, count), BF16),
                pltpu.VMEM((count, width), F32),
                pltpu.VMEM((count, width), BF16),
                pltpu.VMEM((width + 16, count), BF16),
                pltpu.VMEM((width, count), BF16),
                pltpu.VMEM((count, width), BF16),
                pltpu.VMEM((count, width), BF16),
                pltpu.VMEM((count, width), F32),
                pltpu.VMEM((count, width), F32),
            ]
            + [pltpu.VMEM((TALL, width), F32)] * 4
            + [pltpu.VMEM(outs[1][0], BF16), pltpu.SemaphoreType.DMA((QUARTERS, 2))],
        ),
        out_shape=[jax.ShapeDtypeStruct(shape, kind) for shape, kind in outs],
        compiler_params=pltpu.CompilerParams(vmem_limit_bytes=66_000_000),
        cost_estimate=pl.CostEstimate(
            flops=40_000_000_000, bytes_accessed=40_000_000, transcendentals=3_200_000
        ),
        name="middle",
    )(info, tokens, cotangent, out_t, vectors, bank, bank, *mixed)


def add_back(grad, tokens_ref, vec_ref, grad_ref):
    unit, scale = normalise(tokens_ref[...].astype(F32))
    return grad_ref[...] + normalise_back(grad * vec_ref[0:1], unit, scale)


def exit_first_kernel(heads, info, *refs):
    count = heads * QUARTERS
    deltas, weights, refs = refs[:count], refs[count : count + 4], refs[count + 4 :]
    tokens_ref, grad_ref, vec_ref, sum_ref, rest_ref, d_all, w_all = refs
    span = deltas[0].shape[0]

    @pl.when(pl.program_id(0) == 0)
    def _():
        for x in range(QUARTERS):
            at = x * heads * span
            w_all[:, at : at + heads * span] = weights[x][:, : heads * span]
            rest_ref[:, x * span : (x + 1) * span] = weights[x][
                :, heads * span : (heads + 1) * span
            ]

    for x in range(QUARTERS):
        for h in range(heads):
            at = (x * heads + h) * span
            d_all[at : at + span, :] = deltas[h * QUARTERS + x][...]
    sum_ref[...] = add_back(product(w_all[...], d_all[...], NN).T, tokens_ref, vec_ref, grad_ref)


def exit_last_kernel(skip, info, *refs):
    deltas, refs = refs[:4], refs[4:]
    w_ref, tokens_ref, grad_ref, vec_ref, *refs = refs
    out_ref, d_all = refs[skip:]
    span = deltas[0].shape[0]
    for x in range(QUARTERS):
        d_all[x * span : (x + 1) * span, :] = deltas[x][...]
    grad = product(w_ref[...], d_all[...], NN).T
    out_ref[...] = add_back(grad, tokens_ref, vec_ref, grad_ref).astype(BF16)


def lanes(rows):
    return pl.BlockSpec((rows, TILE), lambda i, info: (0, i))


def lines(columns):
    return pl.BlockSpec((TILE, columns), lambda i, info: (i, 0))


def exit_first(info, deltas, bank, tokens, grad, vectors):
    count, width = tokens.shape
    span = deltas[0].shape[0]
    heads = len(deltas) // QUARTERS
    depth = len(deltas) * span
    blocks = [
        pl.BlockSpec(
            (width, width),
            lambda i, info, x=x: (jnp.bitwise_xor(info[1], x), 2),
            pipeline_mode=pl.Buffered(1),
        )
        for x in range(QUARTERS)
    ]
    return pl.pallas_call(
        functools.partial(exit_first_kernel, heads),
        grid_spec=pltpu.PrefetchScalarGridSpec(
            num_scalar_prefetch=1,
            grid=(count // TILE,),
            in_specs=[lanes(span)] * len(deltas)
            + blocks
            + [lines(width), lines(width), whole(*vectors.shape)],
            out_specs=[lines(width), whole(width, QUARTERS * span)],
            scratch_shapes=[pltpu.VMEM((depth, TILE), BF16), pltpu.VMEM((width, depth), BF16)],
        ),
        out_shape=[
            jax.ShapeDtypeStruct((count, width), F32),
            jax.ShapeDtypeStruct((width, QUARTERS * span), BF16),
        ],
        cost_estimate=SHORT,
        name="exit_first",
    )(info, *deltas, *[bank] * QUARTERS, tokens, grad, vectors)


def exit_last(info, deltas, weights, tokens, grad, vectors, after):
    count, width = tokens.shape
    span = deltas[0].shape[0]
    return pl.pallas_call(
        functools.partial(exit_last_kernel, len(after)),
        grid_spec=pltpu.PrefetchScalarGridSpec(
            num_scalar_prefetch=1,
            grid=(count // TILE,),
            in_specs=[lanes(span)] * QUARTERS
            + [whole(*weights.shape), lines(width), lines(width), whole(*vectors.shape)]
            + [ANYWHERE] * len(after),
            out_specs=lines(width),
            scratch_shapes=[pltpu.VMEM((QUARTERS * span, TILE), BF16)],
        ),
        out_shape=jax.ShapeDtypeStruct((count, width), BF16),
        cost_estimate=SHORT,
        name="exit_last",
    )(info, *deltas, weights, tokens, grad, vectors, *after)


def pack_first_kernel(rows, weights, stats_ref, out_ref):
    span = weights[0].shape[1]
    count, depth, columns = out_ref.shape
    stats = jnp.concatenate(pieces(stats_ref[...]), axis=0)
    for p in range(count):
        for h, weight in enumerate(weights):
            out_ref[p, 0:rows, h * span : (h + 1) * span] = weight[p * rows : (p + 1) * rows]
        part = jnp.concatenate(
            [stats[:, p * rows : (p + 1) * rows], jnp.zeros((24, columns - rows), F32)], axis=1
        )
        part = jnp.concatenate([part, jnp.zeros((8, columns), F32)], axis=0)
        out_ref[p, depth - 32 :, :] = part.astype(BF16)


def pack_last_kernel(rows, weight, sums, out_ref):
    span = weight.shape[1]
    count, depth, columns = out_ref.shape
    lined = [jnp.broadcast_to(item[...], (span, 128)).T[0:1] for item in sums]
    lined = [piece for item in lined for piece in pieces(item)]
    lined = jnp.concatenate(lined + [jnp.zeros((16 - len(lined), span), F32)], axis=0)
    lined = jnp.concatenate([lined, jnp.zeros((16, columns - span), F32)], axis=1).astype(BF16)
    out_ref[...] = jnp.zeros_like(out_ref)
    for p in range(count):
        out_ref[p, 0:rows, 0:span] = weight[p * rows : (p + 1) * rows]
        out_ref[p, depth - 16 :, :] = lined


def exchange(kernel, count, items, below, columns, after, name):
    width = items[0].shape[0]
    rows = width // count
    fixed = lambda shape: pl.BlockSpec(shape, lambda i: (0,) * len(shape))
    shape = (count, -(-rows // 16) * 16 + below, columns)

    def body(*refs):
        kernel(rows, refs[: len(items)], refs[-1])

    packed = pl.pallas_call(
        body,
        grid=(1,),
        in_specs=[fixed(item.shape) for item in items] + [ANYWHERE] * len(after),
        out_specs=fixed(shape),
        out_shape=jax.ShapeDtypeStruct(shape, BF16),
        cost_estimate=SHORT,
        name=name,
    )(*items, *after)
    received = lax.all_to_all(
        packed.reshape(-1, columns), "dp", split_axis=0, concat_axis=0, tiled=True
    )
    return received.reshape(shape)


def exchange_first(weights, stats, count):
    kernel = lambda rows, refs, out: pack_first_kernel(rows, refs[:-1], refs[-1], out)
    columns = sum(weight.shape[1] for weight in weights)
    return exchange(kernel, count, [*weights, stats], 32, columns, [], "pack_first")


def exchange_last(weight, sums, count, after):
    kernel = lambda rows, refs, out: pack_last_kernel(rows, refs[0], refs[1:], out)
    return exchange(kernel, count, [weight, *sums], 16, 256, after, "pack_last")


def finish_kernel(heads, early_ref, late_ref, weight_ref, small_ref, total_ref, stats_ref, sums_ref):
    rows, columns = weight_ref.shape
    span = columns // heads
    early, late = early_ref[0].astype(F32), late_ref[0].astype(F32)
    for p in range(1, early_ref.shape[0]):
        early = early + early_ref[p].astype(F32)
        late = late + late_ref[p].astype(F32)
    grads = jnp.concatenate([early[:rows], late[:rows, :span]], axis=1)
    base = early.shape[0] - 32
    stats = early[base : base + 8] + early[base + 8 : base + 16] + early[base + 16 : base + 24]
    lined = late[late.shape[0] - 16 :, :span]
    sums = jnp.concatenate(
        [lined[3 * h : 3 * h + 1] + lined[3 * h + 1 : 3 * h + 2] + lined[3 * h + 2 : 3 * h + 3]
         for h in range(heads)],
        axis=1,
    )
    weights = weight_ref[...].astype(F32)
    shift = jnp.sum(weights * sums, axis=1, keepdims=True)
    gain = jnp.sum(weights * grads, axis=1, keepdims=True)
    gain = (gain - small_ref[:, 1:2] * shift) / small_ref[:, 0:1]
    sums_ref[...] = sums
    for n in range(columns // HEAD_DIM):
        at = n // 3 * HEAD_DIM
        total_ref[n % 3, :, at : at + HEAD_DIM] = grads[:, n * HEAD_DIM : (n + 1) * HEAD_DIM]
    turned = jnp.concatenate([shift, gain, jnp.zeros((rows, 6), F32)], axis=1).T
    stats_ref[...] = jnp.concatenate([stats[:, :rows], turned], axis=0)


def finish(early, late, weights, small):
    rows, columns = weights.shape
    heads = columns // (3 * HEAD_DIM)
    fixed = lambda shape: pl.BlockSpec(shape, lambda i: (0,) * len(shape))
    outs = [(3, rows, columns // 3), (16, rows), (1, columns)]
    return pl.pallas_call(
        functools.partial(finish_kernel, heads),
        grid=(1,),
        in_specs=[fixed(item.shape) for item in (early, late, weights, small)],
        out_specs=[fixed(shape) for shape in outs],
        out_shape=[jax.ShapeDtypeStruct(shape, F32) for shape in outs],
        cost_estimate=SHORT,
        name="finish",
    )(early, late, weights, small)


def unpack_kernel(shard_ref, up_ref, down_ref, out_ref):
    first, second = up_ref.shape[1], up_ref.shape[1] + down_ref.shape[1]
    up_ref[...] = shard_ref[:, :first].astype(F32)
    down_ref[...] = shard_ref[:, first:second].astype(F32)
    out_ref[...] = shard_ref[:, second:].astype(F32).T


def unpack(shard, first, second):
    rows, columns = shard.shape
    outs = [(rows, first), (rows, second - first), (columns - second, rows)]
    fixed = lambda shape: pl.BlockSpec(shape, lambda i: (0, 0))
    return pl.pallas_call(
        unpack_kernel,
        grid=(1,),
        in_specs=[fixed(shard.shape)],
        out_specs=[fixed(shape) for shape in outs],
        out_shape=[jax.ShapeDtypeStruct(shape, F32) for shape in outs],
        cost_estimate=SHORT,
        name="unpack",
    )(shard)


def local(
    n_dp,
    tokens,
    cotangent,
    tie_index,
    image_start,
    qkv_bank,
    out_bank,
    up_bank,
    down_bank,
    gain_bank,
    shift_bank,
    head_bias_bank,
    hidden_bias_bank,
):
    own = lax.axis_index("tensor")
    own_dp = lax.axis_index("dp")
    width = tokens.shape[1]
    rows = qkv_bank.shape[1]
    local_width = qkv_bank.shape[3]
    hidden_cols = up_bank.shape[2]
    heads = local_width // HEAD_DIM
    qkv_cols = 3 * local_width
    few = head_bias_bank.shape[2]
    info = jnp.stack([image_start[0], own, own_dp, tie_index[0]]).astype(jnp.int32)

    step = QUARTER // 2
    far = [swap(tokens[n * step : (n + 1) * step], 2) for n in range(2)]
    near = swap(tokens, 1)

    packed = pick_first(info, qkv_bank, gain_bank, shift_bank, head_bias_bank, hidden_bias_bank)
    turned, vectors, bias, qkv_part, started, ended = gather_qkv(info, packed, n_dp, rows)
    held = jnp.where(ended[0, 0, 0] > 1e30, jnp.zeros_like(far[1]), far[1])
    far_near = [swap(far[0], 1), swap(held, 1)]
    own_small = packed[0, -16:].astype(F32)
    bank_part = pick_rest(info, up_bank, down_bank, out_bank, packed, [started, far[0]])
    bank = lax.all_gather(bank_part, ("tensor", "dp"), axis=0, tiled=True)
    c_out = 2 * hidden_cols
    out_t = jnp.concatenate(
        [
            lax.dynamic_slice(
                bank,
                (jnp.bitwise_xor(own, x) * width, c_out + qkv_cols),
                (width, local_width),
            )
            for x in range(QUARTERS)
        ],
        axis=1,
    )

    qkv, normed, hidden_bias = enter([tokens, near] + far + far_near, turned, vectors, bias)
    hidden_bias = jnp.concatenate(
        [hidden_bias] + [swap(hidden_bias, x) for x in range(1, QUARTERS)]
    )

    outs, lses, mixed = [], [], [[None] * heads for _ in range(QUARTERS)]
    for head in range(heads):
        after = [mixed[x][head - 2] for x in range(1, QUARTERS)] if head > 1 else []
        *out, lse = attend_forward(info, qkv, head, after)
        if head == heads - 1:
            out = gate(out, [mixed[x][head - 1] for x in range(1, QUARTERS)])
        outs.append(out)
        lses.append(lse)
        for x in range(QUARTERS):
            mixed[x][head] = swap(out[x], x) if x else out[x]

    rows_two = jnp.concatenate([vectors[0:8], hidden_bias, vectors[8:12]])
    result, grads, grad_middle, stats, *mixed_grads = middle_part(
        info, tokens, cotangent, out_t, rows_two, bank, [part for quarter in mixed for part in quarter]
    )
    shard = lax.psum_scatter(grads, ("tensor", "dp"), scatter_dimension=0, tiled=True)
    up_shard, down_shard, out_shard = unpack(shard, hidden_cols, c_out)

    deltas, weight_grads, sums = [], [], []
    grads_first = [swap(mixed_grads[2 * x], x) if x else mixed_grads[0] for x in range(QUARTERS)]
    rest = gate([mixed_grads[2 * x + 1] for x in range(QUARTERS)], grads_first[1:])
    grads_rest = [swap(rest[x], x) if x else rest[0] for x in range(QUARTERS)]
    for head in range(heads):
        *parts, weight_grad, summed = attend_backward(
            info,
            qkv,
            grads_rest if head else grads_first,
            max(head - 1, 0),
            outs[head],
            lses[head],
            normed,
            head,
            [rest[0]] if head == 0 else deltas[head - 2][1:] if head > 1 else [],
        )
        deltas.append([swap(parts[x], x) if x else parts[x] for x in range(QUARTERS)])
        weight_grads.append(weight_grad)
        sums.append(summed)
        if head == heads - 2:
            early_sums = exchange_first(weight_grads, stats, n_dp)
    early = [part for parts in deltas[:-1] for part in parts]

    late_sums = exchange_last(weight_grads[-1], sums, n_dp, [*deltas[-2][1:], early_sums])
    small = jnp.stack([own_small[0, :rows], own_small[2, :rows]], axis=1)
    qkv_total, stats, sums = finish(early_sums, late_sums, qkv_part, small)
    found = stats
    stats = (stats + swap(stats, 1)) + (swap(stats, 2) + swap(stats, 3))

    by_part = sums.reshape(heads, 3, HEAD_DIM)
    head_sums = jnp.stack([by_part[:, 0].reshape(-1), by_part[:, 2].reshape(-1)])
    head_shard = lax.dynamic_slice_in_dim(head_sums, own_dp * few, few, 1)
    hidden_shard = lax.dynamic_index_in_dim(stats[4:8], own, 0, keepdims=False)
    gain_grads = jnp.stack([stats[9], stats[0]])
    shift_grads = jnp.stack([stats[8], stats[1], stats[2], stats[3]])

    grad_part, weights = exit_first(info, early, bank, tokens, grad_middle, vectors)
    grad_tokens = exit_last(info, deltas[-1], weights, tokens, grad_part, vectors, [found])

    return (
        result,
        grad_tokens,
        qkv_total.transpose(1, 0, 2),
        out_shard,
        up_shard,
        down_shard.T,
        gain_grads,
        shift_grads,
        head_shard,
        hidden_shard,
    )


def solution(mesh):
    placed = (
        P(("dp", "tensor"), None),
        P(("dp", "tensor"), None),
        P(),
        P("dp"),
        P(None, "dp", None, "tensor"),
        P(None, "tensor", "dp"),
        P(None, "dp", "tensor"),
        P(None, "tensor", "dp"),
        P(None, None, "dp"),
        P(None, None, "dp"),
        P(None, None, ("tensor", "dp")),
        P(None, ("tensor", "dp")),
    )
    return jax.shard_map(
        functools.partial(local, mesh.shape["dp"]),
        mesh=mesh,
        in_specs=placed,
        out_specs=(
            P(("dp", "tensor"), None),
            P(("dp", "tensor"), None),
            P("dp", None, "tensor"),
            P("tensor", "dp"),
            P("dp", "tensor"),
            P("tensor", "dp"),
            P(None, "dp"),
            P(None, "dp"),
            P(None, ("tensor", "dp")),
            P(("tensor", "dp")),
        ),
        check_vma=False,
    )
```

```python
import functools
import math

import jax
import jax.numpy as jnp
from jax import lax
from jax.experimental import pallas as pl
from jax.experimental.pallas import tpu as pltpu
from jax.sharding import PartitionSpec as P

HEAD_DIM = 64
SEQ_LEN = 4096
IMG = 256
EPSILON = 1e-05
LOG2E = 1.4426950408889634
BLOCK = 512
BLOCKS = SEQ_LEN // BLOCK
QUARTERS = 4
QUARTER = SEQ_LEN // QUARTERS
PER_QUARTER = QUARTER // BLOCK
PAIRS = BLOCKS * (BLOCKS + 1) // 2
F32 = jnp.float32
BF16 = jnp.bfloat16

NT = (((1,), (1,)), ((), ()))
NN = (((1,), (0,)), ((), ()))
TN = (((0,), (0,)), ((), ()))
CT = (((0,), (1,)), ((), ()))


def product(left, right, dims):
    return lax.dot_general(left, right, dims, preferred_element_type=F32)


def place(block, own):
    quarter = jnp.bitwise_xor(block // PER_QUARTER, own)
    return pl.multiple_of((quarter * PER_QUARTER + block % PER_QUARTER) * BLOCK, BLOCK)


def following(row, col, cross):
    wrap = col + 1 >= row + 1 + jnp.where(cross == row, 1, 0)
    return jnp.where(wrap, row + 1, row), jnp.where(wrap, 0, col + 1)


def crossing(start):
    low, high = start // BLOCK, (start + IMG - 1) // BLOCK
    cross = jnp.where(high > low, low, -1)
    return cross, PAIRS + jnp.where(cross >= 0, 1, 0)


def last_key(pos, start):
    return jnp.where((pos >= start) & (pos < start + IMG), start + (IMG - 1), pos)


def forward_kernel(
    skip, info, q_ref, k_ref, v_ref, *refs
):
    o_0, o_1, o_2, o_3, lse_ref, k_rows, v_ones, s_a, s_b, top_a, top_b, top, total, o_all = refs[skip:]
    start, own = info[0], info[1]
    cross, pairs = crossing(start)

    def prepare(block, carry):
        at = pl.ds(pl.multiple_of(block * BLOCK, BLOCK), BLOCK)
        k_rows[at, :] = k_ref[:, at].T
        return carry

    lax.fori_loop(0, BLOCKS, prepare, 0)
    v_ones[0:64, :] = v_ref[...]
    v_ones[64:80, :] = jnp.ones((16, SEQ_LEN), BF16)
    total[...] = jnp.zeros_like(total)

    def score(row, col, dst, dst_top, masked):
        rows = pl.ds(place(jnp.minimum(row, BLOCKS - 1), own), BLOCK)
        s = product(k_rows[pl.ds(place(col, own), BLOCK), :], q_ref[:, rows], NN)
        if masked:
            pos = row * BLOCK + lax.broadcasted_iota(jnp.int32, (1, BLOCK), 1)
            limit = last_key(pos, start) - col * BLOCK
            s = jnp.where(lax.broadcasted_iota(jnp.int32, (BLOCK, BLOCK), 0) <= limit, s, -1e30)
        dst[...] = s
        dst_top[...] = jnp.max(s, axis=0, keepdims=True)

    def step(src, src_top, dst, dst_top, col, next_row, next_col, masked):
        score(next_row, next_col, dst, dst_top, masked)
        old = jnp.where(col == 0, -1e30, top[...])
        new = jnp.maximum(old, src_top[...])
        p = jnp.exp2(src[...] - new).astype(BF16)
        mixed = product(v_ones[:, pl.ds(place(col, own), BLOCK)], p, NN)
        total[...] = total[...] * jnp.exp2(old - new) + mixed
        top[...] = new

    def half(src, src_top, dst, dst_top, row, col, live):
        next_row, next_col = following(row, col, cross)
        masked = next_col >= next_row

        @pl.when(live & masked)
        def _():
            step(src, src_top, dst, dst_top, col, next_row, next_col, True)

        @pl.when(live & jnp.logical_not(masked))
        def _():
            step(src, src_top, dst, dst_top, col, next_row, next_col, False)

        @pl.when(live & (next_col == 0))
        def _():
            at = pl.ds(place(row, own), BLOCK)
            summed = total[64:65]
            o_all[:, at] = (total[0:64] / summed).astype(BF16)
            lse_ref[:, at] = top[...] + jnp.log2(summed)

        return next_row, next_col

    score(0, 0, s_a, top_a, True)

    def both(turn, carry):
        row, col = half(s_a, top_a, s_b, top_b, *carry, turn >= 0)
        return half(s_b, top_b, s_a, top_a, row, col, 2 * turn + 1 < pairs)

    lax.fori_loop(0, (pairs + 1) // 2, both, (jnp.int32(0), jnp.int32(0)))

    for x, o_ref in enumerate((o_0, o_1, o_2, o_3)):
        o_ref[...] = o_all[:, x * QUARTER : (x + 1) * QUARTER]


def gate(items, after):
    def kernel(*refs):
        pass

    return pl.pallas_call(
        kernel,
        in_specs=[ANYWHERE] * (len(items) + len(after)),
        out_specs=[ANYWHERE] * len(items),
        out_shape=[jax.ShapeDtypeStruct(item.shape, item.dtype) for item in items],
        input_output_aliases={n: n for n in range(len(items))},
        cost_estimate=SHORT,
        name="gate",
    )(*items, *after)


def head_spec(head, part):
    return pl.BlockSpec((HEAD_DIM, SEQ_LEN), lambda i, info: (head * 3 + part, 0))


def whole(*shape):
    return pl.BlockSpec(shape, lambda i, info: (0, 0), pipeline_mode=pl.Buffered(1))


ANYWHERE = pl.BlockSpec(memory_space=pl.ANY)
SHORT = pl.CostEstimate(flops=1, bytes_accessed=1, transcendentals=0)


def attend_forward(info, qkv, head, after):
    return pl.pallas_call(
        functools.partial(forward_kernel, len(after)),
        grid_spec=pltpu.PrefetchScalarGridSpec(
            num_scalar_prefetch=1,
            grid=(1,),
            in_specs=[head_spec(head, part) for part in range(3)] + [ANYWHERE] * len(after),
            out_specs=[whole(HEAD_DIM, QUARTER)] * QUARTERS + [whole(1, SEQ_LEN)],
            scratch_shapes=[
                pltpu.VMEM((SEQ_LEN, HEAD_DIM), BF16),
                pltpu.VMEM((80, SEQ_LEN), BF16),
                pltpu.VMEM((BLOCK, BLOCK), F32),
                pltpu.VMEM((BLOCK, BLOCK), F32),
                pltpu.VMEM((1, BLOCK), F32),
                pltpu.VMEM((1, BLOCK), F32),
                pltpu.VMEM((1, BLOCK), F32),
                pltpu.VMEM((80, BLOCK), F32),
                pltpu.VMEM((HEAD_DIM, SEQ_LEN), BF16),
            ],
        ),
        out_shape=[jax.ShapeDtypeStruct((HEAD_DIM, QUARTER), BF16)] * QUARTERS
        + [jax.ShapeDtypeStruct((1, SEQ_LEN), F32)],
        cost_estimate=pl.CostEstimate(
            flops=18_000_000_000, bytes_accessed=2_200_000, transcendentals=9_000_000
        ),
        name="attend_forward",
    )(info, qkv, qkv, qkv, *after)


def pieces(values):
    high = values.astype(BF16).astype(F32)
    rest = values - high
    middle = rest.astype(BF16).astype(F32)
    return [high, middle, (rest - middle).astype(BF16).astype(F32)]


def backward_kernel(
    skip, info, q_ref, k_ref, v_ref, g_0, g_1, g_2, g_3, o_0, o_1, o_2, o_3, lse_ref, normed_ref, *refs
):
    d_0, d_1, d_2, d_3, weight_ref, sums_ref, *refs = refs[skip:]
    g_ref, q_wide, k_wide, v_wide, g_wide, p_a, ds_a, p_b, ds_b, *refs = refs
    dq, dk, dv, d_ref, normed, arrived = refs
    start, own = info[0], info[1]
    cross, pairs = crossing(start)
    fetch = pltpu.make_async_copy(normed_ref, normed, arrived)
    fetch.start()
    ones = [jnp.ones((1, BLOCK), F32)] * 3

    def widen(columns, rows):
        rest = jnp.concatenate(rows + [jnp.zeros((HEAD_DIM - 3, BLOCK), F32)], axis=0)
        return jnp.concatenate([columns, rest.astype(BF16)], axis=0).T

    for x, (g_part, o_part) in enumerate(zip((g_0, g_1, g_2, g_3), (o_0, o_1, o_2, o_3))):
        g_ref[:, x * QUARTER : (x + 1) * QUARTER] = g_part[...]
        d_ref[0:HEAD_DIM, x * QUARTER : (x + 1) * QUARTER] = o_part[...]

    def prepare(block, carry):
        at = pl.ds(pl.multiple_of(block * BLOCK, BLOCK), BLOCK)
        grad = g_ref[:, at]
        centre = jnp.sum(
            grad.astype(F32) * d_ref[0:HEAD_DIM, at].astype(F32), axis=0, keepdims=True
        )
        q_wide[at, :] = widen(q_ref[:, at], pieces(-lse_ref[:, at]))
        k_wide[at, :] = widen(k_ref[:, at], ones)
        v_wide[at, :] = widen(v_ref[:, at], ones)
        g_wide[at, :] = widen(grad, pieces(-centre))
        return carry

    lax.fori_loop(0, BLOCKS, prepare, 0)
    dq[...] = jnp.zeros_like(dq)
    dk[...] = jnp.zeros_like(dk)
    dv[...] = jnp.zeros_like(dv)

    def score(row, col, p_dst, ds_dst, masked):
        rows = pl.ds(place(jnp.minimum(row, BLOCKS - 1), own), BLOCK)
        cols = pl.ds(place(col, own), BLOCK)
        s = product(q_wide[rows, :], k_wide[cols, :], NT)
        grad_p = product(g_wide[rows, :], v_wide[cols, :], NT)
        if masked:
            pos = row * BLOCK + lax.broadcasted_iota(jnp.int32, (BLOCK, 1), 0)
            limit = last_key(pos, start) - col * BLOCK
            s = jnp.where(lax.broadcasted_iota(jnp.int32, (BLOCK, BLOCK), 1) <= limit, s, -1e30)
        p = jnp.exp2(s)
        p_dst[...] = p.astype(BF16)
        ds_dst[...] = (p * grad_p).astype(BF16)

    def step(p, ds, p_dst, ds_dst, row, col, next_row, next_col, masked):
        score(next_row, next_col, p_dst, ds_dst, masked)
        rows = pl.ds(place(row, own), BLOCK)
        cols = pl.ds(place(col, own), BLOCK)
        dv[:, cols] += product(g_ref[:, rows], p[...], NN)
        dk[:, cols] += product(q_ref[:, rows], ds[...], NN)
        dq[:, rows] += product(k_ref[:, cols], ds[...], NT)

    def half(p, ds, p_dst, ds_dst, row, col, live):
        next_row, next_col = following(row, col, cross)
        masked = next_col >= next_row

        @pl.when(live & masked)
        def _():
            step(p, ds, p_dst, ds_dst, row, col, next_row, next_col, True)

        @pl.when(live & jnp.logical_not(masked))
        def _():
            step(p, ds, p_dst, ds_dst, row, col, next_row, next_col, False)

        return next_row, next_col

    score(0, 0, p_a, ds_a, True)

    def both(turn, carry):
        row, col = half(p_a, ds_a, p_b, ds_b, *carry, turn >= 0)
        return half(p_b, ds_b, p_a, ds_a, row, col, 2 * turn + 1 < pairs)

    lax.fori_loop(0, (pairs + 1) // 2, both, (jnp.int32(0), jnp.int32(0)))

    d_ref[0:64, :] = (dq[...] * 0.125).astype(BF16)
    d_ref[64:128, :] = (dk[...] * (1.0 / LOG2E)).astype(BF16)
    d_ref[128:192, :] = dv[...].astype(BF16)
    for x, part in enumerate((d_0, d_1, d_2, d_3)):
        part[...] = d_ref[:, x * QUARTER : (x + 1) * QUARTER]
    sums_ref[...] = jnp.sum(d_ref[...].astype(F32), axis=1, keepdims=True)
    fetch.wait()
    weight_ref[...] = product(d_ref[...], normed[...], NN).T.astype(BF16)


def attend_backward(info, qkv, grads, grad_row, outs, lse, normed, head, after):
    quarter = [whole(HEAD_DIM, QUARTER)] * QUARTERS
    grad_quarter = [
        pl.BlockSpec(
            (HEAD_DIM, QUARTER), lambda i, info: (grad_row, 0), pipeline_mode=pl.Buffered(1)
        )
    ] * QUARTERS
    rows = 3 * HEAD_DIM
    width = normed.shape[1]
    return pl.pallas_call(
        functools.partial(backward_kernel, len(after)),
        grid_spec=pltpu.PrefetchScalarGridSpec(
            num_scalar_prefetch=1,
            grid=(1,),
            in_specs=[head_spec(head, part) for part in range(3)]
            + grad_quarter
            + quarter
            + [whole(1, SEQ_LEN), ANYWHERE]
            + [ANYWHERE] * len(after),
            out_specs=[whole(rows, QUARTER)] * QUARTERS + [whole(width, rows), whole(rows, 1)],
            scratch_shapes=[pltpu.VMEM((HEAD_DIM, SEQ_LEN), BF16)]
            + [pltpu.VMEM((SEQ_LEN, 128), BF16)] * 4
            + [pltpu.VMEM((BLOCK, BLOCK), BF16)] * 4
            + [pltpu.VMEM((HEAD_DIM, SEQ_LEN), F32)] * 3
            + [
                pltpu.VMEM((rows, SEQ_LEN), BF16),
                pltpu.VMEM(normed.shape, BF16),
                pltpu.SemaphoreType.DMA,
            ],
        ),
        out_shape=[jax.ShapeDtypeStruct((rows, QUARTER), BF16)] * QUARTERS
        + [jax.ShapeDtypeStruct((width, rows), BF16), jax.ShapeDtypeStruct((rows, 1), F32)],
        cost_estimate=pl.CostEstimate(
            flops=32_000_000_000, bytes_accessed=12_000_000, transcendentals=9_000_000
        ),
        name="attend_backward",
    )(info, qkv, qkv, qkv, *grads, *outs, lse, normed, *after)


def normalise(values):
    centred = values - jnp.mean(values, axis=-1, keepdims=True)
    scale = lax.rsqrt(jnp.mean(centred * centred, axis=-1, keepdims=True) + EPSILON)
    return centred * scale, scale


def normalise_back(grad, unit, scale):
    return scale * (
        grad
        - jnp.mean(grad, axis=-1, keepdims=True)
        - unit * jnp.mean(grad * unit, axis=-1, keepdims=True)
    )


def gelu_both(u):
    square = u * u
    weight = 0.7978845608028654 + (0.7978845608028654 * 0.044715) * square
    share = 0.5 + 0.5 * jnp.tanh(u * weight)
    value = u * share
    rise = 6.0 * weight - 4.0 * 0.7978845608028654
    return value, share + value * (1.0 - share) * rise


def swap(values, mask):
    return lax.ppermute(values, "tensor", [(i, i ^ mask) for i in range(QUARTERS)])


def pick_first_kernel(info, qkv_ref, gain_ref, shift_ref, head_ref, hidden_ref, out_ref):
    rows = qkv_ref.shape[2]
    heads = qkv_ref.shape[3] // HEAD_DIM
    base = out_ref.shape[1] - 16
    out_ref[...] = jnp.zeros_like(out_ref)
    for h in range(heads):
        for part in range(3):
            at = (h * 3 + part) * HEAD_DIM
            out_ref[0, 0:rows, at : at + HEAD_DIM] = qkv_ref[
                0, part, :, h * HEAD_DIM : (h + 1) * HEAD_DIM
            ]
    few = head_ref.shape[2]
    hidden = hidden_ref[...].astype(F32)
    mine = lax.broadcasted_iota(jnp.int32, hidden.shape, 0) == info[3]
    hidden = jnp.sum(jnp.where(mine, hidden, 0.0), axis=0, keepdims=True)
    wide = lambda item: jnp.pad(
        item.astype(F32), ((0, 0), (0, out_ref.shape[2] - item.shape[1]))
    )
    out_ref[0, base:, :] = jnp.concatenate(
        [
            wide(gain_ref[0]),
            wide(shift_ref[0]),
            wide(head_ref[0]),
            wide(hidden),
            jnp.zeros((7, out_ref.shape[2]), F32),
        ],
        axis=0,
    ).astype(BF16)


def chosen_block(bank):
    rest = bank.shape[1:]
    return pl.BlockSpec((1, *rest), lambda i, info: (info[3],) + (0,) * len(rest))


def pick_first(info, qkv_bank, gain_bank, shift_bank, head_bank, hidden_bank):
    qkv_bank = qkv_bank.transpose(0, 2, 1, 3)
    rows, columns = qkv_bank.shape[2], 3 * qkv_bank.shape[3]
    shape = (1, -(-rows // 16) * 16 + 16, columns)
    return pl.pallas_call(
        pick_first_kernel,
        grid_spec=pltpu.PrefetchScalarGridSpec(
            num_scalar_prefetch=1,
            grid=(1,),
            in_specs=[
                chosen_block(bank) for bank in (qkv_bank, gain_bank, shift_bank, head_bank)
            ]
            + [whole(*hidden_bank.shape)],
            out_specs=pl.BlockSpec(shape, lambda i, info: (0, 0, 0)),
        ),
        out_shape=jax.ShapeDtypeStruct(shape, BF16),
        cost_estimate=SHORT,
        name="pick_first",
    )(info, qkv_bank, gain_bank, shift_bank, head_bank, hidden_bank)


def pick_rest_kernel(info, up_ref, down_ref, out_ref, qkv_ref, *refs):
    packed_ref = refs[-1]
    rows, first = up_ref.shape[1:]
    second = first + down_ref.shape[2]
    third = second + qkv_ref.shape[2]
    packed_ref[:, :first] = up_ref[0]
    packed_ref[:, first:second] = down_ref[0]
    packed_ref[:, second:third] = qkv_ref[0, :rows]
    packed_ref[:, third:] = out_ref[0].astype(F32).T.astype(BF16)


def pick_rest(info, up_bank, down_bank, out_bank, first, after):
    down_bank = down_bank.transpose(0, 2, 1)
    columns = up_bank.shape[2] + down_bank.shape[2] + out_bank.shape[1] + first.shape[2]
    shape = (up_bank.shape[1], columns)
    return pl.pallas_call(
        pick_rest_kernel,
        grid_spec=pltpu.PrefetchScalarGridSpec(
            num_scalar_prefetch=1,
            grid=(1,),
            in_specs=[chosen_block(bank) for bank in (up_bank, down_bank, out_bank)]
            + [pl.BlockSpec(first.shape, lambda i, info: (0, 0, 0))]
            + [ANYWHERE] * len(after),
            out_specs=whole(*shape),
        ),
        out_shape=jax.ShapeDtypeStruct(shape, BF16),
        cost_estimate=SHORT,
        name="pick_rest",
    )(info, up_bank, down_bank, out_bank, first, *after)


def assemble_kernel(order, info, *refs):
    parts, refs = refs[:-6], refs[-6:]
    turned_ref, vec_ref, bias_ref, own_ref, rows_ref, small_ref = refs
    count = len(order)
    held = [(part, n) for part in parts for n in range(part.shape[0])]
    rows = turned_ref.shape[1] // count
    for (part, n), k in zip(held, order):
        owner = jnp.bitwise_xor(info[2], k)
        at = pl.ds(pl.multiple_of(owner * rows, rows), rows)
        rows_ref[at, :] = part[n, :rows]
        small_ref[at, :] = part[n, rows:, 0:128].astype(F32).T[:rows]
    own_ref[...] = parts[0][0, :rows]
    turned_ref[...] = rows_ref[...].T
    small = small_ref[...]
    wide = jnp.concatenate([small, jnp.zeros((small.shape[0], 112), F32)], axis=1)
    vec_ref[...] = wide.T[0:16]
    heads = turned_ref.shape[0] // (3 * HEAD_DIM)
    few = heads * HEAD_DIM // count
    column = lambda n: jnp.concatenate(
        [small[p * rows : p * rows + few, n : n + 1] for p in range(count)], axis=0
    )
    q_bias, v_bias = column(6), column(7)
    for h in range(heads):
        at = h * 3 * HEAD_DIM
        bias_ref[at : at + HEAD_DIM, :] = q_bias[h * HEAD_DIM : (h + 1) * HEAD_DIM]
        bias_ref[at + HEAD_DIM : at + 2 * HEAD_DIM, :] = jnp.zeros((HEAD_DIM, 1), F32)
        bias_ref[at + 2 * HEAD_DIM : at + 3 * HEAD_DIM, :] = v_bias[h * HEAD_DIM : (h + 1) * HEAD_DIM]


def gather_qkv(info, part, count, rows):
    _, depth, columns = part.shape
    heads = columns // (3 * HEAD_DIM)
    few = heads * HEAD_DIM // count
    if count != 8 or rows % 16 or few % 8:
        parts = lax.all_gather(part[0], "dp", axis=0, tiled=False)
        turned = parts[:, :rows].reshape(count * rows, columns).T
        small = parts[:, depth - 16 :].astype(F32).transpose(1, 0, 2)
        vectors = small[:, :, :rows].reshape(16, count * rows)
        bias = small[6:8, :, :few].reshape(2, heads, HEAD_DIM)
        bias = jnp.stack([bias[0], jnp.zeros_like(bias[0]), bias[1]], axis=1)
        return turned, vectors, bias.reshape(columns, 1), part[0, :rows], part, part
    joined, order, others = part, [0], []
    for mask in (4, 2, 1):
        other = lax.ppermute(joined, "dp", [(i, i ^ mask) for i in range(count)])
        others.append(other)
        if mask > 1:
            joined = jnp.concatenate([joined, other])
        order = order + [k ^ mask for k in order]
    fixed = lambda *shape: pl.BlockSpec(shape, lambda i, info: (0,) * len(shape))
    outs = [
        ((columns, count * rows), BF16),
        ((16, count * rows), F32),
        ((columns, 1), F32),
        ((rows, columns), BF16),
    ]
    found = pl.pallas_call(
        functools.partial(assemble_kernel, order),
        grid_spec=pltpu.PrefetchScalarGridSpec(
            num_scalar_prefetch=1,
            grid=(1,),
            in_specs=[fixed(*item.shape) for item in (part, *others)],
            out_specs=[fixed(*shape) for shape, _ in outs],
            scratch_shapes=[
                pltpu.VMEM((count * rows, columns), BF16),
                pltpu.VMEM((count * rows, 16), F32),
            ],
        ),
        out_shape=[jax.ShapeDtypeStruct(shape, kind) for shape, kind in outs],
        cost_estimate=SHORT,
        name="assemble",
    )(info, part, *others)
    return *found, others[0], others[2]


def enter_kernel(spans, w_ref, vec_ref, bias_ref, *refs):
    parts, (qkv_ref, normed_ref, hidden_ref, held) = refs[:-4], refs[-4:]
    for part, (first, last, at) in zip(parts, spans):

        @pl.when((pl.program_id(0) >= first) & (pl.program_id(0) < last))
        def _():
            held[at : at + part.shape[0], :] = part[...]

    row = lax.broadcasted_iota(jnp.int32, (w_ref.shape[0], 1), 0)
    scale = jnp.where(lax.rem(row, 3 * HEAD_DIM) < HEAD_DIM, LOG2E / 8.0, 1.0)
    unit, _ = normalise(held[...].astype(F32))
    rounded = (unit * vec_ref[0:1] + vec_ref[2:3]).astype(BF16)
    normed_ref[...] = rounded
    flat = product(w_ref[...], rounded, NT)
    qkv_ref[...] = ((flat + bias_ref[...]) * scale).astype(BF16)
    hidden_ref[...] = vec_ref[8:9]


def enter(parts, turned, vectors, bias):
    block = BLOCK
    width = parts[0].shape[1]
    columns = turned.shape[0]
    fixed = lambda shape: pl.BlockSpec(shape, lambda i: (0, 0), pipeline_mode=pl.Buffered(1))
    spans, specs, row = [], [], 0
    for part in parts:
        size = min(part.shape[0], block)
        first, blocks = row // block, part.shape[0] // size
        spans.append((first, first + blocks, row % block))
        specs.append(
            pl.BlockSpec(
                (size, width), lambda i, first=first, n=blocks: (jnp.clip(i - first, 0, n - 1), 0)
            )
        )
        row += part.shape[0]
    first = row // block
    return pl.pallas_call(
        functools.partial(enter_kernel, spans),
        grid=(first,),
        in_specs=[fixed(turned.shape), fixed(vectors.shape), fixed(bias.shape)] + specs,
        out_specs=[
            pl.BlockSpec((columns, block), lambda i: (0, i)),
            pl.BlockSpec((block, width), lambda i: (i, 0)),
            fixed((1, width)),
        ],
        out_shape=[
            jax.ShapeDtypeStruct((columns, first * block), BF16),
            jax.ShapeDtypeStruct((first * block, width), BF16),
            jax.ShapeDtypeStruct((1, width), F32),
        ],
        scratch_shapes=[pltpu.VMEM((block, width), BF16)],
        cost_estimate=SHORT,
        name="enter",
    )(turned, vectors, bias, *parts)


TILE = 256
TALL = 512


def stored_blocks(width):
    return [
        pl.BlockSpec(
            (width, width),
            lambda i, info, x=x: (jnp.bitwise_xor(info[1], x), 2),
            pipeline_mode=pl.Buffered(1),
        )
        for x in range(QUARTERS)
    ]


def middle_kernel(parts, info, tokens_ref, cot_ref, vec_ref, up_ref, down_ref, *refs):
    stored, hidden, refs = refs[:4], refs[4:8], refs[8:]
    given, refs = refs[:parts], refs[parts:]
    (result_ref, grads_out, grad_ref, stats_ref), refs = refs[:4], refs[4:]
    back, refs = refs[: 2 * QUARTERS], refs[2 * QUARTERS :]
    mixed, middle, low, low_t, cot_t, activ, grad_u, branch, grad_two, *bufs = refs
    *bufs, grads_ref, out_ref, bias_ref, sent = bufs
    k = pl.program_id(0)
    count, width = tokens_ref.shape
    tiles = count // TALL
    local_width = width // QUARTERS
    spans = [slice(m * TALL, (m + 1) * TALL) for m in range(tiles)]

    def tiled(body):
        def at_tile(m, carry):
            return body(pl.ds(pl.multiple_of(m * TALL, TALL), TALL), carry)

        return at_tile

    @pl.when(k == 0)
    def _():
        for n, part in enumerate(given):
            mixed[n * HEAD_DIM : (n + 1) * HEAD_DIM, :] = part[...]
        low_t[width:, :] = jnp.ones((16, count), BF16)
        for x in range(QUARTERS):
            out_ref[:, x * local_width : (x + 1) * local_width] = stored[x][:, width - local_width :]
            bias_ref[x : x + 1, :] = hidden[x][...]

        @tiled
        def begin(at, carry):
            attended = product(mixed[:, at], out_ref[...], CT)
            value = tokens_ref[at, :].astype(F32) + attended + vec_ref[4:5]
            middle[at, :] = value
            unit, _ = normalise(value)
            rounded = (unit * vec_ref[1:2] + vec_ref[3:4]).astype(BF16)
            low[at, :] = rounded
            low_t[0:width, at] = rounded.T
            cot_t[:, at] = cot_ref[at, :].T
            branch[at, :] = jnp.zeros((TALL, width), F32)
            grad_two[at, :] = jnp.zeros((TALL, width), F32)
            return carry

        lax.fori_loop(0, tiles, begin, 0)

    bias = bias_ref[pl.ds(jnp.bitwise_xor(k, info[1]), 1), :]

    def first(m, u, g):
        u[...] = product(low[spans[m], :], up_ref[...], NN) + bias
        g[...] = product(cot_ref[spans[m], :], down_ref[...], NN)

    def second(m, u, g):
        value, slope = gelu_both(u[...])
        a = value.astype(BF16)
        gu = (g[...] * slope).astype(BF16)
        activ[spans[m], :] = a
        grad_u[spans[m], :] = gu
        branch[spans[m], :] += product(a, down_ref[...], NT)
        grad_two[spans[m], :] += product(gu, up_ref[...], NT)

    turns = (bufs[:2], bufs[2:])
    first(0, *turns[0])
    for m in range(tiles):
        if m + 1 < tiles:
            first(m + 1, *turns[(m + 1) % 2])
        second(m, *turns[m % 2])
    rows = pl.ds(pl.multiple_of(k * width, width), width)

    grad_up = product(low_t[...], grad_u[...], NN)
    grads_ref[rows, 0:width] = grad_up[:width].astype(BF16)
    stats_ref[pl.ds(4 + k, 1), :] = grad_up[width : width + 1]
    grads_ref[rows, width : 2 * width] = product(cot_t[...], activ[...], NN).astype(BF16)

    def leaving(n, columns):
        part = pl.ds(n * width, width)
        return pltpu.make_async_copy(
            grads_ref.at[part, columns], grads_out.at[part, columns], sent.at[n, columns.start // width // 2]
        )

    wide, narrow = slice(0, 2 * width), slice(2 * width, 2 * width + local_width)
    for n in range(QUARTERS):

        @pl.when(k == n)
        def _():
            leaving(n, wide).start()

    @pl.when(k == pl.num_programs(0) - 1)
    def _():
        @tiled
        def end(at, sums):
            value = middle[at, :]
            result_ref[at, :] = (value + branch[at, :] + vec_ref[5:6]).astype(BF16)
            unit, scale = normalise(value)
            grad = grad_two[at, :]
            cot = cot_ref[at, :].astype(F32)
            total = cot + normalise_back(grad * vec_ref[1:2], unit, scale)
            grad_ref[at, :] = total
            e = total.astype(BF16)
            low[at, :] = e
            mixed_grad = product(out_ref[...], e, CT).astype(BF16)
            for n, part in enumerate(back):
                row = n // 2 * local_width + n % 2 * HEAD_DIM
                part[:, at] = mixed_grad[row : row + part.shape[0]]
            items = (grad * unit, grad, e.astype(F32), cot)
            return tuple(
                old + jnp.sum(item, axis=0, keepdims=True) for old, item in zip(sums, items)
            )

        sums = lax.fori_loop(0, tiles, end, (jnp.zeros((1, width), F32),) * 4)
        for n in range(4):
            stats_ref[n : n + 1, :] = sums[n]
        grad_out = product(low[...], mixed[...], CT).astype(BF16)
        for x in range(QUARTERS):
            owner = jnp.bitwise_xor(info[1], x)
            grads_ref[pl.ds(pl.multiple_of(owner * width, width), width), 2 * width :] = grad_out[
                :, x * local_width : (x + 1) * local_width
            ]
        for n in range(QUARTERS):
            leaving(n, narrow).start()
        for n in range(QUARTERS):
            leaving(n, wide).wait()
            leaving(n, narrow).wait()


def middle_part(info, tokens, cotangent, vectors, hidden, bank, mixed):
    count, width = tokens.shape
    local_width = width // QUARTERS
    outs = [
        ((count, width), BF16),
        ((QUARTERS * width, 2 * width + local_width), BF16),
        ((count, width), F32),
        ((8, width), F32),
    ] + [((HEAD_DIM, count), BF16), ((local_width - HEAD_DIM, count), BF16)] * QUARTERS
    return pl.pallas_call(
        functools.partial(middle_kernel, len(mixed)),
        grid_spec=pltpu.PrefetchScalarGridSpec(
            num_scalar_prefetch=1,
            grid=(QUARTERS,),
            in_specs=[
                whole(count, width),
                whole(count, width),
                whole(16, width),
                pl.BlockSpec((width, width), lambda k, info: (k, 0)),
                pl.BlockSpec((width, width), lambda k, info: (k, 1)),
            ]
            + stored_blocks(width)
            + [whole(1, width)] * QUARTERS
            + [whole(HEAD_DIM, count)] * len(mixed),
            out_specs=[whole(*outs[0][0]), ANYWHERE] + [whole(*shape) for shape, _ in outs[2:]],
            scratch_shapes=[
                pltpu.VMEM((width, count), BF16),
                pltpu.VMEM((count, width), F32),
                pltpu.VMEM((count, width), BF16),
                pltpu.VMEM((width + 16, count), BF16),
                pltpu.VMEM((width, count), BF16),
                pltpu.VMEM((count, width), BF16),
                pltpu.VMEM((count, width), BF16),
                pltpu.VMEM((count, width), F32),
                pltpu.VMEM((count, width), F32),
            ]
            + [pltpu.VMEM((TALL, width), F32)] * 4
            + [
                pltpu.VMEM(outs[1][0], BF16),
                pltpu.VMEM((width, width), BF16),
                pltpu.VMEM((8, width), F32),
                pltpu.SemaphoreType.DMA((QUARTERS, 2)),
            ],
        ),
        out_shape=[jax.ShapeDtypeStruct(shape, kind) for shape, kind in outs],
        compiler_params=pltpu.CompilerParams(vmem_limit_bytes=66_000_000),
        cost_estimate=pl.CostEstimate(
            flops=40_000_000_000, bytes_accessed=40_000_000, transcendentals=3_200_000
        ),
        name="middle",
    )(info, tokens, cotangent, vectors, bank, bank, *[bank] * QUARTERS, *hidden, *mixed)


def add_back(grad, tokens_ref, vec_ref, grad_ref):
    unit, scale = normalise(tokens_ref[...].astype(F32))
    return grad_ref[...] + normalise_back(grad * vec_ref[0:1], unit, scale)


def exit_first_kernel(heads, info, *refs):
    count = heads * QUARTERS
    deltas, weights, refs = refs[:count], refs[count : count + 4], refs[count + 4 :]
    tokens_ref, grad_ref, vec_ref, sum_ref, rest_ref, d_all, w_all = refs
    span = deltas[0].shape[0]

    @pl.when(pl.program_id(0) == 0)
    def _():
        for x in range(QUARTERS):
            at = x * heads * span
            w_all[:, at : at + heads * span] = weights[x][:, : heads * span]
            rest_ref[:, x * span : (x + 1) * span] = weights[x][
                :, heads * span : (heads + 1) * span
            ]

    for x in range(QUARTERS):
        for h in range(heads):
            at = (x * heads + h) * span
            d_all[at : at + span, :] = deltas[h * QUARTERS + x][...]
    sum_ref[...] = add_back(product(w_all[...], d_all[...], NN).T, tokens_ref, vec_ref, grad_ref)


def exit_last_kernel(skip, info, *refs):
    deltas, refs = refs[:4], refs[4:]
    w_ref, tokens_ref, grad_ref, vec_ref, *refs = refs
    out_ref, d_all = refs[skip:]
    span = deltas[0].shape[0]
    for x in range(QUARTERS):
        d_all[x * span : (x + 1) * span, :] = deltas[x][...]
    grad = product(w_ref[...], d_all[...], NN).T
    out_ref[...] = add_back(grad, tokens_ref, vec_ref, grad_ref).astype(BF16)


def lanes(rows):
    return pl.BlockSpec((rows, TILE), lambda i, info: (0, i))


def lines(columns):
    return pl.BlockSpec((TILE, columns), lambda i, info: (i, 0))


def exit_first(info, deltas, bank, tokens, grad, vectors):
    count, width = tokens.shape
    span = deltas[0].shape[0]
    heads = len(deltas) // QUARTERS
    depth = len(deltas) * span
    return pl.pallas_call(
        functools.partial(exit_first_kernel, heads),
        grid_spec=pltpu.PrefetchScalarGridSpec(
            num_scalar_prefetch=1,
            grid=(count // TILE,),
            in_specs=[lanes(span)] * len(deltas)
            + stored_blocks(width)
            + [lines(width), lines(width), whole(*vectors.shape)],
            out_specs=[lines(width), whole(width, QUARTERS * span)],
            scratch_shapes=[pltpu.VMEM((depth, TILE), BF16), pltpu.VMEM((width, depth), BF16)],
        ),
        out_shape=[
            jax.ShapeDtypeStruct((count, width), F32),
            jax.ShapeDtypeStruct((width, QUARTERS * span), BF16),
        ],
        cost_estimate=SHORT,
        name="exit_first",
    )(info, *deltas, *[bank] * QUARTERS, tokens, grad, vectors)


def exit_last(info, deltas, weights, tokens, grad, vectors, after):
    count, width = tokens.shape
    span = deltas[0].shape[0]
    return pl.pallas_call(
        functools.partial(exit_last_kernel, len(after)),
        grid_spec=pltpu.PrefetchScalarGridSpec(
            num_scalar_prefetch=1,
            grid=(count // TILE,),
            in_specs=[lanes(span)] * QUARTERS
            + [whole(*weights.shape), lines(width), lines(width), whole(*vectors.shape)]
            + [ANYWHERE] * len(after),
            out_specs=lines(width),
            scratch_shapes=[pltpu.VMEM((QUARTERS * span, TILE), BF16)],
        ),
        out_shape=jax.ShapeDtypeStruct((count, width), BF16),
        cost_estimate=SHORT,
        name="exit_last",
    )(info, *deltas, weights, tokens, grad, vectors, *after)


def pack_first_kernel(rows, weights, stats_ref, out_ref):
    span = weights[0].shape[1]
    count, depth, columns = out_ref.shape
    stats = jnp.concatenate(pieces(stats_ref[...]), axis=0)
    for p in range(count):
        for h, weight in enumerate(weights):
            out_ref[p, 0:rows, h * span : (h + 1) * span] = weight[p * rows : (p + 1) * rows]
        part = jnp.concatenate(
            [stats[:, p * rows : (p + 1) * rows], jnp.zeros((24, columns - rows), F32)], axis=1
        )
        part = jnp.concatenate([part, jnp.zeros((8, columns), F32)], axis=0)
        out_ref[p, depth - 32 :, :] = part.astype(BF16)


def pack_last_kernel(rows, weight, sums, out_ref):
    span = weight.shape[1]
    count, depth, columns = out_ref.shape
    lined = [jnp.broadcast_to(item[...], (span, 128)).T[0:1] for item in sums]
    lined = [piece for item in lined for piece in pieces(item)]
    lined = jnp.concatenate(lined + [jnp.zeros((16 - len(lined), span), F32)], axis=0)
    lined = jnp.concatenate([lined, jnp.zeros((16, columns - span), F32)], axis=1).astype(BF16)
    out_ref[...] = jnp.zeros_like(out_ref)
    for p in range(count):
        out_ref[p, 0:rows, 0:span] = weight[p * rows : (p + 1) * rows]
        out_ref[p, depth - 16 :, :] = lined


def exchange(kernel, count, items, below, columns, after, name):
    width = items[0].shape[0]
    rows = width // count
    fixed = lambda shape: pl.BlockSpec(shape, lambda i: (0,) * len(shape))
    shape = (count, -(-rows // 16) * 16 + below, columns)

    def body(*refs):
        kernel(rows, refs[: len(items)], refs[-1])

    packed = pl.pallas_call(
        body,
        grid=(1,),
        in_specs=[fixed(item.shape) for item in items] + [ANYWHERE] * len(after),
        out_specs=fixed(shape),
        out_shape=jax.ShapeDtypeStruct(shape, BF16),
        cost_estimate=SHORT,
        name=name,
    )(*items, *after)
    received = lax.all_to_all(
        packed.reshape(-1, columns), "dp", split_axis=0, concat_axis=0, tiled=True
    )
    return received.reshape(shape)


def exchange_first(weights, stats, count):
    kernel = lambda rows, refs, out: pack_first_kernel(rows, refs[:-1], refs[-1], out)
    columns = sum(weight.shape[1] for weight in weights)
    return exchange(kernel, count, [*weights, stats], 32, columns, [], "pack_first")


def exchange_last(weight, sums, count, after):
    kernel = lambda rows, refs, out: pack_last_kernel(rows, refs[0], refs[1:], out)
    return exchange(kernel, count, [weight, *sums], 16, 256, after, "pack_last")


def finish_kernel(heads, early_ref, late_ref, weight_ref, small_ref, total_ref, stats_ref, sums_ref):
    rows, columns = weight_ref.shape
    span = columns // heads
    early, late = early_ref[0].astype(F32), late_ref[0].astype(F32)
    for p in range(1, early_ref.shape[0]):
        early = early + early_ref[p].astype(F32)
        late = late + late_ref[p].astype(F32)
    grads = jnp.concatenate([early[:rows], late[:rows, :span]], axis=1)
    base = early.shape[0] - 32
    stats = early[base : base + 8] + early[base + 8 : base + 16] + early[base + 16 : base + 24]
    lined = late[late.shape[0] - 16 :, :span]
    sums = jnp.concatenate(
        [lined[3 * h : 3 * h + 1] + lined[3 * h + 1 : 3 * h + 2] + lined[3 * h + 2 : 3 * h + 3]
         for h in range(heads)],
        axis=1,
    )
    weights = weight_ref[...].astype(F32)
    shift = jnp.sum(weights * sums, axis=1, keepdims=True)
    gain = jnp.sum(weights * grads, axis=1, keepdims=True)
    gain = (gain - small_ref[:, 1:2] * shift) / small_ref[:, 0:1]
    sums_ref[...] = sums
    for n in range(columns // HEAD_DIM):
        at = n // 3 * HEAD_DIM
        total_ref[n % 3, :, at : at + HEAD_DIM] = grads[:, n * HEAD_DIM : (n + 1) * HEAD_DIM]
    turned = jnp.concatenate([shift, gain, jnp.zeros((rows, 6), F32)], axis=1).T
    stats_ref[...] = jnp.concatenate([stats[:, :rows], turned], axis=0)


def finish(early, late, weights, small):
    rows, columns = weights.shape
    heads = columns // (3 * HEAD_DIM)
    fixed = lambda shape: pl.BlockSpec(shape, lambda i: (0,) * len(shape))
    outs = [(3, rows, columns // 3), (16, rows), (1, columns)]
    return pl.pallas_call(
        functools.partial(finish_kernel, heads),
        grid=(1,),
        in_specs=[fixed(item.shape) for item in (early, late, weights, small)],
        out_specs=[fixed(shape) for shape in outs],
        out_shape=[jax.ShapeDtypeStruct(shape, F32) for shape in outs],
        cost_estimate=SHORT,
        name="finish",
    )(early, late, weights, small)


def unpack_kernel(info, shard_ref, a_ref, b_ref, c_ref, d_ref, *refs):
    up_ref, down_ref, out_ref, gain_ref, shift_ref, hidden_ref, sum_ref = refs
    first, second = up_ref.shape[1], up_ref.shape[1] + down_ref.shape[1]
    up_ref[...] = shard_ref[:, :first].astype(F32)
    down_ref[...] = shard_ref[:, first:second].astype(F32)
    out_ref[...] = shard_ref[:, second:].astype(F32).T
    total = (a_ref[...] + b_ref[...]) + (c_ref[...] + d_ref[...])
    sum_ref[...] = total
    gain_ref[...] = jnp.concatenate([total[9:10], total[0:1]], axis=0)
    shift_ref[...] = jnp.concatenate([total[8:9], total[1:4]], axis=0)
    hidden_ref[...] = sum_ref[pl.ds(4 + info[1], 1), :]


def unpack(info, shard, stats, first, second):
    rows, columns = shard.shape
    outs = [(rows, first), (rows, second - first), (columns - second, rows), (2, rows), (4, rows), (1, rows)]
    fixed = lambda shape: pl.BlockSpec(shape, lambda i, info: (0, 0))
    return pl.pallas_call(
        unpack_kernel,
        grid_spec=pltpu.PrefetchScalarGridSpec(
            num_scalar_prefetch=1,
            grid=(1,),
            in_specs=[fixed(item.shape) for item in (shard, *stats)],
            out_specs=[fixed(shape) for shape in outs],
            scratch_shapes=[pltpu.VMEM(stats[0].shape, F32)],
        ),
        out_shape=[jax.ShapeDtypeStruct(shape, F32) for shape in outs],
        cost_estimate=SHORT,
        name="unpack",
    )(info, shard, *stats)


def local(
    n_dp,
    tokens,
    cotangent,
    tie_index,
    image_start,
    qkv_bank,
    out_bank,
    up_bank,
    down_bank,
    gain_bank,
    shift_bank,
    head_bias_bank,
    hidden_bias_bank,
):
    own = lax.axis_index("tensor")
    own_dp = lax.axis_index("dp")
    width = tokens.shape[1]
    rows = qkv_bank.shape[1]
    local_width = qkv_bank.shape[3]
    hidden_cols = up_bank.shape[2]
    heads = local_width // HEAD_DIM
    qkv_cols = 3 * local_width
    few = head_bias_bank.shape[2]
    info = jnp.stack([image_start[0], own, own_dp, tie_index[0]]).astype(jnp.int32)

    cuts = (0, QUARTER // 4, QUARTER // 2, QUARTER)
    far = [swap(tokens[low:high], 2) for low, high in zip(cuts, cuts[1:])]
    near = swap(tokens, 1)

    packed = pick_first(info, qkv_bank, gain_bank, shift_bank, head_bias_bank, hidden_bias_bank)
    turned, vectors, bias, qkv_part, started, ended = gather_qkv(info, packed, n_dp, rows)
    far[2:] = gate([far[2]], [ended])
    far_near = [swap(part, 1) for part in far]
    own_small = packed[0, -16:].astype(F32)
    bank_part = pick_rest(info, up_bank, down_bank, out_bank, packed, [started, far[0]])
    bank = lax.all_gather(bank_part, ("tensor", "dp"), axis=0, tiled=True)
    c_out = 2 * hidden_cols

    qkv, normed, hidden_bias = enter([tokens, near] + far + far_near, turned, vectors, bias)
    hidden = [hidden_bias] + [swap(hidden_bias, x) for x in range(1, QUARTERS)]

    outs, lses, mixed = [], [], [[None] * heads for _ in range(QUARTERS)]
    for head in range(heads):
        after = [mixed[x][head - 2] for x in range(1, QUARTERS)] if head > 1 else []
        *out, lse = attend_forward(info, qkv, head, after)
        if head == heads - 1:
            out = gate(out, [mixed[x][head - 1] for x in range(1, QUARTERS)])
        outs.append(out)
        lses.append(lse)
        for x in range(QUARTERS):
            mixed[x][head] = swap(out[x], x) if x else out[x]

    result, grads, grad_middle, stats, *mixed_grads = middle_part(
        info, tokens, cotangent, vectors, hidden, bank, [part for quarter in mixed for part in quarter]
    )
    shard = lax.psum_scatter(grads, ("tensor", "dp"), scatter_dimension=0, tiled=True)

    deltas, weight_grads, sums = [], [], []
    grads_first = [swap(mixed_grads[2 * x], x) if x else mixed_grads[0] for x in range(QUARTERS)]
    rest = gate([mixed_grads[2 * x + 1] for x in range(QUARTERS)], grads_first[1:])
    grads_rest = [swap(rest[x], x) if x else rest[0] for x in range(QUARTERS)]
    for head in range(heads):
        *parts, weight_grad, summed = attend_backward(
            info,
            qkv,
            grads_rest if head else grads_first,
            max(head - 1, 0),
            outs[head],
            lses[head],
            normed,
            head,
            [rest[0]] if head == 0 else deltas[head - 2][1:] if head > 1 else [],
        )
        deltas.append([swap(parts[x], x) if x else parts[x] for x in range(QUARTERS)])
        weight_grads.append(weight_grad)
        sums.append(summed)
        if head == heads - 2:
            early_sums = exchange_first(weight_grads, stats, n_dp)
    early = [part for parts in deltas[:-1] for part in parts]

    late_sums = exchange_last(weight_grads[-1], sums, n_dp, [*deltas[-2][1:], early_sums])
    small = jnp.stack([own_small[0, :rows], own_small[2, :rows]], axis=1)
    qkv_total, stats, sums = finish(early_sums, late_sums, qkv_part, small)
    found = [stats] + [swap(stats, x) for x in range(1, QUARTERS)]

    by_part = sums.reshape(heads, 3, HEAD_DIM)
    head_sums = jnp.stack([by_part[:, 0].reshape(-1), by_part[:, 2].reshape(-1)])
    head_shard = lax.dynamic_slice_in_dim(head_sums, own_dp * few, few, 1)

    grad_part, weights = exit_first(info, early, bank, tokens, grad_middle, vectors)
    grad_tokens = exit_last(info, deltas[-1], weights, tokens, grad_part, vectors, [found[0]])
    up_shard, down_shard, out_shard, gain_grads, shift_grads, hidden_shard = unpack(
        info, shard, found, hidden_cols, c_out
    )

    return (
        result,
        grad_tokens,
        qkv_total.transpose(1, 0, 2),
        out_shard,
        up_shard,
        down_shard.T,
        gain_grads,
        shift_grads,
        head_shard,
        hidden_shard.reshape(rows),
    )


def solution(mesh):
    placed = (
        P(("dp", "tensor"), None),
        P(("dp", "tensor"), None),
        P(),
        P("dp"),
        P(None, "dp", None, "tensor"),
        P(None, "tensor", "dp"),
        P(None, "dp", "tensor"),
        P(None, "tensor", "dp"),
        P(None, None, "dp"),
        P(None, None, "dp"),
        P(None, None, ("tensor", "dp")),
        P(None, ("tensor", "dp")),
    )
    return jax.shard_map(
        functools.partial(local, mesh.shape["dp"]),
        mesh=mesh,
        in_specs=placed,
        out_specs=(
            P(("dp", "tensor"), None),
            P(("dp", "tensor"), None),
            P("dp", None, "tensor"),
            P("tensor", "dp"),
            P("dp", "tensor"),
            P("tensor", "dp"),
            P(None, "dp"),
            P(None, "dp"),
            P(None, ("tensor", "dp")),
            P(("tensor", "dp")),
        ),
        check_vma=False,
    )
```

```python
import functools
import math

import jax
import jax.numpy as jnp
from jax import lax
from jax.experimental import pallas as pl
from jax.experimental.pallas import tpu as pltpu
from jax.sharding import PartitionSpec as P

HEAD_DIM = 64
SEQ_LEN = 4096
IMG = 256
EPSILON = 1e-05
LOG2E = 1.4426950408889634
BLOCK = 512
BLOCKS = SEQ_LEN // BLOCK
QUARTERS = 4
QUARTER = SEQ_LEN // QUARTERS
PER_QUARTER = QUARTER // BLOCK
PAIRS = BLOCKS * (BLOCKS + 1) // 2
F32 = jnp.float32
BF16 = jnp.bfloat16

NT = (((1,), (1,)), ((), ()))
NN = (((1,), (0,)), ((), ()))
TN = (((0,), (0,)), ((), ()))
CT = (((0,), (1,)), ((), ()))


def product(left, right, dims):
    return lax.dot_general(left, right, dims, preferred_element_type=F32)


def place(block, own):
    quarter = jnp.bitwise_xor(block // PER_QUARTER, own)
    return pl.multiple_of((quarter * PER_QUARTER + block % PER_QUARTER) * BLOCK, BLOCK)


def following(row, col, cross):
    wrap = col + 1 >= row + 1 + jnp.where(cross == row, 1, 0)
    return jnp.where(wrap, row + 1, row), jnp.where(wrap, 0, col + 1)


def crossing(start):
    low, high = start // BLOCK, (start + IMG - 1) // BLOCK
    cross = jnp.where(high > low, low, -1)
    return cross, PAIRS + jnp.where(cross >= 0, 1, 0)


def last_key(pos, start):
    return jnp.where((pos >= start) & (pos < start + IMG), start + (IMG - 1), pos)


def forward_kernel(
    skip, info, q_ref, k_ref, v_ref, *refs
):
    o_0, o_1, o_2, o_3, lse_ref, k_rows, v_ones, s_a, s_b, top_a, top_b, top, total, o_all = refs[skip:]
    start, own = info[0], info[1]
    cross, pairs = crossing(start)

    def prepare(block, carry):
        at = pl.ds(pl.multiple_of(block * BLOCK, BLOCK), BLOCK)
        k_rows[at, :] = k_ref[:, at].T
        return carry

    lax.fori_loop(0, BLOCKS, prepare, 0)
    v_ones[0:64, :] = v_ref[...]
    v_ones[64:80, :] = jnp.ones((16, SEQ_LEN), BF16)
    total[...] = jnp.zeros_like(total)

    def score(row, col, dst, dst_top, masked):
        rows = pl.ds(place(jnp.minimum(row, BLOCKS - 1), own), BLOCK)
        s = product(k_rows[pl.ds(place(col, own), BLOCK), :], q_ref[:, rows], NN)
        if masked:
            pos = row * BLOCK + lax.broadcasted_iota(jnp.int32, (1, BLOCK), 1)
            limit = last_key(pos, start) - col * BLOCK
            s = jnp.where(lax.broadcasted_iota(jnp.int32, (BLOCK, BLOCK), 0) <= limit, s, -1e30)
        dst[...] = s
        dst_top[...] = jnp.max(s, axis=0, keepdims=True)

    def step(src, src_top, dst, dst_top, col, next_row, next_col, masked):
        score(next_row, next_col, dst, dst_top, masked)
        old = jnp.where(col == 0, -1e30, top[...])
        new = jnp.maximum(old, src_top[...])
        p = jnp.exp2(src[...] - new).astype(BF16)
        mixed = product(v_ones[:, pl.ds(place(col, own), BLOCK)], p, NN)
        total[...] = total[...] * jnp.exp2(old - new) + mixed
        top[...] = new

    def half(src, src_top, dst, dst_top, row, col, live):
        next_row, next_col = following(row, col, cross)
        masked = next_col >= next_row

        @pl.when(live & masked)
        def _():
            step(src, src_top, dst, dst_top, col, next_row, next_col, True)

        @pl.when(live & jnp.logical_not(masked))
        def _():
            step(src, src_top, dst, dst_top, col, next_row, next_col, False)

        @pl.when(live & (next_col == 0))
        def _():
            at = pl.ds(place(row, own), BLOCK)
            summed = total[64:65]
            o_all[:, at] = (total[0:64] / summed).astype(BF16)
            lse_ref[:, at] = top[...] + jnp.log2(summed)

        return next_row, next_col

    score(0, 0, s_a, top_a, True)

    def both(turn, carry):
        row, col = half(s_a, top_a, s_b, top_b, *carry, turn >= 0)
        return half(s_b, top_b, s_a, top_a, row, col, 2 * turn + 1 < pairs)

    lax.fori_loop(0, (pairs + 1) // 2, both, (jnp.int32(0), jnp.int32(0)))

    for x, o_ref in enumerate((o_0, o_1, o_2, o_3)):
        o_ref[...] = o_all[:, x * QUARTER : (x + 1) * QUARTER]


def gate(items, after):
    def kernel(*refs):
        pass

    return pl.pallas_call(
        kernel,
        in_specs=[ANYWHERE] * (len(items) + len(after)),
        out_specs=[ANYWHERE] * len(items),
        out_shape=[jax.ShapeDtypeStruct(item.shape, item.dtype) for item in items],
        input_output_aliases={n: n for n in range(len(items))},
        cost_estimate=SHORT,
        name="gate",
    )(*items, *after)


def head_spec(head, part):
    return pl.BlockSpec((HEAD_DIM, SEQ_LEN), lambda i, info: (head * 3 + part, 0))


def whole(*shape):
    return pl.BlockSpec(shape, lambda i, info: (0, 0), pipeline_mode=pl.Buffered(1))


ANYWHERE = pl.BlockSpec(memory_space=pl.ANY)
SHORT = pl.CostEstimate(flops=1, bytes_accessed=1, transcendentals=0)


def attend_forward(info, qkv, head, after):
    return pl.pallas_call(
        functools.partial(forward_kernel, len(after)),
        grid_spec=pltpu.PrefetchScalarGridSpec(
            num_scalar_prefetch=1,
            grid=(1,),
            in_specs=[head_spec(head, part) for part in range(3)] + [ANYWHERE] * len(after),
            out_specs=[whole(HEAD_DIM, QUARTER)] * QUARTERS + [whole(1, SEQ_LEN)],
            scratch_shapes=[
                pltpu.VMEM((SEQ_LEN, HEAD_DIM), BF16),
                pltpu.VMEM((80, SEQ_LEN), BF16),
                pltpu.VMEM((BLOCK, BLOCK), F32),
                pltpu.VMEM((BLOCK, BLOCK), F32),
                pltpu.VMEM((1, BLOCK), F32),
                pltpu.VMEM((1, BLOCK), F32),
                pltpu.VMEM((1, BLOCK), F32),
                pltpu.VMEM((80, BLOCK), F32),
                pltpu.VMEM((HEAD_DIM, SEQ_LEN), BF16),
            ],
        ),
        out_shape=[jax.ShapeDtypeStruct((HEAD_DIM, QUARTER), BF16)] * QUARTERS
        + [jax.ShapeDtypeStruct((1, SEQ_LEN), F32)],
        cost_estimate=pl.CostEstimate(
            flops=18_000_000_000, bytes_accessed=2_200_000, transcendentals=9_000_000
        ),
        name="attend_forward",
    )(info, qkv, qkv, qkv, *after)


def pieces(values):
    high = values.astype(BF16).astype(F32)
    rest = values - high
    middle = rest.astype(BF16).astype(F32)
    return [high, middle, (rest - middle).astype(BF16).astype(F32)]


def backward_kernel(
    skip, info, q_ref, k_ref, v_ref, g_0, g_1, g_2, g_3, o_0, o_1, o_2, o_3, lse_ref, normed_ref, *refs
):
    d_0, d_1, d_2, d_3, weight_ref, sums_ref, *refs = refs[skip:]
    g_ref, q_wide, k_wide, v_wide, g_wide, p_a, ds_a, p_b, ds_b, *refs = refs
    dq, dk, dv, d_ref, normed, arrived = refs
    start, own = info[0], info[1]
    cross, pairs = crossing(start)
    fetch = pltpu.make_async_copy(normed_ref, normed, arrived)
    fetch.start()
    ones = [jnp.ones((1, BLOCK), F32)] * 3

    def widen(columns, rows):
        rest = jnp.concatenate(rows + [jnp.zeros((HEAD_DIM - 3, BLOCK), F32)], axis=0)
        return jnp.concatenate([columns, rest.astype(BF16)], axis=0).T

    for x, (g_part, o_part) in enumerate(zip((g_0, g_1, g_2, g_3), (o_0, o_1, o_2, o_3))):
        g_ref[:, x * QUARTER : (x + 1) * QUARTER] = g_part[...]
        d_ref[0:HEAD_DIM, x * QUARTER : (x + 1) * QUARTER] = o_part[...]

    def prepare(block, carry):
        at = pl.ds(pl.multiple_of(block * BLOCK, BLOCK), BLOCK)
        grad = g_ref[:, at]
        centre = jnp.sum(
            grad.astype(F32) * d_ref[0:HEAD_DIM, at].astype(F32), axis=0, keepdims=True
        )
        q_wide[at, :] = widen(q_ref[:, at], pieces(-lse_ref[:, at]))
        k_wide[at, :] = widen(k_ref[:, at], ones)
        v_wide[at, :] = widen(v_ref[:, at], ones)
        g_wide[at, :] = widen(grad, pieces(-centre))
        return carry

    lax.fori_loop(0, BLOCKS, prepare, 0)
    dq[...] = jnp.zeros_like(dq)
    dk[...] = jnp.zeros_like(dk)
    dv[...] = jnp.zeros_like(dv)

    def score(row, col, p_dst, ds_dst, masked):
        rows = pl.ds(place(jnp.minimum(row, BLOCKS - 1), own), BLOCK)
        cols = pl.ds(place(col, own), BLOCK)
        s = product(q_wide[rows, :], k_wide[cols, :], NT)
        grad_p = product(g_wide[rows, :], v_wide[cols, :], NT)
        if masked:
            pos = row * BLOCK + lax.broadcasted_iota(jnp.int32, (BLOCK, 1), 0)
            limit = last_key(pos, start) - col * BLOCK
            s = jnp.where(lax.broadcasted_iota(jnp.int32, (BLOCK, BLOCK), 1) <= limit, s, -1e30)
        p = jnp.exp2(s)
        p_dst[...] = p.astype(BF16)
        ds_dst[...] = (p * grad_p).astype(BF16)

    def step(p, ds, p_dst, ds_dst, row, col, next_row, next_col, masked):
        score(next_row, next_col, p_dst, ds_dst, masked)
        rows = pl.ds(place(row, own), BLOCK)
        cols = pl.ds(place(col, own), BLOCK)
        dv[:, cols] += product(g_ref[:, rows], p[...], NN)
        dk[:, cols] += product(q_ref[:, rows], ds[...], NN)
        dq[:, rows] += product(k_ref[:, cols], ds[...], NT)

    def half(p, ds, p_dst, ds_dst, row, col, live):
        next_row, next_col = following(row, col, cross)
        masked = next_col >= next_row

        @pl.when(live & masked)
        def _():
            step(p, ds, p_dst, ds_dst, row, col, next_row, next_col, True)

        @pl.when(live & jnp.logical_not(masked))
        def _():
            step(p, ds, p_dst, ds_dst, row, col, next_row, next_col, False)

        return next_row, next_col

    score(0, 0, p_a, ds_a, True)

    def both(turn, carry):
        row, col = half(p_a, ds_a, p_b, ds_b, *carry, turn >= 0)
        return half(p_b, ds_b, p_a, ds_a, row, col, 2 * turn + 1 < pairs)

    lax.fori_loop(0, (pairs + 1) // 2, both, (jnp.int32(0), jnp.int32(0)))

    d_ref[0:64, :] = (dq[...] * 0.125).astype(BF16)
    d_ref[64:128, :] = (dk[...] * (1.0 / LOG2E)).astype(BF16)
    d_ref[128:192, :] = dv[...].astype(BF16)
    for x, part in enumerate((d_0, d_1, d_2, d_3)):
        part[...] = d_ref[:, x * QUARTER : (x + 1) * QUARTER]
    sums_ref[...] = jnp.sum(d_ref[...].astype(F32), axis=1, keepdims=True)
    fetch.wait()
    weight_ref[...] = product(d_ref[...], normed[...], NN).T.astype(BF16)


def attend_backward(info, qkv, grads, grad_row, outs, lse, normed, head, after):
    quarter = [whole(HEAD_DIM, QUARTER)] * QUARTERS
    grad_quarter = [
        pl.BlockSpec(
            (HEAD_DIM, QUARTER), lambda i, info: (grad_row, 0), pipeline_mode=pl.Buffered(1)
        )
    ] * QUARTERS
    rows = 3 * HEAD_DIM
    width = normed.shape[1]
    return pl.pallas_call(
        functools.partial(backward_kernel, len(after)),
        grid_spec=pltpu.PrefetchScalarGridSpec(
            num_scalar_prefetch=1,
            grid=(1,),
            in_specs=[head_spec(head, part) for part in range(3)]
            + grad_quarter
            + quarter
            + [whole(1, SEQ_LEN), ANYWHERE]
            + [ANYWHERE] * len(after),
            out_specs=[whole(rows, QUARTER)] * QUARTERS + [whole(width, rows), whole(rows, 1)],
            scratch_shapes=[pltpu.VMEM((HEAD_DIM, SEQ_LEN), BF16)]
            + [pltpu.VMEM((SEQ_LEN, 128), BF16)] * 4
            + [pltpu.VMEM((BLOCK, BLOCK), BF16)] * 4
            + [pltpu.VMEM((HEAD_DIM, SEQ_LEN), F32)] * 3
            + [
                pltpu.VMEM((rows, SEQ_LEN), BF16),
                pltpu.VMEM(normed.shape, BF16),
                pltpu.SemaphoreType.DMA,
            ],
        ),
        out_shape=[jax.ShapeDtypeStruct((rows, QUARTER), BF16)] * QUARTERS
        + [jax.ShapeDtypeStruct((width, rows), BF16), jax.ShapeDtypeStruct((rows, 1), F32)],
        cost_estimate=pl.CostEstimate(
            flops=32_000_000_000, bytes_accessed=12_000_000, transcendentals=9_000_000
        ),
        name="attend_backward",
    )(info, qkv, qkv, qkv, *grads, *outs, lse, normed, *after)


def normalise(values):
    centred = values - jnp.mean(values, axis=-1, keepdims=True)
    scale = lax.rsqrt(jnp.mean(centred * centred, axis=-1, keepdims=True) + EPSILON)
    return centred * scale, scale


def normalise_back(grad, unit, scale):
    return scale * (
        grad
        - jnp.mean(grad, axis=-1, keepdims=True)
        - unit * jnp.mean(grad * unit, axis=-1, keepdims=True)
    )


def gelu_both(u):
    square = u * u
    weight = 0.7978845608028654 + (0.7978845608028654 * 0.044715) * square
    share = 0.5 + 0.5 * jnp.tanh(u * weight)
    value = u * share
    rise = 6.0 * weight - 4.0 * 0.7978845608028654
    return value, share + value * (1.0 - share) * rise


def swap(values, mask):
    return lax.ppermute(values, "tensor", [(i, i ^ mask) for i in range(QUARTERS)])


def pick_first_kernel(info, qkv_ref, gain_ref, shift_ref, head_ref, hidden_ref, out_ref):
    rows = qkv_ref.shape[2]
    heads = qkv_ref.shape[3] // HEAD_DIM
    base = out_ref.shape[1] - 16
    out_ref[...] = jnp.zeros_like(out_ref)
    for h in range(heads):
        for part in range(3):
            at = (h * 3 + part) * HEAD_DIM
            out_ref[0, 0:rows, at : at + HEAD_DIM] = qkv_ref[
                0, part, :, h * HEAD_DIM : (h + 1) * HEAD_DIM
            ]
    few = head_ref.shape[2]
    hidden = hidden_ref[...].astype(F32)
    mine = lax.broadcasted_iota(jnp.int32, hidden.shape, 0) == info[3]
    hidden = jnp.sum(jnp.where(mine, hidden, 0.0), axis=0, keepdims=True)
    wide = lambda item: jnp.pad(
        item.astype(F32), ((0, 0), (0, out_ref.shape[2] - item.shape[1]))
    )
    out_ref[0, base:, :] = jnp.concatenate(
        [
            wide(gain_ref[0]),
            wide(shift_ref[0]),
            wide(head_ref[0]),
            wide(hidden),
            jnp.zeros((7, out_ref.shape[2]), F32),
        ],
        axis=0,
    ).astype(BF16)


def chosen_block(bank):
    rest = bank.shape[1:]
    return pl.BlockSpec((1, *rest), lambda i, info: (info[3],) + (0,) * len(rest))


def pick_first(info, qkv_bank, gain_bank, shift_bank, head_bank, hidden_bank):
    qkv_bank = qkv_bank.transpose(0, 2, 1, 3)
    rows, columns = qkv_bank.shape[2], 3 * qkv_bank.shape[3]
    shape = (1, -(-rows // 16) * 16 + 16, columns)
    return pl.pallas_call(
        pick_first_kernel,
        grid_spec=pltpu.PrefetchScalarGridSpec(
            num_scalar_prefetch=1,
            grid=(1,),
            in_specs=[
                chosen_block(bank) for bank in (qkv_bank, gain_bank, shift_bank, head_bank)
            ]
            + [whole(*hidden_bank.shape)],
            out_specs=pl.BlockSpec(shape, lambda i, info: (0, 0, 0)),
        ),
        out_shape=jax.ShapeDtypeStruct(shape, BF16),
        cost_estimate=SHORT,
        name="pick_first",
    )(info, qkv_bank, gain_bank, shift_bank, head_bank, hidden_bank)


def pick_rest_kernel(info, up_ref, down_ref, out_ref, qkv_ref, *refs):
    packed_ref = refs[-1]
    rows, first = up_ref.shape[1:]
    second = first + down_ref.shape[2]
    third = second + qkv_ref.shape[2]
    packed_ref[:, :first] = up_ref[0]
    packed_ref[:, first:second] = down_ref[0]
    packed_ref[:, second:third] = qkv_ref[0, :rows]
    packed_ref[:, third:] = out_ref[0].astype(F32).T.astype(BF16)


def pick_rest(info, up_bank, down_bank, out_bank, first, after):
    down_bank = down_bank.transpose(0, 2, 1)
    columns = up_bank.shape[2] + down_bank.shape[2] + out_bank.shape[1] + first.shape[2]
    shape = (up_bank.shape[1], columns)
    return pl.pallas_call(
        pick_rest_kernel,
        grid_spec=pltpu.PrefetchScalarGridSpec(
            num_scalar_prefetch=1,
            grid=(1,),
            in_specs=[chosen_block(bank) for bank in (up_bank, down_bank, out_bank)]
            + [pl.BlockSpec(first.shape, lambda i, info: (0, 0, 0))]
            + [ANYWHERE] * len(after),
            out_specs=whole(*shape),
        ),
        out_shape=jax.ShapeDtypeStruct(shape, BF16),
        cost_estimate=SHORT,
        name="pick_rest",
    )(info, up_bank, down_bank, out_bank, first, *after)


def assemble_kernel(order, info, *refs):
    parts, refs = refs[:-6], refs[-6:]
    turned_ref, vec_ref, bias_ref, own_ref, rows_ref, small_ref = refs
    count = len(order)
    held = [(part, n) for part in parts for n in range(part.shape[0])]
    rows = turned_ref.shape[1] // count
    for (part, n), k in zip(held, order):
        owner = jnp.bitwise_xor(info[2], k)
        at = pl.ds(pl.multiple_of(owner * rows, rows), rows)
        rows_ref[at, :] = part[n, :rows]
        small_ref[at, :] = part[n, rows:, 0:128].astype(F32).T[:rows]
    own_ref[...] = parts[0][0, :rows]
    turned_ref[...] = rows_ref[...].T
    small = small_ref[...]
    wide = jnp.concatenate([small, jnp.zeros((small.shape[0], 112), F32)], axis=1)
    vec_ref[...] = wide.T[0:16]
    heads = turned_ref.shape[0] // (3 * HEAD_DIM)
    few = heads * HEAD_DIM // count
    column = lambda n: jnp.concatenate(
        [small[p * rows : p * rows + few, n : n + 1] for p in range(count)], axis=0
    )
    q_bias, v_bias = column(6), column(7)
    for h in range(heads):
        at = h * 3 * HEAD_DIM
        bias_ref[at : at + HEAD_DIM, :] = q_bias[h * HEAD_DIM : (h + 1) * HEAD_DIM]
        bias_ref[at + HEAD_DIM : at + 2 * HEAD_DIM, :] = jnp.zeros((HEAD_DIM, 1), F32)
        bias_ref[at + 2 * HEAD_DIM : at + 3 * HEAD_DIM, :] = v_bias[h * HEAD_DIM : (h + 1) * HEAD_DIM]


def gather_qkv(info, part, count, rows):
    _, depth, columns = part.shape
    heads = columns // (3 * HEAD_DIM)
    few = heads * HEAD_DIM // count
    if count != 8 or rows % 16 or few % 8:
        parts = lax.all_gather(part[0], "dp", axis=0, tiled=False)
        turned = parts[:, :rows].reshape(count * rows, columns).T
        small = parts[:, depth - 16 :].astype(F32).transpose(1, 0, 2)
        vectors = small[:, :, :rows].reshape(16, count * rows)
        bias = small[6:8, :, :few].reshape(2, heads, HEAD_DIM)
        bias = jnp.stack([bias[0], jnp.zeros_like(bias[0]), bias[1]], axis=1)
        return turned, vectors, bias.reshape(columns, 1), part[0, :rows], part, part
    joined, order, others = part, [0], []
    for mask in (4, 2, 1):
        other = lax.ppermute(joined, "dp", [(i, i ^ mask) for i in range(count)])
        others.append(other)
        if mask > 1:
            joined = jnp.concatenate([joined, other])
        order = order + [k ^ mask for k in order]
    fixed = lambda *shape: pl.BlockSpec(shape, lambda i, info: (0,) * len(shape))
    outs = [
        ((columns, count * rows), BF16),
        ((16, count * rows), F32),
        ((columns, 1), F32),
        ((rows, columns), BF16),
    ]
    found = pl.pallas_call(
        functools.partial(assemble_kernel, order),
        grid_spec=pltpu.PrefetchScalarGridSpec(
            num_scalar_prefetch=1,
            grid=(1,),
            in_specs=[fixed(*item.shape) for item in (part, *others)],
            out_specs=[fixed(*shape) for shape, _ in outs],
            scratch_shapes=[
                pltpu.VMEM((count * rows, columns), BF16),
                pltpu.VMEM((count * rows, 16), F32),
            ],
        ),
        out_shape=[jax.ShapeDtypeStruct(shape, kind) for shape, kind in outs],
        cost_estimate=SHORT,
        name="assemble",
    )(info, part, *others)
    return *found, others[0], others[2]


def enter_kernel(spans, w_ref, vec_ref, bias_ref, *refs):
    parts, (qkv_ref, normed_ref, hidden_ref, held) = refs[:-4], refs[-4:]
    for part, (first, last, at) in zip(parts, spans):

        @pl.when((pl.program_id(0) >= first) & (pl.program_id(0) < last))
        def _():
            held[at : at + part.shape[0], :] = part[...]

    row = lax.broadcasted_iota(jnp.int32, (w_ref.shape[0], 1), 0)
    scale = jnp.where(lax.rem(row, 3 * HEAD_DIM) < HEAD_DIM, LOG2E / 8.0, 1.0)
    unit, _ = normalise(held[...].astype(F32))
    rounded = (unit * vec_ref[0:1] + vec_ref[2:3]).astype(BF16)
    normed_ref[...] = rounded
    flat = product(w_ref[...], rounded, NT)
    qkv_ref[...] = ((flat + bias_ref[...]) * scale).astype(BF16)
    hidden_ref[...] = vec_ref[8:9]


def enter(parts, turned, vectors, bias):
    block = BLOCK
    width = parts[0].shape[1]
    columns = turned.shape[0]
    fixed = lambda shape: pl.BlockSpec(shape, lambda i: (0, 0), pipeline_mode=pl.Buffered(1))
    spans, specs, row = [], [], 0
    for part in parts:
        size = min(part.shape[0], block)
        first, blocks = row // block, part.shape[0] // size
        spans.append((first, first + blocks, row % block))
        specs.append(
            pl.BlockSpec(
                (size, width), lambda i, first=first, n=blocks: (jnp.clip(i - first, 0, n - 1), 0)
            )
        )
        row += part.shape[0]
    first = row // block
    return pl.pallas_call(
        functools.partial(enter_kernel, spans),
        grid=(first,),
        in_specs=[fixed(turned.shape), fixed(vectors.shape), fixed(bias.shape)] + specs,
        out_specs=[
            pl.BlockSpec((columns, block), lambda i: (0, i)),
            pl.BlockSpec((block, width), lambda i: (i, 0)),
            fixed((1, width)),
        ],
        out_shape=[
            jax.ShapeDtypeStruct((columns, first * block), BF16),
            jax.ShapeDtypeStruct((first * block, width), BF16),
            jax.ShapeDtypeStruct((1, width), F32),
        ],
        scratch_shapes=[pltpu.VMEM((block, width), BF16)],
        cost_estimate=SHORT,
        name="enter",
    )(turned, vectors, bias, *parts)


TILE = 256
TALL = 512


def stored_blocks(width):
    return [
        pl.BlockSpec(
            (width, width),
            lambda i, info, x=x: (jnp.bitwise_xor(info[1], x), 2),
            pipeline_mode=pl.Buffered(1),
        )
        for x in range(QUARTERS)
    ]


def middle_kernel(parts, info, tokens_ref, cot_ref, vec_ref, up_ref, down_ref, *refs):
    stored, hidden, refs = refs[:4], refs[4:8], refs[8:]
    given, refs = refs[:parts], refs[parts:]
    (result_ref, grads_out, grad_ref, stats_ref), refs = refs[:4], refs[4:]
    back, refs = refs[: 2 * QUARTERS], refs[2 * QUARTERS :]
    mixed, middle, low, low_t, cot_t, activ, grad_u, branch, grad_two, *bufs = refs
    *bufs, grads_ref, out_ref, bias_ref, sent = bufs
    k = pl.program_id(0)
    count, width = tokens_ref.shape
    tiles = count // TALL
    local_width = width // QUARTERS
    spans = [slice(m * TALL, (m + 1) * TALL) for m in range(tiles)]

    def tiled(body):
        def at_tile(m, carry):
            return body(pl.ds(pl.multiple_of(m * TALL, TALL), TALL), carry)

        return at_tile

    @pl.when(k == 0)
    def _():
        for n, part in enumerate(given):
            mixed[n * HEAD_DIM : (n + 1) * HEAD_DIM, :] = part[...]
        low_t[width:, :] = jnp.ones((16, count), BF16)
        for x in range(QUARTERS):
            out_ref[:, x * local_width : (x + 1) * local_width] = stored[x][:, width - local_width :]
            bias_ref[x : x + 1, :] = hidden[x][...]

        @tiled
        def begin(at, carry):
            attended = product(mixed[:, at], out_ref[...], CT)
            value = tokens_ref[at, :].astype(F32) + attended + vec_ref[4:5]
            middle[at, :] = value
            unit, _ = normalise(value)
            rounded = (unit * vec_ref[1:2] + vec_ref[3:4]).astype(BF16)
            low[at, :] = rounded
            low_t[0:width, at] = rounded.T
            cot_t[:, at] = cot_ref[at, :].T
            branch[at, :] = jnp.zeros((TALL, width), F32)
            grad_two[at, :] = jnp.zeros((TALL, width), F32)
            return carry

        lax.fori_loop(0, tiles, begin, 0)

    bias = bias_ref[pl.ds(jnp.bitwise_xor(k, info[1]), 1), :]

    def first(m, u, g):
        u[...] = product(low[spans[m], :], up_ref[...], NN) + bias
        g[...] = product(cot_ref[spans[m], :], down_ref[...], NN)

    def second(m, u, g):
        value, slope = gelu_both(u[...])
        a = value.astype(BF16)
        gu = (g[...] * slope).astype(BF16)
        activ[spans[m], :] = a
        grad_u[spans[m], :] = gu
        branch[spans[m], :] += product(a, down_ref[...], NT)
        grad_two[spans[m], :] += product(gu, up_ref[...], NT)

    turns = (bufs[:2], bufs[2:])
    first(0, *turns[0])
    for m in range(tiles):
        if m + 1 < tiles:
            first(m + 1, *turns[(m + 1) % 2])
        second(m, *turns[m % 2])
    rows = pl.ds(pl.multiple_of(k * width, width), width)

    grad_up = product(low_t[...], grad_u[...], NN)
    grads_ref[rows, 0:width] = grad_up[:width].astype(BF16)
    stats_ref[pl.ds(4 + k, 1), :] = grad_up[width : width + 1]
    grads_ref[rows, width : 2 * width] = product(cot_t[...], activ[...], NN).astype(BF16)

    def leaving(n, columns):
        part = pl.ds(n * width, width)
        return pltpu.make_async_copy(
            grads_ref.at[part, columns], grads_out.at[part, columns], sent.at[n, columns.start // width // 2]
        )

    wide, narrow = slice(0, 2 * width), slice(2 * width, 2 * width + local_width)
    for n in range(QUARTERS):

        @pl.when(k == n)
        def _():
            leaving(n, wide).start()

    @pl.when(k == pl.num_programs(0) - 1)
    def _():
        @tiled
        def end(at, sums):
            value = middle[at, :]
            result_ref[at, :] = (value + branch[at, :] + vec_ref[5:6]).astype(BF16)
            unit, scale = normalise(value)
            grad = grad_two[at, :]
            cot = cot_ref[at, :].astype(F32)
            total = cot + normalise_back(grad * vec_ref[1:2], unit, scale)
            grad_ref[at, :] = total
            e = total.astype(BF16)
            low[at, :] = e
            mixed_grad = product(out_ref[...], e, CT).astype(BF16)
            for n, part in enumerate(back):
                row = n // 2 * local_width + n % 2 * HEAD_DIM
                part[:, at] = mixed_grad[row : row + part.shape[0]]
            items = (grad * unit, grad, e.astype(F32), cot)
            return tuple(
                old + jnp.sum(item, axis=0, keepdims=True) for old, item in zip(sums, items)
            )

        sums = lax.fori_loop(0, tiles, end, (jnp.zeros((1, width), F32),) * 4)
        for n in range(4):
            stats_ref[n : n + 1, :] = sums[n]
        grad_out = product(low[...], mixed[...], CT).astype(BF16)
        for x in range(QUARTERS):
            owner = jnp.bitwise_xor(info[1], x)
            grads_ref[pl.ds(pl.multiple_of(owner * width, width), width), 2 * width :] = grad_out[
                :, x * local_width : (x + 1) * local_width
            ]
        for n in range(QUARTERS):
            leaving(n, narrow).start()
        for n in range(QUARTERS):
            leaving(n, wide).wait()
            leaving(n, narrow).wait()


def middle_part(info, tokens, cotangent, vectors, hidden, bank, mixed):
    count, width = tokens.shape
    local_width = width // QUARTERS
    outs = [
        ((count, width), BF16),
        ((QUARTERS * width, 2 * width + local_width), BF16),
        ((count, width), F32),
        ((8, width), F32),
    ] + [((HEAD_DIM, count), BF16), ((local_width - HEAD_DIM, count), BF16)] * QUARTERS
    return pl.pallas_call(
        functools.partial(middle_kernel, len(mixed)),
        grid_spec=pltpu.PrefetchScalarGridSpec(
            num_scalar_prefetch=1,
            grid=(QUARTERS,),
            in_specs=[
                whole(count, width),
                whole(count, width),
                whole(16, width),
                pl.BlockSpec((width, width), lambda k, info: (k, 0)),
                pl.BlockSpec((width, width), lambda k, info: (k, 1)),
            ]
            + stored_blocks(width)
            + [whole(1, width)] * QUARTERS
            + [whole(HEAD_DIM, count)] * len(mixed),
            out_specs=[whole(*outs[0][0]), ANYWHERE] + [whole(*shape) for shape, _ in outs[2:]],
            scratch_shapes=[
                pltpu.VMEM((width, count), BF16),
                pltpu.VMEM((count, width), F32),
                pltpu.VMEM((count, width), BF16),
                pltpu.VMEM((width + 16, count), BF16),
                pltpu.VMEM((width, count), BF16),
                pltpu.VMEM((count, width), BF16),
                pltpu.VMEM((count, width), BF16),
                pltpu.VMEM((count, width), F32),
                pltpu.VMEM((count, width), F32),
            ]
            + [pltpu.VMEM((TALL, width), F32)] * 4
            + [
                pltpu.VMEM(outs[1][0], BF16),
                pltpu.VMEM((width, width), BF16),
                pltpu.VMEM((8, width), F32),
                pltpu.SemaphoreType.DMA((QUARTERS, 2)),
            ],
        ),
        out_shape=[jax.ShapeDtypeStruct(shape, kind) for shape, kind in outs],
        compiler_params=pltpu.CompilerParams(vmem_limit_bytes=66_000_000),
        cost_estimate=pl.CostEstimate(
            flops=40_000_000_000, bytes_accessed=40_000_000, transcendentals=3_200_000
        ),
        name="middle",
    )(info, tokens, cotangent, vectors, bank, bank, *[bank] * QUARTERS, *hidden, *mixed)


def add_back(grad, tokens_ref, vec_ref, grad_ref):
    unit, scale = normalise(tokens_ref[...].astype(F32))
    return grad_ref[...] + normalise_back(grad * vec_ref[0:1], unit, scale)


def exit_first_kernel(heads, skip, info, *refs):
    count = heads * QUARTERS
    deltas, weights, refs = refs[:count], refs[count : count + 4], refs[count + 4 :]
    tokens_ref, grad_ref, vec_ref, *refs = refs
    sum_ref, rest_ref, d_all, w_all = refs[skip:]
    span = deltas[0].shape[0]

    @pl.when(pl.program_id(0) == 0)
    def _():
        for x in range(QUARTERS):
            at = x * heads * span
            w_all[:, at : at + heads * span] = weights[x][:, : heads * span]
            rest_ref[:, x * span : (x + 1) * span] = weights[x][
                :, heads * span : (heads + 1) * span
            ]

    for x in range(QUARTERS):
        for h in range(heads):
            at = (x * heads + h) * span
            d_all[at : at + span, :] = deltas[h * QUARTERS + x][...]
    sum_ref[...] = add_back(product(w_all[...], d_all[...], NN).T, tokens_ref, vec_ref, grad_ref)


def exit_last_kernel(skip, info, *refs):
    deltas, refs = refs[:4], refs[4:]
    w_ref, tokens_ref, grad_ref, vec_ref, *refs = refs
    out_ref, d_all = refs[skip:]
    span = deltas[0].shape[0]
    for x in range(QUARTERS):
        d_all[x * span : (x + 1) * span, :] = deltas[x][...]
    grad = product(w_ref[...], d_all[...], NN).T
    out_ref[...] = add_back(grad, tokens_ref, vec_ref, grad_ref).astype(BF16)


def lanes(rows):
    return pl.BlockSpec((rows, TILE), lambda i, info: (0, i))


def lines(columns):
    return pl.BlockSpec((TILE, columns), lambda i, info: (i, 0))


def exit_first(info, deltas, bank, tokens, grad, vectors, after):
    count, width = tokens.shape
    span = deltas[0].shape[0]
    heads = len(deltas) // QUARTERS
    depth = len(deltas) * span
    return pl.pallas_call(
        functools.partial(exit_first_kernel, heads, len(after)),
        grid_spec=pltpu.PrefetchScalarGridSpec(
            num_scalar_prefetch=1,
            grid=(count // TILE,),
            in_specs=[lanes(span)] * len(deltas)
            + stored_blocks(width)
            + [lines(width), lines(width), whole(*vectors.shape)]
            + [ANYWHERE] * len(after),
            out_specs=[lines(width), whole(width, QUARTERS * span)],
            scratch_shapes=[pltpu.VMEM((depth, TILE), BF16), pltpu.VMEM((width, depth), BF16)],
        ),
        out_shape=[
            jax.ShapeDtypeStruct((count, width), F32),
            jax.ShapeDtypeStruct((width, QUARTERS * span), BF16),
        ],
        cost_estimate=pl.CostEstimate(
            flops=10_000_000_000, bytes_accessed=10_000_000, transcendentals=0
        ),
        name="exit_first",
    )(info, *deltas, *[bank] * QUARTERS, tokens, grad, vectors, *after)


def exit_last(info, deltas, weights, tokens, grad, vectors, after):
    count, width = tokens.shape
    span = deltas[0].shape[0]
    return pl.pallas_call(
        functools.partial(exit_last_kernel, len(after)),
        grid_spec=pltpu.PrefetchScalarGridSpec(
            num_scalar_prefetch=1,
            grid=(count // TILE,),
            in_specs=[lanes(span)] * QUARTERS
            + [whole(*weights.shape), lines(width), lines(width), whole(*vectors.shape)]
            + [ANYWHERE] * len(after),
            out_specs=lines(width),
            scratch_shapes=[pltpu.VMEM((QUARTERS * span, TILE), BF16)],
        ),
        out_shape=jax.ShapeDtypeStruct((count, width), BF16),
        cost_estimate=pl.CostEstimate(
            flops=8_000_000_000, bytes_accessed=8_000_000, transcendentals=0
        ),
        name="exit_last",
    )(info, *deltas, weights, tokens, grad, vectors, *after)


def pack_first_kernel(rows, weights, stats_ref, out_ref):
    span = weights[0].shape[1]
    count, depth, columns = out_ref.shape
    stats = jnp.concatenate(pieces(stats_ref[...]), axis=0)
    for p in range(count):
        for h, weight in enumerate(weights):
            out_ref[p, 0:rows, h * span : (h + 1) * span] = weight[p * rows : (p + 1) * rows]
        part = jnp.concatenate(
            [stats[:, p * rows : (p + 1) * rows], jnp.zeros((24, columns - rows), F32)], axis=1
        )
        part = jnp.concatenate([part, jnp.zeros((8, columns), F32)], axis=0)
        out_ref[p, depth - 32 :, :] = part.astype(BF16)


def pack_last_kernel(rows, weight, sums, out_ref):
    span = weight.shape[1]
    count, depth, columns = out_ref.shape
    lined = [jnp.broadcast_to(item[...], (span, 128)).T[0:1] for item in sums]
    lined = [piece for item in lined for piece in pieces(item)]
    lined = jnp.concatenate(lined + [jnp.zeros((16 - len(lined), span), F32)], axis=0)
    lined = jnp.concatenate([lined, jnp.zeros((16, columns - span), F32)], axis=1).astype(BF16)
    out_ref[...] = jnp.zeros_like(out_ref)
    for p in range(count):
        out_ref[p, 0:rows, 0:span] = weight[p * rows : (p + 1) * rows]
        out_ref[p, depth - 16 :, :] = lined


def exchange(kernel, count, items, below, columns, after, name):
    width = items[0].shape[0]
    rows = width // count
    fixed = lambda shape: pl.BlockSpec(shape, lambda i: (0,) * len(shape))
    shape = (count, -(-rows // 16) * 16 + below, columns)

    def body(*refs):
        kernel(rows, refs[: len(items)], refs[-1])

    packed = pl.pallas_call(
        body,
        grid=(1,),
        in_specs=[fixed(item.shape) for item in items] + [ANYWHERE] * len(after),
        out_specs=fixed(shape),
        out_shape=jax.ShapeDtypeStruct(shape, BF16),
        cost_estimate=SHORT,
        name=name,
    )(*items, *after)
    received = lax.all_to_all(
        packed.reshape(-1, columns), "dp", split_axis=0, concat_axis=0, tiled=True
    )
    return received.reshape(shape), packed


def exchange_first(weights, stats, count):
    kernel = lambda rows, refs, out: pack_first_kernel(rows, refs[:-1], refs[-1], out)
    columns = sum(weight.shape[1] for weight in weights)
    return exchange(kernel, count, [*weights, stats], 32, columns, [], "pack_first")


def exchange_last(weight, sums, count, after):
    kernel = lambda rows, refs, out: pack_last_kernel(rows, refs[0], refs[1:], out)
    return exchange(kernel, count, [weight, *sums], 16, 256, after, "pack_last")


def finish_kernel(heads, early_ref, late_ref, weight_ref, small_ref, *refs):
    total_ref, stats_ref, sums_ref = refs[-3:]
    rows, columns = weight_ref.shape
    span = columns // heads
    early, late = early_ref[0].astype(F32), late_ref[0].astype(F32)
    for p in range(1, early_ref.shape[0]):
        early = early + early_ref[p].astype(F32)
        late = late + late_ref[p].astype(F32)
    grads = jnp.concatenate([early[:rows], late[:rows, :span]], axis=1)
    base = early.shape[0] - 32
    stats = early[base : base + 8] + early[base + 8 : base + 16] + early[base + 16 : base + 24]
    lined = late[late.shape[0] - 16 :, :span]
    sums = jnp.concatenate(
        [lined[3 * h : 3 * h + 1] + lined[3 * h + 1 : 3 * h + 2] + lined[3 * h + 2 : 3 * h + 3]
         for h in range(heads)],
        axis=1,
    )
    weights = weight_ref[...].astype(F32)
    shift = jnp.sum(weights * sums, axis=1, keepdims=True)
    gain = jnp.sum(weights * grads, axis=1, keepdims=True)
    gain = (gain - small_ref[:, 1:2] * shift) / small_ref[:, 0:1]
    sums_ref[...] = sums
    for n in range(columns // HEAD_DIM):
        at = n // 3 * HEAD_DIM
        total_ref[n % 3, :, at : at + HEAD_DIM] = grads[:, n * HEAD_DIM : (n + 1) * HEAD_DIM]
    turned = jnp.concatenate([shift, gain, jnp.zeros((rows, 6), F32)], axis=1).T
    stats_ref[...] = jnp.concatenate([stats[:, :rows], turned], axis=0)


def finish(early, late, weights, small, after):
    rows, columns = weights.shape
    heads = columns // (3 * HEAD_DIM)
    fixed = lambda shape: pl.BlockSpec(shape, lambda i: (0,) * len(shape))
    outs = [(3, rows, columns // 3), (16, rows), (1, columns)]
    return pl.pallas_call(
        functools.partial(finish_kernel, heads),
        grid=(1,),
        in_specs=[fixed(item.shape) for item in (early, late, weights, small)]
        + [ANYWHERE] * len(after),
        out_specs=[fixed(shape) for shape in outs],
        out_shape=[jax.ShapeDtypeStruct(shape, F32) for shape in outs],
        cost_estimate=SHORT,
        name="finish",
    )(early, late, weights, small, *after)


def unpack_kernel(info, shard_ref, a_ref, b_ref, c_ref, d_ref, *refs):
    up_ref, down_ref, out_ref, gain_ref, shift_ref, hidden_ref, sum_ref = refs
    first, second = up_ref.shape[1], up_ref.shape[1] + down_ref.shape[1]
    up_ref[...] = shard_ref[:, :first].astype(F32)
    down_ref[...] = shard_ref[:, first:second].astype(F32)
    out_ref[...] = shard_ref[:, second:].astype(F32).T
    total = (a_ref[...] + b_ref[...]) + (c_ref[...] + d_ref[...])
    sum_ref[...] = total
    gain_ref[...] = jnp.concatenate([total[9:10], total[0:1]], axis=0)
    shift_ref[...] = jnp.concatenate([total[8:9], total[1:4]], axis=0)
    hidden_ref[...] = sum_ref[pl.ds(4 + info[1], 1), :]


def unpack(info, shard, stats, first, second):
    rows, columns = shard.shape
    outs = [(rows, first), (rows, second - first), (columns - second, rows), (2, rows), (4, rows), (1, rows)]
    fixed = lambda shape: pl.BlockSpec(shape, lambda i, info: (0, 0))
    return pl.pallas_call(
        unpack_kernel,
        grid_spec=pltpu.PrefetchScalarGridSpec(
            num_scalar_prefetch=1,
            grid=(1,),
            in_specs=[fixed(item.shape) for item in (shard, *stats)],
            out_specs=[fixed(shape) for shape in outs],
            scratch_shapes=[pltpu.VMEM(stats[0].shape, F32)],
        ),
        out_shape=[jax.ShapeDtypeStruct(shape, F32) for shape in outs],
        cost_estimate=SHORT,
        name="unpack",
    )(info, shard, *stats)


def local(
    n_dp,
    tokens,
    cotangent,
    tie_index,
    image_start,
    qkv_bank,
    out_bank,
    up_bank,
    down_bank,
    gain_bank,
    shift_bank,
    head_bias_bank,
    hidden_bias_bank,
):
    own = lax.axis_index("tensor")
    own_dp = lax.axis_index("dp")
    width = tokens.shape[1]
    rows = qkv_bank.shape[1]
    local_width = qkv_bank.shape[3]
    hidden_cols = up_bank.shape[2]
    heads = local_width // HEAD_DIM
    qkv_cols = 3 * local_width
    few = head_bias_bank.shape[2]
    info = jnp.stack([image_start[0], own, own_dp, tie_index[0]]).astype(jnp.int32)

    cuts = (0, QUARTER // 4, QUARTER // 2, QUARTER)
    far = [swap(tokens[low:high], 2) for low, high in zip(cuts, cuts[1:])]
    near = swap(tokens, 1)

    packed = pick_first(info, qkv_bank, gain_bank, shift_bank, head_bias_bank, hidden_bias_bank)
    turned, vectors, bias, qkv_part, started, ended = gather_qkv(info, packed, n_dp, rows)
    far[2:] = gate([far[2]], [ended])
    far_near = [swap(part, 1) for part in far]
    own_small = packed[0, -16:].astype(F32)
    bank_part = pick_rest(info, up_bank, down_bank, out_bank, packed, [started, far[0]])
    bank = lax.all_gather(bank_part, ("tensor", "dp"), axis=0, tiled=True)
    c_out = 2 * hidden_cols

    qkv, normed, hidden_bias = enter([tokens, near] + far + far_near, turned, vectors, bias)
    hidden = [hidden_bias] + [swap(hidden_bias, x) for x in range(1, QUARTERS)]

    outs, lses, mixed = [], [], [[None] * heads for _ in range(QUARTERS)]
    for head in range(heads):
        after = [mixed[x][head - 2] for x in range(1, QUARTERS)] if head > 1 else []
        *out, lse = attend_forward(info, qkv, head, after)
        if head == heads - 1:
            out = gate(out, [mixed[x][head - 1] for x in range(1, QUARTERS)])
        outs.append(out)
        lses.append(lse)
        for x in range(QUARTERS):
            mixed[x][head] = swap(out[x], x) if x else out[x]

    result, grads, grad_middle, stats, *mixed_grads = middle_part(
        info, tokens, cotangent, vectors, hidden, bank, [part for quarter in mixed for part in quarter]
    )
    shard = lax.psum_scatter(grads, ("tensor", "dp"), scatter_dimension=0, tiled=True)

    deltas, weight_grads, sums = [], [], []
    grads_first = [swap(mixed_grads[2 * x], x) if x else mixed_grads[0] for x in range(QUARTERS)]
    rest = gate([mixed_grads[2 * x + 1] for x in range(QUARTERS)], grads_first[1:])
    grads_rest = [swap(rest[x], x) if x else rest[0] for x in range(QUARTERS)]
    for head in range(heads):
        *parts, weight_grad, summed = attend_backward(
            info,
            qkv,
            grads_rest if head else grads_first,
            max(head - 1, 0),
            outs[head],
            lses[head],
            normed,
            head,
            [rest[0]] if head == 0 else deltas[head - 2][1:] if head > 1 else [],
        )
        deltas.append([swap(parts[x], x) if x else parts[x] for x in range(QUARTERS)])
        weight_grads.append(weight_grad)
        sums.append(summed)
        if head == heads - 2:
            early_sums, _ = exchange_first(weight_grads, stats, n_dp)
    early = [part for parts in deltas[:-1] for part in parts]

    late_sums, packed_last = exchange_last(weight_grads[-1], sums, n_dp, [*deltas[-2][1:], early_sums])
    grad_part, weights = exit_first(
        info, early, bank, tokens, grad_middle, vectors, [packed_last]
    )
    grad_tokens = exit_last(info, deltas[-1], weights, tokens, grad_part, vectors, [])
    small = jnp.stack([own_small[0, :rows], own_small[2, :rows]], axis=1)
    qkv_total, stats, sums = finish(early_sums, late_sums, qkv_part, small, [grad_tokens])
    found = [stats] + [swap(stats, x) for x in range(1, QUARTERS)]

    by_part = sums.reshape(heads, 3, HEAD_DIM)
    head_sums = jnp.stack([by_part[:, 0].reshape(-1), by_part[:, 2].reshape(-1)])
    head_shard = lax.dynamic_slice_in_dim(head_sums, own_dp * few, few, 1)

    up_shard, down_shard, out_shard, gain_grads, shift_grads, hidden_shard = unpack(
        info, shard, found, hidden_cols, c_out
    )

    return (
        result,
        grad_tokens,
        qkv_total.transpose(1, 0, 2),
        out_shard,
        up_shard,
        down_shard.T,
        gain_grads,
        shift_grads,
        head_shard,
        hidden_shard.reshape(rows),
    )


def solution(mesh):
    placed = (
        P(("dp", "tensor"), None),
        P(("dp", "tensor"), None),
        P(),
        P("dp"),
        P(None, "dp", None, "tensor"),
        P(None, "tensor", "dp"),
        P(None, "dp", "tensor"),
        P(None, "tensor", "dp"),
        P(None, None, "dp"),
        P(None, None, "dp"),
        P(None, None, ("tensor", "dp")),
        P(None, ("tensor", "dp")),
    )
    return jax.shard_map(
        functools.partial(local, mesh.shape["dp"]),
        mesh=mesh,
        in_specs=placed,
        out_specs=(
            P(("dp", "tensor"), None),
            P(("dp", "tensor"), None),
            P("dp", None, "tensor"),
            P("tensor", "dp"),
            P("dp", "tensor"),
            P("tensor", "dp"),
            P(None, "dp"),
            P(None, "dp"),
            P(None, ("tensor", "dp")),
            P(("tensor", "dp")),
        ),
        check_vma=False,
    )
```
